512 devices in a mesh: section: 32 (over x, y, core), grp: 16 (over z).
Axes of the slice: x: 4, y: 4, z: 16, core: 2. Of those that a mesh axis runs over, the one named last changes fastest.
Arguments:
- planes: bfloat16 [4, 64, 64, 2048], P(None, 'section', None, 'grp'), may hold values from -6 to 6
- w_reduce: bfloat16 [3, 2048, 2048], P(None, None, 'grp'), may hold values from -0.125 to 0.125
- w_group: bfloat16 [3, 9, 32, 2048], P(None, None, None, 'grp'), may hold values from -0.375 to 0.375
- w_expand: bfloat16 [3, 2048, 2048], P(None, None, 'grp'), may hold values from -0.125 to 0.125
- gains: float32 [3, 3, 2048], P(None, None, 'grp'), may hold values from 0.25 to 1.75
- biases: float32 [3, 3, 2048], P(None, None, 'grp'), may hold values from -1.5 to 1.5
Outputs:
- feats: bfloat16 [4, 64, 64, 2048], P(None, 'section', None, 'grp')
The draws below stay inside these ranges and needn't reach their ends.
All inputs are finite; a program needn't handle non-finite values.
Results may differ from the reference program's by a relative error of at most 0.014.
Values may be sent and summed in bfloat16 or wider, within the bound.
No kernel may reach another device: no remote copies, remote signals or barrier semaphores. Data moves between devices by JAX's collectives and lax.ppermute only.
A program may use at most 64 MiB of HBM per device.

```python
import jax
import jax.numpy as jnp
from jax import lax

C = 2048
GW = 32
SIDE = 64
TILES = 4
BLOCKS = 3


def shard_levels(rng, shape, split, low, largest):
    gain, own = 1.0, jax.random.fold_in(rng, 6)
    for axis_at, parts in split:
        steps = jnp.exp(jax.random.uniform(jax.random.fold_in(own, axis_at), (parts,), jnp.float32, low / len(split), largest / len(split)))
        gain = gain * jnp.repeat(steps, shape[axis_at] // parts).reshape([-1 if axis == axis_at else 1 for axis in range(len(shape))])
    return gain


def scatter_about(own_key, dims, spread, limit, shards=(), kind=jnp.bfloat16):
    values = spread * jax.random.normal(own_key, dims, jnp.float32)
    if shards:
        values = values * shard_levels(own_key, dims, shards, -0.22, 0.18)
    return jnp.clip(values, -limit, limit).astype(kind)


def setup_inputs(seed: int = 0) -> dict:
    streams_of = jax.random.split(jax.random.key(seed), 7)
    return {
        "planes": scatter_about(streams_of[0], (TILES, SIDE, SIDE, C), 1.0, 6.0, ((1, 32), (3, 16))),
        "w_reduce": scatter_about(streams_of[1], (BLOCKS, C, C), C ** -0.5, 0.125, ((2, 16),)),
        "w_group": scatter_about(streams_of[2], (BLOCKS, 9, GW, C), (9 * GW) ** -0.5, 0.375, ((3, 16),)),
        "w_expand": scatter_about(streams_of[3], (BLOCKS, C, C), C ** -0.5, 0.125, ((2, 16),)),
        "gains": jnp.clip(1.0 + 0.15 * jax.random.normal(streams_of[4], (BLOCKS, 3, C), jnp.float32), 0.25, 1.75),
        "biases": scatter_about(streams_of[5], (BLOCKS, 3, C), 0.3, 1.5, ((2, 16),), jnp.float32),
    }


def run_block(planes, w_reduce, kernel, w_expand, gains, biases):
    channels = planes.shape[3]
    stream = planes.reshape(-1, channels)
    first = jnp.dot(stream, w_reduce, preferred_element_type=jnp.float32)
    hidden = jnp.maximum(gains[0] * first + biases[0], 0.0).astype(jnp.bfloat16)
    group_width = kernel.shape[1]
    filters = kernel.astype(jnp.float32).reshape(3, 3, group_width, channels)
    spatial = lax.conv_general_dilated(
        hidden.reshape(planes.shape).astype(jnp.float32), filters, (1, 1), "SAME",
        dimension_numbers=("NHWC", "HWIO", "NHWC"),
        feature_group_count=channels // group_width,
        precision=lax.Precision.HIGHEST).reshape(-1, channels)
    middle = jnp.maximum(gains[1] * spatial + biases[1], 0.0).astype(jnp.bfloat16)
    second = jnp.dot(middle, w_expand, preferred_element_type=jnp.float32)
    result = jnp.maximum(gains[2] * second + biases[2] + stream.astype(jnp.float32), 0.0)
    return result.astype(jnp.bfloat16).reshape(planes.shape)


def reference(planes, w_reduce, w_group, w_expand, gains, biases):
    current = planes
    for block in range(BLOCKS):
        current = run_block(current, w_reduce[block], w_group[block], w_expand[block], gains[block], biases[block])
    return current
```

```python
import jax
import jax.numpy as jnp
import numpy as np
from jax import lax
from jax.sharding import Mesh
from jax.sharding import PartitionSpec as P

BF16 = jnp.bfloat16
F32 = jnp.float32
SEG = ("x", "y", "c")
LEFT = 4
HALO = 3


def dot_nt(a, b):
    return lax.dot_general(a, b, (((1,), (1,)), ((), ())), preferred_element_type=F32)


def selector(rows, cols, base):
    i = lax.broadcasted_iota(jnp.int32, (rows, cols), 0)
    j = lax.broadcasted_iota(jnp.int32, (rows, cols), 1)
    return (j == i + base).astype(BF16)


def split_terms(v):
    terms = []
    for _ in range(3):
        t = lax.reduce_precision(v, 8, 7)
        terms.append(t.astype(BF16))
        v = v - t
    return terms


def pick(c, a, b):
    return jnp.where(c == 0, a, b)


def swap_core(v, c):
    both = lax.all_gather(v, "c", axis=0)
    return pick(c, both[1], both[0])


def contract(x, w, c):
    part = dot_nt(x, w)
    half = part.shape[1] // 2
    mine, other = pick(c, part[:, :half], part[:, half:]), pick(c, part[:, half:], part[:, :half])
    return mine + swap_core(other.astype(BF16), c).astype(F32)


def local(planes, w_reduce, w_group, w_expand, gains, biases):
    nx, ny, nc, nz = (lax.axis_size(a) for a in ("x", "y", "c", "z"))
    x, y, c, z = (lax.axis_index(a) for a in ("x", "y", "c", "z"))
    tiles, rows, side, lanes = planes.shape
    blocks, taps, width, _ = w_group.shape
    channels = lanes * nz
    half = channels // nc
    zhalf = nz // nc
    own = zhalf * width
    across = nz // tiles
    patch = side // across
    tall = rows * ny * nc
    frame = patch + 2 * LEFT

    sel = selector(width, lanes, width * y)

    def part(w, natural):
        w = lax.dynamic_slice_in_dim(w, half * c, half, axis=0)
        if not natural:
            w = w.reshape(zhalf, ny, width, lanes).transpose(1, 0, 2, 3).reshape(half, lanes)
        return dot_nt(sel, w).astype(BF16)

    early = jnp.stack([part(w_reduce[0], True), part(w_expand[0], False), part(w_reduce[1], False), part(w_expand[1], False)])
    late = jnp.stack([part(w_reduce[2], False), part(w_expand[2], False)])
    early = lax.all_gather(early, "z", axis=1, tiled=True)
    late = lax.all_gather(late, "z", axis=1, tiled=True)
    matrices = [(early[0], early[1]), (early[2], early[3]), (late[0], late[1])]

    wide = jnp.pad(planes, ((0, 0), (0, 0), (LEFT, LEFT), (0, 0)))
    strips = jnp.stack([wide[:, :, patch * q : patch * q + frame] for q in range(across)], axis=1)
    strips = strips.reshape(nz, rows, frame, lanes)
    mixed = lax.all_to_all(strips, "z", 0, 0, tiled=True)
    mine = pick(c, mixed[:zhalf], mixed[zhalf:])
    theirs = swap_core(pick(c, mixed[zhalf:], mixed[:zhalf]), c)
    chip = jnp.concatenate([pick(c, mine, theirs), pick(c, theirs, mine)], axis=1)
    chip = chip.transpose(1, 2, 0, 3).reshape(rows * nc, frame, half)
    body = lax.all_gather(chip, "y", axis=0, tiled=True)
    above = lax.ppermute(body[tall - HALO :], "x", [(i, i + 1) for i in range(nx - 1)])
    below = lax.ppermute(body[:HALO], "x", [(i + 1, i) for i in range(nx - 1)])
    gathered = jnp.concatenate([above, body, below], axis=0)

    small = jnp.stack([gains, biases]).reshape(-1, lanes)
    table = jnp.concatenate([w_group.reshape(-1, lanes)] + split_terms(small), axis=0)
    count = blocks * taps * width
    table = lax.all_gather(dot_nt(sel, table).astype(BF16), "z", axis=0, tiled=True)
    table = lax.dynamic_slice_in_dim(table, own * c, own, axis=0)
    small = table[:, count:].astype(F32).reshape(own, 3, -1)
    small = (small[:, 0] + small[:, 1] + small[:, 2]).T.reshape(2, blocks, 3, own)
    spread = jnp.tile(jnp.eye(width, dtype=BF16), (1, zhalf))
    group = lax.broadcasted_iota(jnp.int32, (own, own), 0) // width == lax.broadcasted_iota(jnp.int32, (own, own), 1) // width

    def dense(b):
        out = []
        for r in range(3):
            for_row = []
            for s in range(3):
                at = (b * taps + 3 * r + s) * width
                full = jnp.dot(table[:, at : at + width], spread, preferred_element_type=F32)
                for_row.append(jnp.where(group, full, 0.0).astype(BF16))
            out.append(jnp.concatenate(for_row, axis=0))
        return jnp.concatenate(out, axis=1)

    kernels = [dense(b) for b in range(blocks)]

    j = lax.broadcasted_iota(jnp.int32, (half, own), 0)
    k = lax.broadcasted_iota(jnp.int32, (half, own), 1)
    pull = (j == (k // width) * lanes + width * y + k % width).astype(BF16)
    stream = jnp.dot(gathered.reshape(-1, half), pull, preferred_element_type=F32).astype(BF16)
    stream = stream.reshape(tall + 2 * HALO, frame, own)

    column = patch * (z % across) - LEFT + lax.broadcasted_iota(jnp.int32, (1, frame, 1), 1)
    in_columns = (column >= 0) & (column < side)
    for b in range(blocks):
        gain, bias = small[0, b], small[1, b]
        reach = HALO - b
        high = tall + 2 * reach
        if b:
            gathered = lax.all_gather(stream.reshape(-1, own), "y", axis=1, tiled=True)
        first = contract(gathered.reshape(-1, half), matrices[b][0], c).reshape(high, frame, own)
        row = tall * x - reach + lax.broadcasted_iota(jnp.int32, (high, 1, 1), 0)
        inside = (row >= 0) & (row < side) & in_columns
        hidden = jnp.where(inside, jnp.maximum(gain[0] * first + bias[0], 0.0), 0.0).astype(BF16)
        high -= 2
        rows3 = jnp.concatenate([hidden[r : r + high] for r in range(3)], axis=-1).reshape(-1, 3 * own)
        wide = dot_nt(rows3, kernels[b]).reshape(high, frame, 3, own)
        edge = jnp.zeros((high, 1, own), F32)
        spatial = (
            jnp.concatenate([edge, wide[:, :-1, 0]], axis=1)
            + wide[:, :, 1]
            + jnp.concatenate([wide[:, 1:, 2], edge], axis=1)
        )
        middle = jnp.maximum(gain[1] * spatial + bias[1], 0.0).astype(BF16)
        middle = lax.all_gather(middle.reshape(-1, own), "y", axis=1, tiled=True)
        second = contract(middle, matrices[b][1], c).reshape(high, frame, own)
        stream = jnp.maximum(gain[2] * second + bias[2] + stream[1:-1].astype(F32), 0.0).astype(BF16)

    done = stream[:, LEFT : LEFT + patch].reshape(ny, nc, rows, patch, own)
    done = lax.all_to_all(done, "y", 0, 0, tiled=True)
    mine = pick(c, done[:, 0], done[:, 1])
    theirs = swap_core(pick(c, done[:, 1], done[:, 0]), c)
    both = jnp.stack([pick(c, mine, theirs), pick(c, theirs, mine)]).reshape(nc, ny, rows, patch, zhalf, width)
    both = both.transpose(0, 4, 2, 3, 1, 5).reshape(nz, rows, patch, lanes)
    out = lax.all_to_all(both, "z", 0, 0, tiled=True).reshape(tiles, across, rows, patch, lanes)
    return out.transpose(0, 2, 1, 3, 4).reshape(tiles, rows, side, lanes)


def solution(mesh):
    grid = Mesh(mesh.devices.reshape(4, 4, 2, 16), ("x", "y", "c", "z"))
    placed = (
        P(None, SEG, None, "z"),
        P(None, None, "z"),
        P(None, None, None, "z"),
        P(None, None, "z"),
        P(None, None, "z"),
        P(None, None, "z"),
    )
    return jax.shard_map(local, mesh=grid, in_specs=placed, out_specs=P(None, SEG, None, "z"), check_vma=False)
```

```python
import jax
import jax.numpy as jnp
import numpy as np
from jax import lax
from jax.sharding import Mesh
from jax.sharding import PartitionSpec as P

BF16 = jnp.bfloat16
F32 = jnp.float32
SEG = ("x", "y", "c")
LEFT = 4
HALO = 3


def dot_nt(a, b):
    return lax.dot_general(a, b, (((1,), (1,)), ((), ())), preferred_element_type=F32)


def selector(rows, cols, base):
    i = lax.broadcasted_iota(jnp.int32, (rows, cols), 0)
    j = lax.broadcasted_iota(jnp.int32, (rows, cols), 1)
    return (j == i + base).astype(BF16)


def split_terms(v):
    terms = []
    for _ in range(3):
        t = lax.reduce_precision(v, 8, 7)
        terms.append(t.astype(BF16))
        v = v - t
    return terms


def pick(c, a, b):
    return jnp.where(c == 0, a, b)


def swap_core(v, c):
    both = lax.all_gather(v, "c", axis=0)
    return pick(c, both[1], both[0])


def contract(x, w, c):
    part = dot_nt(x, w)
    half = part.shape[1] // 2
    mine, other = pick(c, part[:, :half], part[:, half:]), pick(c, part[:, half:], part[:, :half])
    return mine + swap_core(other.astype(BF16), c).astype(F32)


def local(planes, w_reduce, w_group, w_expand, gains, biases):
    nx, ny, nc, nz = (lax.axis_size(a) for a in ("x", "y", "c", "z"))
    x, y, c, z = (lax.axis_index(a) for a in ("x", "y", "c", "z"))
    tiles, rows, side, lanes = planes.shape
    blocks, taps, width, _ = w_group.shape
    channels = lanes * nz
    half = channels // nc
    zhalf = nz // nc
    own = zhalf * width
    across = nz // tiles
    patch = side // across
    tall = rows * ny * nc
    frame = patch + 2 * LEFT

    sel = selector(width, lanes, width * y)

    def ordered(w):
        w = lax.dynamic_slice_in_dim(w, half * c, half, axis=0)
        return w.reshape(zhalf, ny, width, lanes).transpose(1, 0, 2, 3).reshape(half, lanes)

    def part(w, natural):
        w = lax.dynamic_slice_in_dim(w, half * c, half, axis=0) if natural else ordered(w)
        return dot_nt(sel, w).astype(BF16)

    small = jnp.stack([gains, biases]).reshape(-1, lanes)
    last = jnp.stack([gains[-1, -1], biases[-1, -1]])
    spots = [0, 320, 640]
    room = spots[1] - taps * width
    filters = jnp.pad(w_group.reshape(blocks, -1, lanes), ((0, 0), (0, room), (0, 0))).reshape(-1, lanes)
    owned = dot_nt(sel, jnp.concatenate([filters[: filters.shape[0] - room]] + split_terms(small), axis=0))
    every = [dot_nt(selector(width, lanes, width * g), jnp.concatenate(split_terms(last), axis=0)) for g in range(ny)]
    table = jnp.concatenate([owned] + every, axis=1)
    at_small = spots[2] + taps * width
    at_last = owned.shape[1]
    table = jnp.pad(table, ((0, 0), (0, half - table.shape[1]))).astype(BF16)

    early = jnp.stack(
        [
            part(w_reduce[0], True),
            part(w_expand[0], False),
            part(w_reduce[1], False),
            part(w_expand[1], False),
            part(w_reduce[2], False),
            table,
        ]
    )
    early = lax.all_gather(early, "z", axis=1, tiled=True)
    final = lax.all_gather(ordered(w_expand[2]), "z", axis=0)
    matrices = [(early[0], early[1]), (early[2], early[3]), (early[4], None)]

    wide = jnp.pad(planes, ((0, 0), (0, 0), (LEFT, LEFT), (0, 0)))
    strips = jnp.stack([wide[:, :, patch * q : patch * q + frame] for q in range(across)], axis=1)
    strips = strips.reshape(nz, rows, frame, lanes)
    mixed = lax.all_to_all(strips, "z", 0, 0, tiled=True)
    mine = pick(c, mixed[:zhalf], mixed[zhalf:])
    theirs = swap_core(pick(c, mixed[zhalf:], mixed[:zhalf]), c)
    chip = jnp.concatenate([pick(c, mine, theirs), pick(c, theirs, mine)], axis=1)
    chip = chip.transpose(1, 2, 0, 3).reshape(rows * nc, frame, half)
    body = lax.all_gather(chip, "y", axis=0, tiled=True)
    above = lax.ppermute(body[tall - HALO :], "x", [(i, i + 1) for i in range(nx - 1)])
    below = lax.ppermute(body[:HALO], "x", [(i + 1, i) for i in range(nx - 1)])
    gathered = jnp.concatenate([above, body, below], axis=0)

    table = early[5]
    last = table[:, at_last : at_last + 6 * ny].astype(F32).reshape(nz, width, ny, 3, 2)
    last = (last[:, :, :, 0] + last[:, :, :, 1] + last[:, :, :, 2]).transpose(3, 0, 2, 1).reshape(2, nz, lanes)
    table = lax.dynamic_slice_in_dim(table, own * c, own, axis=0)
    small = table[:, at_small:at_last].astype(F32).reshape(own, 3, -1)
    small = (small[:, 0] + small[:, 1] + small[:, 2]).T.reshape(2, blocks, 3, own)
    group = lax.broadcasted_iota(jnp.int32, (own, 3 * own), 0) // width
    group = group == lax.broadcasted_iota(jnp.int32, (own, 3 * own), 1) % own // width

    def dense(b, s):
        start = spots[b] // lanes * lanes
        j = lax.broadcasted_iota(jnp.int32, (3 * lanes, 3 * own), 0) + start - spots[b]
        k = lax.broadcasted_iota(jnp.int32, (3 * lanes, 3 * own), 1)
        take = (j == (3 * (k // own) + s) * width + k % width).astype(BF16)
        full = jnp.dot(table[:, start : start + 3 * lanes], take, preferred_element_type=F32)
        return jnp.where(group, full, 0.0).astype(BF16)

    j = lax.broadcasted_iota(jnp.int32, (half, own), 0)
    k = lax.broadcasted_iota(jnp.int32, (half, own), 1)
    pull = (j == (k // width) * lanes + width * y + k % width).astype(BF16)
    stream = jnp.dot(gathered.reshape(-1, half), pull, preferred_element_type=F32).astype(BF16)
    stream = stream.reshape(tall + 2 * HALO, frame, own)

    column = patch * (z % across) - LEFT + lax.broadcasted_iota(jnp.int32, (1, frame, 1), 1)
    in_columns = (column >= 0) & (column < side)
    for b in range(blocks):
        gain, bias = small[0, b], small[1, b]
        reach = HALO - b
        high = tall + 2 * reach
        if b:
            gathered = lax.all_gather(stream.reshape(-1, own), "y", axis=1, tiled=True)
        first = contract(gathered.reshape(-1, half), matrices[b][0], c).reshape(high, frame, own)
        row = tall * x - reach + lax.broadcasted_iota(jnp.int32, (high, 1, 1), 0)
        inside = (row >= 0) & (row < side) & in_columns
        hidden = jnp.where(inside, jnp.maximum(gain[0] * first + bias[0], 0.0), 0.0).astype(BF16)
        high -= 2
        rows3 = jnp.concatenate([hidden[r : r + high] for r in range(3)], axis=-1).reshape(-1, 3 * own)
        left, mid, right = (dot_nt(rows3, dense(b, s)).reshape(high, frame, own) for s in range(3))
        edge = jnp.zeros((high, 1, own), F32)
        spatial = (
            jnp.concatenate([edge, left[:, :-1]], axis=1) + mid + jnp.concatenate([right[:, 1:], edge], axis=1)
        )
        middle = jnp.maximum(gain[1] * spatial + bias[1], 0.0).astype(BF16)
        if b < blocks - 1:
            middle = lax.all_gather(middle.reshape(-1, own), "y", axis=1, tiled=True)
            second = contract(middle, matrices[b][1], c).reshape(high, frame, own)
            stream = jnp.maximum(gain[2] * second + bias[2] + stream[1:-1].astype(F32), 0.0).astype(BF16)

    deep = rows * nc
    spots_of_chip = deep * patch
    middle = middle[:, LEFT : LEFT + patch].reshape(ny, spots_of_chip, own)
    middle = lax.all_to_all(middle, "y", 0, 0, tiled=True).transpose(1, 0, 2).reshape(spots_of_chip, half)
    partial = lax.dot_general(middle, final, (((1,), (1,)), ((), ())), preferred_element_type=F32)
    partial = partial.reshape(nc, rows * patch, nz, lanes)
    kept = gathered.reshape(tall + 2, frame, half)[:, LEFT : LEFT + patch]
    kept = lax.dynamic_slice_in_dim(kept, 1 + deep * y, deep, axis=0).reshape(spots_of_chip, half)
    j = lax.broadcasted_iota(jnp.int32, (half, half), 0)
    k = lax.broadcasted_iota(jnp.int32, (half, half), 1)
    natural = (j == (k // width % ny) * own + k // lanes * width + k % width).astype(BF16)
    kept = jnp.dot(kept, natural, preferred_element_type=F32).astype(BF16)
    kept = kept.reshape(nc, rows * patch, zhalf, lanes)
    send = jnp.concatenate([pick(c, partial[1], partial[0]).astype(BF16), pick(c, kept[1], kept[0])], axis=1)
    got = swap_core(send, c)
    mine, theirs = pick(c, kept[0], kept[1]), got[:, nz:]
    residual = jnp.concatenate([pick(c, mine, theirs), pick(c, theirs, mine)], axis=1)
    second = pick(c, partial[0], partial[1]) + got[:, :nz].astype(F32)
    out = jnp.maximum(last[0] * second + last[1] + residual.astype(F32), 0.0).astype(BF16)
    out = out.transpose(1, 0, 2).reshape(nz, rows, patch, lanes)
    out = lax.all_to_all(out, "z", 0, 0, tiled=True).reshape(tiles, across, rows, patch, lanes)
    return out.transpose(0, 2, 1, 3, 4).reshape(tiles, rows, side, lanes)


def solution(mesh):
    grid = Mesh(mesh.devices.reshape(4, 4, 2, 16), ("x", "y", "c", "z"))
    placed = (
        P(None, SEG, None, "z"),
        P(None, None, "z"),
        P(None, None, None, "z"),
        P(None, None, "z"),
        P(None, None, "z"),
        P(None, None, "z"),
    )
    return jax.shard_map(local, mesh=grid, in_specs=placed, out_specs=P(None, SEG, None, "z"), check_vma=False)
```

```python
import functools

import jax
import jax.numpy as jnp
from jax import lax
from jax.experimental import pallas as pl
from jax.experimental.pallas import tpu as pltpu
from jax.sharding import Mesh
from jax.sharding import PartitionSpec as P

BF16 = jnp.bfloat16
F32 = jnp.float32
SEG = ("x", "y", "c")
LEFT = 4
HALO = 3


def dot_nt(a, b):
    return lax.dot_general(a, b, (((1,), (1,)), ((), ())), preferred_element_type=F32)


def selector(rows, cols, base):
    i = lax.broadcasted_iota(jnp.int32, (rows, cols), 0)
    j = lax.broadcasted_iota(jnp.int32, (rows, cols), 1)
    return (j == i + base).astype(BF16)


def terms(v):
    out = []
    for _ in range(3):
        t = v.astype(BF16).astype(F32)
        out.append(t)
        v = v - t
    return out


def pick(c, a, b):
    return jnp.where(c == 0, a, b)


def swap_core(v, c):
    both = lax.all_gather(v, "c", axis=0)
    return pick(c, both[1], both[0])


SPOTS = (0, 320, 640)
OWNED, OWNED_STEP = 928, 24
LAST, LAST_STEP = 1000, 8
VMEM_LIMIT = 24 * 1024 * 1024


def prep_kernel(at, wr_ref, we_ref, wg_ref, owned_ref, last_ref, out_ref, table):
    y = at[0]
    width, half = out_ref.shape[1:]
    lanes = wr_ref.shape[2]
    ny = lanes // width
    zhalf = half // lanes
    sel = selector(width, lanes, width * y)

    def put(slot, w):
        w = w.reshape(zhalf, ny, width, lanes)
        for g in range(ny):
            rows = w[:, g].reshape(zhalf * width, lanes)
            out_ref[slot, :, g * zhalf * width : (g + 1) * zhalf * width] = dot_nt(sel, rows).astype(BF16)

    out_ref[0] = dot_nt(sel, wr_ref[0]).astype(BF16)
    put(1, we_ref[0])
    put(2, wr_ref[1])
    put(3, we_ref[1])
    put(4, wr_ref[2])
    table[...] = jnp.zeros_like(table)
    for b, spot in enumerate(SPOTS):
        table[spot : spot + wg_ref.shape[1]] = wg_ref[b].astype(F32)
    for t, v in enumerate(terms(owned_ref[...])):
        table[OWNED + OWNED_STEP * t : OWNED + OWNED_STEP * (t + 1)] = v
    for t, v in enumerate(terms(last_ref[...])):
        table[LAST + LAST_STEP * t : LAST + LAST_STEP * (t + 1)] = v
    row = lax.broadcasted_iota(jnp.int32, table.shape, 0)
    lane = lax.broadcasted_iota(jnp.int32, table.shape, 1)
    wanted = jnp.where(row < LAST, y, ((row - LAST) & (LAST_STEP - 1)) >> 1)
    kept = jnp.where((lane >> 5) == wanted, table[...], 0.0).astype(BF16)
    i = lax.broadcasted_iota(jnp.int32, (width, lanes), 0)
    j = lax.broadcasted_iota(jnp.int32, (width, lanes), 1)
    out_ref[5] = dot_nt(((j & (width - 1)) == i).astype(BF16), kept).astype(BF16)


def prepare(y, c, w_reduce, w_expand, w_group, gains, biases):
    blocks, depth, lanes = w_reduce.shape
    width = w_group.shape[2]
    half = depth // 2
    owned = jnp.stack([gains, biases]).reshape(-1, lanes)
    owned = jnp.pad(owned, ((0, OWNED_STEP - owned.shape[0]), (0, 0)))
    last = jnp.tile(jnp.stack([gains[-1, -1], biases[-1, -1]]), (lanes // width, 1))
    whole = lambda *shape: pl.BlockSpec(shape, lambda i, at: (0,) * len(shape))
    return pl.pallas_call(
        prep_kernel,
        out_shape=jax.ShapeDtypeStruct((6, width, half), BF16),
        grid_spec=pltpu.PrefetchScalarGridSpec(
            num_scalar_prefetch=1,
            grid=(1,),
            in_specs=[
                pl.BlockSpec((3, half, lanes), lambda i, at: (0, at[1], 0)),
                pl.BlockSpec((2, half, lanes), lambda i, at: (0, at[1], 0)),
                whole(blocks, 9 * width, lanes),
                whole(OWNED_STEP, lanes),
                whole(LAST_STEP, lanes),
            ],
            out_specs=whole(6, width, half),
            scratch_shapes=[pltpu.VMEM((half, lanes), F32)],
        ),
        compiler_params=pltpu.CompilerParams(vmem_limit_bytes=VMEM_LIMIT),
        cost_estimate=pl.CostEstimate(flops=2 * 6 * half * lanes * width, bytes_accessed=2_500_000, transcendentals=0),
    )(jnp.stack([y, c]), w_reduce, w_expand, w_group.reshape(blocks, -1, lanes), owned, last)


def conv_kernel(b, high, width, trim, side, at, part_ref, got_ref, table_ref, out_ref, after_ref):
    c, row0, col0 = at[0], at[1], at[2]
    own = got_ref.shape[2]
    frame = part_ref.shape[0] // (high + 2)
    table = table_ref[...]
    i = lax.broadcasted_iota(jnp.int32, (own, own), 0)
    j = lax.broadcasted_iota(jnp.int32, (own, own), 1)
    tail = table[:, OWNED // 128 * 128 :]
    eye = (i == j).astype(BF16)
    rows = lax.dot_general(tail, eye, (((0,), (0,)), ((), ())), preferred_element_type=F32)

    def param(which, k):
        at_row = OWNED % 128 + (which * 3 + b) * 3 + k
        return sum(rows[at_row + OWNED_STEP * t : at_row + OWNED_STEP * t + 1] for t in range(3))

    first = part_ref[:, pl.ds(pl.multiple_of(own * c, own), own)] + got_ref[1 - c].astype(F32)
    hidden = jnp.maximum(param(0, 0) * first + param(1, 0), 0.0).reshape(high + 2, frame, own)
    row = row0 + lax.broadcasted_iota(jnp.int32, hidden.shape, 0)
    col = col0 + lax.broadcasted_iota(jnp.int32, hidden.shape, 1)
    inside = (row >= 0) & (row < side) & (col >= 0) & (col < side)
    hidden = jnp.where(inside, hidden, 0.0)
    spread = ((lax.broadcasted_iota(jnp.int32, (width, own), 1) & (width - 1)) == lax.broadcasted_iota(jnp.int32, (width, own), 0)).astype(BF16)
    same = (i >> 5) == (j >> 5)
    sums = [None] * 3
    for r in range(3):
        shifted = hidden[r : r + high].reshape(high * frame, own).astype(BF16)
        for s in range(3):
            spot = SPOTS[b] + (3 * r + s) * width
            taps = jnp.dot(table[:, spot : spot + width], spread, preferred_element_type=F32)
            taps = jnp.where(same, taps, 0.0).astype(BF16)
            term = dot_nt(shifted, taps)
            sums[s] = term if r == 0 else sums[s] + term
    spatial = pltpu.roll(sums[0], 1, 0) + sums[1] + pltpu.roll(sums[2], high * frame - 1, 0)
    middle = jnp.maximum(param(0, 1) * spatial + param(1, 1), 0.0)
    if trim:
        lo, hi = trim
        middle = middle.reshape(high, frame, own)[:, lo:hi].reshape(high * (hi - lo), own)
    out_ref[...] = middle.astype(BF16)
    after_ref[0:1] = param(0, 2)
    after_ref[1:2] = param(1, 2)


def convolve(b, high, width, trim, side, at, part, got, early):
    own = got.shape[2]
    frame = part.shape[0] // (high + 2)
    cols = trim[1] - trim[0] if trim else frame
    whole = lambda shape: pl.BlockSpec(shape, lambda i, at: (0,) * len(shape))
    return pl.pallas_call(
        functools.partial(conv_kernel, b, high, width, trim, side),
        out_shape=(jax.ShapeDtypeStruct((high * cols, own), BF16), jax.ShapeDtypeStruct((8, own), F32)),
        grid_spec=pltpu.PrefetchScalarGridSpec(
            num_scalar_prefetch=1,
            grid=(1,),
            in_specs=[
                whole(part.shape),
                whole(got.shape),
                pl.BlockSpec((pl.Squeezed(), own, early.shape[2]), lambda i, at: (5, at[0], 0)),
            ],
            out_specs=(whole((high * cols, own)), whole((8, own))),
        ),
        compiler_params=pltpu.CompilerParams(vmem_limit_bytes=VMEM_LIMIT),
        cost_estimate=pl.CostEstimate(flops=18 * high * frame * own * own, bytes_accessed=2_500_000, transcendentals=0),
    )(at, part, got, early)


def halves(part, c):
    half = part.shape[1] // 2
    mine, other = pick(c, part[:, :half], part[:, half:]), pick(c, part[:, half:], part[:, :half])
    return mine, lax.all_gather(other.astype(BF16), "c", axis=0)


def local(planes, w_reduce, w_group, w_expand, gains, biases):
    nx, ny, nc, nz = (lax.axis_size(a) for a in ("x", "y", "c", "z"))
    x, y, c, z = (lax.axis_index(a) for a in ("x", "y", "c", "z"))
    tiles, rows, side, lanes = planes.shape
    blocks, _, width, _ = w_group.shape
    channels = lanes * nz
    half = channels // nc
    zhalf = nz // nc
    own = zhalf * width
    across = nz // tiles
    patch = side // across
    tall = rows * ny * nc
    frame = patch + 2 * LEFT

    early = lax.all_gather(prepare(y, c, w_reduce, w_expand, w_group, gains, biases), "z", axis=1, tiled=True)
    matrices = [(early[0], early[1]), (early[2], early[3]), (early[4], None)]
    final = lax.dynamic_slice_in_dim(w_expand[2], half * c, half, axis=0)
    final = final.reshape(zhalf, ny, width, lanes).transpose(1, 0, 2, 3).reshape(half, lanes)
    final = lax.all_gather(final, "z", axis=0)

    wide = jnp.pad(planes, ((0, 0), (0, 0), (LEFT, LEFT), (0, 0)))
    strips = jnp.stack([wide[:, :, patch * q : patch * q + frame] for q in range(across)], axis=1)
    strips = strips.reshape(nz, rows, frame, lanes)
    mixed = lax.all_to_all(strips, "z", 0, 0, tiled=True)
    mine = pick(c, mixed[:zhalf], mixed[zhalf:])
    theirs = swap_core(pick(c, mixed[zhalf:], mixed[:zhalf]), c)
    chip = jnp.concatenate([pick(c, mine, theirs), pick(c, theirs, mine)], axis=1)
    chip = chip.transpose(1, 2, 0, 3).reshape(rows * nc, frame, half)
    body = lax.all_gather(chip, "y", axis=0, tiled=True)
    above = lax.ppermute(body[tall - HALO :], "x", [(i, i + 1) for i in range(nx - 1)])
    below = lax.ppermute(body[:HALO], "x", [(i + 1, i) for i in range(nx - 1)])
    gathered = jnp.concatenate([above, body, below], axis=0)

    last = early[5, :, LAST : LAST + 3 * LAST_STEP].astype(F32).reshape(nz, width, 3, ny, 2)
    last = (last[:, :, 0] + last[:, :, 1] + last[:, :, 2]).transpose(3, 0, 2, 1).reshape(2, nz, lanes)

    j = lax.broadcasted_iota(jnp.int32, (half, own), 0)
    k = lax.broadcasted_iota(jnp.int32, (half, own), 1)
    pull = (j == (k // width) * lanes + width * y + k % width).astype(BF16)
    stream = jnp.dot(gathered.reshape(-1, half), pull, preferred_element_type=F32).astype(BF16)
    stream = stream.reshape(tall + 2 * HALO, frame, own)

    for b in range(blocks):
        high = tall + 2 * (HALO - b)
        if b:
            gathered = lax.all_gather(stream.reshape(-1, own), "y", axis=1, tiled=True)
        part = dot_nt(gathered.reshape(-1, half), matrices[b][0])
        other = pick(c, part[:, own:], part[:, :own]).astype(BF16)
        at = jnp.stack([c, tall * x - (HALO - b), patch * (z % across) - LEFT])
        high -= 2
        trim = (LEFT, LEFT + patch) if b == blocks - 1 else None
        middle, after = convolve(b, high, width, trim, side, at, part, lax.all_gather(other, "c", axis=0), early)
        if b < blocks - 1:
            middle = lax.all_gather(middle, "y", axis=1, tiled=True)
            mine, got = halves(dot_nt(middle, matrices[b][1]), c)
            second = (mine + pick(c, got[1], got[0]).astype(F32)).reshape(high, frame, own)
            stream = jnp.maximum(after[0] * second + after[1] + stream[1:-1].astype(F32), 0.0).astype(BF16)

    deep = rows * nc
    spots_of_chip = deep * patch
    middle = lax.all_to_all(middle.reshape(ny, spots_of_chip, own), "y", 0, 0, tiled=True).transpose(1, 0, 2).reshape(spots_of_chip, half)
    partial = lax.dot_general(middle, final, (((1,), (1,)), ((), ())), preferred_element_type=F32)
    partial = partial.reshape(nc, rows * patch, nz, lanes)
    kept = gathered.reshape(tall + 2, frame, half)[:, LEFT : LEFT + patch]
    kept = lax.dynamic_slice_in_dim(kept, 1 + deep * y, deep, axis=0).reshape(spots_of_chip, half)
    j = lax.broadcasted_iota(jnp.int32, (half, half), 0)
    k = lax.broadcasted_iota(jnp.int32, (half, half), 1)
    natural = (j == (k // width % ny) * own + k // lanes * width + k % width).astype(BF16)
    kept = jnp.dot(kept, natural, preferred_element_type=F32).astype(BF16)
    kept = kept.reshape(nc, rows * patch, zhalf, lanes)
    send = jnp.concatenate([pick(c, partial[1], partial[0]).astype(BF16), pick(c, kept[1], kept[0])], axis=1)
    got = swap_core(send, c)
    mine, theirs = pick(c, kept[0], kept[1]), got[:, nz:]
    residual = jnp.concatenate([pick(c, mine, theirs), pick(c, theirs, mine)], axis=1)
    second = pick(c, partial[0], partial[1]) + got[:, :nz].astype(F32)
    out = jnp.maximum(last[0] * second + last[1] + residual.astype(F32), 0.0).astype(BF16)
    out = out.transpose(1, 0, 2).reshape(nz, rows, patch, lanes)
    out = lax.all_to_all(out, "z", 0, 0, tiled=True).reshape(tiles, across, rows, patch, lanes)
    return out.transpose(0, 2, 1, 3, 4).reshape(tiles, rows, side, lanes)


def solution(mesh):
    grid = Mesh(mesh.devices.reshape(4, 4, 2, 16), ("x", "y", "c", "z"))
    placed = (
        P(None, SEG, None, "z"),
        P(None, None, "z"),
        P(None, None, None, "z"),
        P(None, None, "z"),
        P(None, None, "z"),
        P(None, None, "z"),
    )
    return jax.shard_map(local, mesh=grid, in_specs=placed, out_specs=P(None, SEG, None, "z"), check_vma=False)
```

```python
import functools

import jax
import jax.numpy as jnp
from jax import lax
from jax.experimental import pallas as pl
from jax.experimental.pallas import tpu as pltpu
from jax.sharding import Mesh
from jax.sharding import PartitionSpec as P

BF16 = jnp.bfloat16
F32 = jnp.float32
SEG = ("x", "y", "c")
LEFT = 4
HALO = 3


def dot_nt(a, b):
    return lax.dot_general(a, b, (((1,), (1,)), ((), ())), preferred_element_type=F32)


def selector(rows, cols, base):
    i = lax.broadcasted_iota(jnp.int32, (rows, cols), 0)
    j = lax.broadcasted_iota(jnp.int32, (rows, cols), 1)
    return (j == i + base).astype(BF16)


def terms(v):
    out = []
    for _ in range(3):
        t = v.astype(BF16).astype(F32)
        out.append(t)
        v = v - t
    return out


def pick(c, a, b):
    return jnp.where(c == 0, a, b)


def swap_core(v, c):
    both = lax.all_gather(v, "c", axis=0)
    return pick(c, both[1], both[0])


SPOTS = (0, 320, 640)
OWNED, OWNED_STEP = 928, 24
LAST, LAST_STEP = 1000, 8
VMEM_LIMIT = 12 * 1024 * 1024


def prep_kernel(at, wr_hbm, we_hbm, wg_hbm, gains_ref, biases_ref, out_ref, wr_ref, we_ref, wg_ref, table, sems):
    y, c = at[0], at[1]
    width, half = out_ref.shape[1:]
    lanes = wr_ref.shape[2]
    ny = lanes // width
    zhalf = half // lanes
    rows = pl.ds(pl.multiple_of(half * c, half), half)
    copies = [pltpu.make_async_copy(wg_hbm, wg_ref, sems.at[0])]
    for b in range(3):
        copies.append(pltpu.make_async_copy(wr_hbm.at[b, rows], wr_ref.at[b], sems.at[1 + b]))
    for b in range(2):
        copies.append(pltpu.make_async_copy(we_hbm.at[b, rows], we_ref.at[b], sems.at[4 + b]))
    for copy in copies:
        copy.start()
    sel = selector(width, lanes, width * y)

    table[...] = jnp.zeros_like(table)
    for which, ref in enumerate((gains_ref, biases_ref)):
        for b in range(3):
            for t, v in enumerate(terms(ref[b])):
                spot = OWNED + OWNED_STEP * t + 3 * (3 * which + b)
                table[spot : spot + 3] = v
                if b == 2:
                    for g in range(ny):
                        spot = LAST + LAST_STEP * t + 2 * g + which
                        table[spot : spot + 1] = v[2:3]
    copies[0].wait()
    for b, spot in enumerate(SPOTS):
        table[spot : spot + wg_ref.shape[1]] = wg_ref[b].astype(F32)
    row = lax.broadcasted_iota(jnp.int32, table.shape, 0)
    lane = lax.broadcasted_iota(jnp.int32, table.shape, 1)
    wanted = jnp.where(row < LAST, y, ((row - LAST) & (LAST_STEP - 1)) >> 1)
    kept = jnp.where((lane >> 5) == wanted, table[...], 0.0).astype(BF16)
    i = lax.broadcasted_iota(jnp.int32, (width, lanes), 0)
    j = lax.broadcasted_iota(jnp.int32, (width, lanes), 1)
    out_ref[5] = dot_nt(((j & (width - 1)) == i).astype(BF16), kept).astype(BF16)

    def put(slot, w):
        w = w.reshape(zhalf, ny, width, lanes)
        for g in range(ny):
            rows = w[:, g].reshape(zhalf * width, lanes)
            out_ref[slot, :, g * zhalf * width : (g + 1) * zhalf * width] = dot_nt(sel, rows).astype(BF16)

    copies[1].wait()
    out_ref[0] = dot_nt(sel, wr_ref[0]).astype(BF16)
    copies[2].wait()
    put(2, wr_ref[1])
    copies[3].wait()
    put(4, wr_ref[2])
    copies[4].wait()
    put(1, we_ref[0])
    copies[5].wait()
    put(3, we_ref[1])


def prepare(y, c, w_reduce, w_expand, w_group, gains, biases):
    blocks, depth, lanes = w_reduce.shape
    width = w_group.shape[2]
    half = depth // 2
    whole = lambda *shape: pl.BlockSpec(shape, lambda i, at: (0,) * len(shape))
    there = pl.BlockSpec(memory_space=pl.ANY)
    return pl.pallas_call(
        prep_kernel,
        out_shape=jax.ShapeDtypeStruct((6, width, half), BF16),
        grid_spec=pltpu.PrefetchScalarGridSpec(
            num_scalar_prefetch=1,
            grid=(1,),
            in_specs=[there, there, there, whole(*gains.shape), whole(*biases.shape)],
            out_specs=whole(6, width, half),
            scratch_shapes=[
                pltpu.VMEM((3, half, lanes), BF16),
                pltpu.VMEM((2, half, lanes), BF16),
                pltpu.VMEM((blocks, 9 * width, lanes), BF16),
                pltpu.VMEM((half, lanes), F32),
                pltpu.SemaphoreType.DMA((6,)),
            ],
        ),
        compiler_params=pltpu.CompilerParams(vmem_limit_bytes=60 * 1024 * 1024),
        cost_estimate=pl.CostEstimate(flops=2 * 6 * half * lanes * width, bytes_accessed=2_500_000, transcendentals=0),
    )(jnp.stack([y, c]), w_reduce, w_expand, w_group.reshape(blocks, -1, lanes), gains, biases)


def conv_kernel(b, high, width, trim, side, at, part_ref, got_ref, table_ref, out_ref, after_ref):
    c, row0, col0 = at[0], at[1], at[2]
    own = got_ref.shape[2]
    frame = part_ref.shape[0] // (high + 2)
    table = table_ref[pl.ds(pl.multiple_of(own * c, own), own)]
    i = lax.broadcasted_iota(jnp.int32, (own, own), 0)
    j = lax.broadcasted_iota(jnp.int32, (own, own), 1)
    tail = table[:, OWNED // 128 * 128 :]
    eye = (i == j).astype(BF16)
    rows = lax.dot_general(tail, eye, (((0,), (0,)), ((), ())), preferred_element_type=F32)

    def param(which, k):
        at_row = OWNED % 128 + (which * 3 + b) * 3 + k
        return sum(rows[at_row + OWNED_STEP * t : at_row + OWNED_STEP * t + 1] for t in range(3))

    first = part_ref[:, pl.ds(pl.multiple_of(own * c, own), own)] + got_ref[1 - c].astype(F32)
    hidden = jnp.maximum(param(0, 0) * first + param(1, 0), 0.0).reshape(high + 2, frame, own)
    row = row0 + lax.broadcasted_iota(jnp.int32, hidden.shape, 0)
    col = col0 + lax.broadcasted_iota(jnp.int32, hidden.shape, 1)
    inside = (row >= 0) & (row < side) & (col >= 0) & (col < side)
    hidden = jnp.where(inside, hidden, 0.0)
    spread = ((lax.broadcasted_iota(jnp.int32, (width, own), 1) & (width - 1)) == lax.broadcasted_iota(jnp.int32, (width, own), 0)).astype(BF16)
    same = (i >> 5) == (j >> 5)
    sums = [None] * 3
    for r in range(3):
        shifted = hidden[r : r + high].reshape(high * frame, own).astype(BF16)
        for s in range(3):
            spot = SPOTS[b] + (3 * r + s) * width
            taps = jnp.dot(table[:, spot : spot + width], spread, preferred_element_type=F32)
            taps = jnp.where(same, taps, 0.0).astype(BF16)
            term = dot_nt(shifted, taps)
            sums[s] = term if r == 0 else sums[s] + term
    spatial = pltpu.roll(sums[0], 1, 0) + sums[1] + pltpu.roll(sums[2], high * frame - 1, 0)
    middle = jnp.maximum(param(0, 1) * spatial + param(1, 1), 0.0)
    if trim:
        lo, hi = trim
        middle = middle.reshape(high, frame, own)[:, lo:hi].reshape(high * (hi - lo), own)
    out_ref[...] = middle.astype(BF16)
    after_ref[0:1] = param(0, 2)
    after_ref[1:2] = param(1, 2)


ON_CHIP = pl.BlockSpec(memory_space=pltpu.VMEM)
SCALARS = pl.BlockSpec(memory_space=pltpu.SMEM)


def convolve(b, high, width, trim, side, at, part, got, table):
    own = got.shape[2]
    frame = part.shape[0] // (high + 2)
    cols = trim[1] - trim[0] if trim else frame
    return pl.pallas_call(
        functools.partial(conv_kernel, b, high, width, trim, side),
        out_shape=(jax.ShapeDtypeStruct((high * cols, own), BF16), jax.ShapeDtypeStruct((8, own), F32)),
        in_specs=[SCALARS, ON_CHIP, ON_CHIP, ON_CHIP],
        out_specs=(ON_CHIP, ON_CHIP),
        compiler_params=pltpu.CompilerParams(vmem_limit_bytes=VMEM_LIMIT),
        cost_estimate=pl.CostEstimate(flops=18 * high * frame * own * own, bytes_accessed=2_500_000, transcendentals=0),
    )(at, part, got, table)


def last_kernel(at, middle_ref, w_ref, kept_ref, mine_ref, send_ref, sums):
    c = at[0]
    many, half, lanes = w_ref.shape
    middle = jnp.concatenate([middle_ref[g] for g in range(middle_ref.shape[0])], axis=1)
    for k in range(many):
        sums[:, k * lanes : (k + 1) * lanes] = jnp.dot(middle, w_ref[k], preferred_element_type=F32)
    rows = mine_ref.shape[0]
    mine = pl.ds(pl.multiple_of(rows * c, rows), rows)
    other = pl.ds(pl.multiple_of(rows * (1 - c), rows), rows)
    mine_ref[...] = sums[mine]
    send_ref[:, : many * lanes] = sums[other].astype(BF16)
    send_ref[:, many * lanes :] = kept_ref[other]


def multiply_last(at, middle, w, kept):
    many, half, lanes = w.shape
    rows = kept.shape[0]
    return pl.pallas_call(
        last_kernel,
        out_shape=(
            jax.ShapeDtypeStruct((rows // 2, many * lanes), F32),
            jax.ShapeDtypeStruct((rows // 2, many * lanes + half), BF16),
        ),
        in_specs=[SCALARS, ON_CHIP, ON_CHIP, ON_CHIP],
        out_specs=(ON_CHIP, ON_CHIP),
        scratch_shapes=[pltpu.VMEM((rows, many * lanes), F32)],
        compiler_params=pltpu.CompilerParams(vmem_limit_bytes=VMEM_LIMIT),
        cost_estimate=pl.CostEstimate(flops=2 * rows * half * many * lanes, bytes_accessed=5_000_000, transcendentals=0),
    )(at, middle, w, kept)


def halves(part, c):
    half = part.shape[1] // 2
    mine, other = pick(c, part[:, :half], part[:, half:]), pick(c, part[:, half:], part[:, :half])
    return mine, lax.all_gather(other.astype(BF16), "c", axis=0)


def local(planes, w_reduce, w_group, w_expand, gains, biases):
    nx, ny, nc, nz = (lax.axis_size(a) for a in ("x", "y", "c", "z"))
    x, y, c, z = (lax.axis_index(a) for a in ("x", "y", "c", "z"))
    tiles, rows, side, lanes = planes.shape
    blocks, _, width, _ = w_group.shape
    channels = lanes * nz
    half = channels // nc
    zhalf = nz // nc
    own = zhalf * width
    across = nz // tiles
    patch = side // across
    tall = rows * ny * nc
    frame = patch + 2 * LEFT

    early = lax.all_gather(prepare(y, c, w_reduce, w_expand, w_group, gains, biases), "z", axis=1, tiled=True)
    table = lax.optimization_barrier(early[5])
    final = lax.dynamic_slice_in_dim(w_expand[2], half * c, half, axis=0)
    final = final.reshape(zhalf, ny, width, lanes).transpose(1, 0, 2, 3).reshape(half, lanes)
    final = lax.all_gather(final, "z", axis=0)

    wide = jnp.pad(planes, ((0, 0), (0, 0), (LEFT, LEFT), (0, 0)))
    strips = jnp.stack([wide[:, :, patch * q : patch * q + frame] for q in range(across)], axis=1)
    strips = strips.reshape(nz, rows, frame, lanes)
    mixed = lax.all_to_all(strips, "z", 0, 0, tiled=True)
    mine = pick(c, mixed[:zhalf], mixed[zhalf:])
    theirs = swap_core(pick(c, mixed[zhalf:], mixed[:zhalf]), c)
    chip = jnp.concatenate([pick(c, mine, theirs), pick(c, theirs, mine)], axis=1)
    chip = chip.transpose(1, 2, 0, 3).reshape(rows * nc, frame, half)
    body = lax.all_gather(chip, "y", axis=0, tiled=True)
    above = lax.ppermute(body[tall - HALO :], "x", [(i, i + 1) for i in range(nx - 1)])
    below = lax.ppermute(body[:HALO], "x", [(i + 1, i) for i in range(nx - 1)])
    gathered = jnp.concatenate([above, body, below], axis=0)

    last = table[:, LAST : LAST + 3 * LAST_STEP].astype(F32).reshape(nz, width, 3, ny, 2)
    last = (last[:, :, 0] + last[:, :, 1] + last[:, :, 2]).transpose(3, 0, 2, 1).reshape(2, nz, lanes)

    j = lax.broadcasted_iota(jnp.int32, (half, own), 0)
    k = lax.broadcasted_iota(jnp.int32, (half, own), 1)
    pull = (j == (k // width) * lanes + width * y + k % width).astype(BF16)
    stream = jnp.dot(gathered.reshape(-1, half), pull, preferred_element_type=F32).astype(BF16)
    stream = stream.reshape(tall + 2 * HALO, frame, own)

    for b in range(blocks):
        high = tall + 2 * (HALO - b)
        if b:
            gathered = lax.all_gather(stream.reshape(-1, own), "y", axis=1, tiled=True)
        part = dot_nt(gathered.reshape(-1, half), early[2 * b])
        other = pick(c, part[:, own:], part[:, :own]).astype(BF16)
        at = jnp.stack([c, tall * x - (HALO - b), patch * (z % across) - LEFT])
        high -= 2
        trim = (LEFT, LEFT + patch) if b == blocks - 1 else None
        middle, after = convolve(b, high, width, trim, side, at, part, lax.all_gather(other, "c", axis=0), table)
        if b < blocks - 1:
            middle = lax.all_gather(middle, "y", axis=1, tiled=True)
            mine, got = halves(dot_nt(middle, early[2 * b + 1]), c)
            second = (mine + pick(c, got[1], got[0]).astype(F32)).reshape(high, frame, own)
            stream = jnp.maximum(after[0] * second + after[1] + stream[1:-1].astype(F32), 0.0).astype(BF16)

    deep = rows * nc
    spots_of_chip = deep * patch
    middle = lax.all_to_all(middle.reshape(ny, spots_of_chip, own), "y", 0, 0, tiled=True)
    kept = gathered.reshape(tall + 2, frame, half)[:, LEFT : LEFT + patch]
    kept = lax.dynamic_slice_in_dim(kept, 1 + deep * y, deep, axis=0).reshape(spots_of_chip, half)
    j = lax.broadcasted_iota(jnp.int32, (half, half), 0)
    k = lax.broadcasted_iota(jnp.int32, (half, half), 1)
    natural = (j == (k // width % ny) * own + k // lanes * width + k % width).astype(BF16)
    kept = jnp.dot(kept, natural, preferred_element_type=F32).astype(BF16)
    second, send = multiply_last(at, middle, final, kept)
    got = swap_core(send, c)
    kept = kept.reshape(nc, rows * patch, half)
    mine, theirs = pick(c, kept[0], kept[1]), got[:, nz * lanes :]
    residual = jnp.concatenate([pick(c, mine, theirs), pick(c, theirs, mine)], axis=1)
    second = second + got[:, : nz * lanes].astype(F32)
    gain, bias = last.reshape(2, 1, nz * lanes)
    out = jnp.maximum(gain * second + bias + residual.astype(F32), 0.0).astype(BF16)
    out = out.reshape(rows * patch, nz, lanes)
    out = out.transpose(1, 0, 2).reshape(nz, rows, patch, lanes)
    out = lax.all_to_all(out, "z", 0, 0, tiled=True).reshape(tiles, across, rows, patch, lanes)
    return out.transpose(0, 2, 1, 3, 4).reshape(tiles, rows, side, lanes)


def solution(mesh):
    grid = Mesh(mesh.devices.reshape(4, 4, 2, 16), ("x", "y", "c", "z"))
    placed = (
        P(None, SEG, None, "z"),
        P(None, None, "z"),
        P(None, None, None, "z"),
        P(None, None, "z"),
        P(None, None, "z"),
        P(None, None, "z"),
    )
    return jax.shard_map(local, mesh=grid, in_specs=placed, out_specs=P(None, SEG, None, "z"), check_vma=False)
```

```python
import functools

import jax
import jax.numpy as jnp
from jax import lax
from jax.experimental import pallas as pl
from jax.experimental.pallas import tpu as pltpu
from jax.sharding import Mesh
from jax.sharding import PartitionSpec as P

BF16 = jnp.bfloat16
F32 = jnp.float32
SEG = ("x", "y", "c")
LEFT = 4
HALO = 3


def dot_nt(a, b):
    return lax.dot_general(a, b, (((1,), (1,)), ((), ())), preferred_element_type=F32)


def selector(rows, cols, base):
    i = lax.broadcasted_iota(jnp.int32, (rows, cols), 0)
    j = lax.broadcasted_iota(jnp.int32, (rows, cols), 1)
    return (j == i + base).astype(BF16)


def terms(v):
    out = []
    for _ in range(3):
        t = v.astype(BF16).astype(F32)
        out.append(t)
        v = v - t
    return out


def pick(c, a, b):
    return jnp.where(c == 0, a, b)


def swap_core(v, c):
    both = lax.all_gather(v, "c", axis=0)
    return pick(c, both[1], both[0])


SPOTS = (0, 320, 640)
OWNED, OWNED_STEP = 928, 24
LAST, LAST_STEP = 1000, 8
VMEM_LIMIT = 12 * 1024 * 1024


def prep_kernel(at, wr_hbm, we_hbm, wg_hbm, gains_ref, biases_ref, out_ref, wr_ref, we_ref, wg_ref, table, sems):
    y, c = at[0], at[1]
    width, half = out_ref.shape[1:]
    lanes = wr_ref.shape[2]
    ny = lanes // width
    zhalf = half // lanes
    rows = pl.ds(pl.multiple_of(half * c, half), half)
    copies = [pltpu.make_async_copy(wg_hbm, wg_ref, sems.at[0])]
    for b in range(3):
        copies.append(pltpu.make_async_copy(wr_hbm.at[b, rows], wr_ref.at[b], sems.at[1 + b]))
    for b in range(2):
        copies.append(pltpu.make_async_copy(we_hbm.at[b, rows], we_ref.at[b], sems.at[4 + b]))
    for copy in copies:
        copy.start()
    sel = selector(width, lanes, width * y)

    table[...] = jnp.zeros_like(table)
    for which, ref in enumerate((gains_ref, biases_ref)):
        for b in range(3):
            for t, v in enumerate(terms(ref[b])):
                spot = OWNED + OWNED_STEP * t + 3 * (3 * which + b)
                table[spot : spot + 3] = v
                if b == 2:
                    for g in range(ny):
                        spot = LAST + LAST_STEP * t + 2 * g + which
                        table[spot : spot + 1] = v[2:3]
    copies[0].wait()
    for b, spot in enumerate(SPOTS):
        table[spot : spot + wg_ref.shape[1]] = wg_ref[b].astype(F32)
    row = lax.broadcasted_iota(jnp.int32, table.shape, 0)
    lane = lax.broadcasted_iota(jnp.int32, table.shape, 1)
    wanted = jnp.where(row < LAST, y, ((row - LAST) & (LAST_STEP - 1)) >> 1)
    kept = jnp.where((lane >> 5) == wanted, table[...], 0.0).astype(BF16)
    i = lax.broadcasted_iota(jnp.int32, (width, lanes), 0)
    j = lax.broadcasted_iota(jnp.int32, (width, lanes), 1)
    out_ref[5] = dot_nt(((j & (width - 1)) == i).astype(BF16), kept).astype(BF16)

    def put(slot, w):
        w = w.reshape(zhalf, ny, width, lanes)
        for g in range(ny):
            rows = w[:, g].reshape(zhalf * width, lanes)
            out_ref[slot, :, g * zhalf * width : (g + 1) * zhalf * width] = dot_nt(sel, rows).astype(BF16)

    copies[1].wait()
    out_ref[0] = dot_nt(sel, wr_ref[0]).astype(BF16)
    copies[2].wait()
    put(2, wr_ref[1])
    copies[3].wait()
    put(4, wr_ref[2])
    copies[4].wait()
    put(1, we_ref[0])
    copies[5].wait()
    put(3, we_ref[1])


def prepare(y, c, w_reduce, w_expand, w_group, gains, biases):
    blocks, depth, lanes = w_reduce.shape
    width = w_group.shape[2]
    half = depth // 2
    whole = lambda *shape: pl.BlockSpec(shape, lambda i, at: (0,) * len(shape))
    there = pl.BlockSpec(memory_space=pl.ANY)
    return pl.pallas_call(
        prep_kernel,
        out_shape=jax.ShapeDtypeStruct((6, width, half), BF16),
        grid_spec=pltpu.PrefetchScalarGridSpec(
            num_scalar_prefetch=1,
            grid=(1,),
            in_specs=[there, there, there, whole(*gains.shape), whole(*biases.shape)],
            out_specs=whole(6, width, half),
            scratch_shapes=[
                pltpu.VMEM((3, half, lanes), BF16),
                pltpu.VMEM((2, half, lanes), BF16),
                pltpu.VMEM((blocks, 9 * width, lanes), BF16),
                pltpu.VMEM((half, lanes), F32),
                pltpu.SemaphoreType.DMA((6,)),
            ],
        ),
        compiler_params=pltpu.CompilerParams(vmem_limit_bytes=60 * 1024 * 1024),
        cost_estimate=pl.CostEstimate(flops=2 * 6 * half * lanes * width, bytes_accessed=2_500_000, transcendentals=0),
    )(jnp.stack([y, c]), w_reduce, w_expand, w_group.reshape(blocks, -1, lanes), gains, biases)


def conv_kernel(b, high, width, trim, side, at, part_ref, got_ref, table_ref, out_ref, after_ref):
    c, row0, col0 = at[0], at[1], at[2]
    own = got_ref.shape[2]
    frame = part_ref.shape[0] // (high + 2)
    i = lax.broadcasted_iota(jnp.int32, (own, own), 0)
    j = lax.broadcasted_iota(jnp.int32, (own, own), 1)
    eye = (i == j).astype(BF16)

    def columns(start, count):
        some = table_ref[:, start : start + count]
        return lax.dot_general(some, eye, (((0,), (0,)), ((), ())), preferred_element_type=F32)

    rows = columns(OWNED // 128 * 128, 128)

    def param(which, k):
        at_row = OWNED % 128 + (which * 3 + b) * 3 + k
        return sum(rows[at_row + OWNED_STEP * t : at_row + OWNED_STEP * t + 1] for t in range(3))

    first = part_ref[:, pl.ds(pl.multiple_of(own * c, own), own)] + got_ref[1 - c].astype(F32)
    hidden = jnp.maximum(param(0, 0) * first + param(1, 0), 0.0).reshape(high + 2, frame, own)
    row = row0 + lax.broadcasted_iota(jnp.int32, hidden.shape, 0)
    col = col0 + lax.broadcasted_iota(jnp.int32, hidden.shape, 1)
    inside = (row >= 0) & (row < side) & (col >= 0) & (col < side)
    hidden = jnp.where(inside, hidden, 0.0)
    spread = (
        (lax.broadcasted_iota(jnp.int32, (own, width), 0) & (width - 1))
        == lax.broadcasted_iota(jnp.int32, (own, width), 1)
    ).astype(BF16)
    same = (i >> 5) == (j >> 5)
    base = SPOTS[b] // 128 * 128
    filters = columns(base, 384).astype(BF16)
    sums = [None] * 3
    for r in range(3):
        shifted = hidden[r : r + high].reshape(high * frame, own).astype(BF16)
        for s in range(3):
            spot = SPOTS[b] - base + (3 * r + s) * width
            taps = jnp.dot(spread, filters[spot : spot + width], preferred_element_type=F32)
            taps = jnp.where(same, taps, 0.0).astype(BF16)
            term = jnp.dot(shifted, taps, preferred_element_type=F32)
            sums[s] = term if r == 0 else sums[s] + term
    spatial = pltpu.roll(sums[0], 1, 0) + sums[1] + pltpu.roll(sums[2], high * frame - 1, 0)
    middle = jnp.maximum(param(0, 1) * spatial + param(1, 1), 0.0)
    if trim:
        lo, hi = trim
        middle = middle.reshape(high, frame, own)[:, lo:hi].reshape(high * (hi - lo), own)
    out_ref[...] = middle.astype(BF16)
    after_ref[0:1] = param(0, 2)
    after_ref[1:2] = param(1, 2)


ON_CHIP = pl.BlockSpec(memory_space=pltpu.VMEM)
SCALARS = pl.BlockSpec(memory_space=pltpu.SMEM)


def convolve(b, high, width, trim, side, at, part, got, table):
    own = got.shape[2]
    frame = part.shape[0] // (high + 2)
    cols = trim[1] - trim[0] if trim else frame
    return pl.pallas_call(
        functools.partial(conv_kernel, b, high, width, trim, side),
        out_shape=(jax.ShapeDtypeStruct((high * cols, own), BF16), jax.ShapeDtypeStruct((8, own), F32)),
        in_specs=[SCALARS, ON_CHIP, ON_CHIP, ON_CHIP],
        out_specs=(ON_CHIP, ON_CHIP),
        compiler_params=pltpu.CompilerParams(vmem_limit_bytes=VMEM_LIMIT),
        cost_estimate=pl.CostEstimate(flops=18 * high * frame * own * own, bytes_accessed=2_500_000, transcendentals=0),
    )(at, part, got, table)


PIECES = 4


def last_kernel(at, middle_ref, w_hbm, kept_ref, mine_ref, send_ref, sums, w_ref, sems):
    c = at[0]
    many, half, lanes = w_ref.shape
    each = many // PIECES
    copies = [
        pltpu.make_async_copy(w_hbm.at[pl.ds(p * each, each)], w_ref.at[pl.ds(p * each, each)], sems.at[p])
        for p in range(PIECES)
    ]
    for copy in copies:
        copy.start()
    middle = jnp.concatenate([middle_ref[g] for g in range(middle_ref.shape[0])], axis=1)
    for k in range(many):
        if k % each == 0:
            copies[k // each].wait()
        sums[:, k * lanes : (k + 1) * lanes] = jnp.dot(middle, w_ref[k], preferred_element_type=F32)
    rows = mine_ref.shape[0]
    mine = pl.ds(pl.multiple_of(rows * c, rows), rows)
    other = pl.ds(pl.multiple_of(rows * (1 - c), rows), rows)
    mine_ref[...] = sums[mine]
    send_ref[:, : many * lanes] = sums[other].astype(BF16)
    send_ref[:, many * lanes :] = kept_ref[other]


def multiply_last(at, middle, w, kept):
    many, half, lanes = w.shape
    rows = kept.shape[0]
    return pl.pallas_call(
        last_kernel,
        out_shape=(
            jax.ShapeDtypeStruct((rows // 2, many * lanes), F32),
            jax.ShapeDtypeStruct((rows // 2, many * lanes + half), BF16),
        ),
        in_specs=[SCALARS, ON_CHIP, pl.BlockSpec(memory_space=pl.ANY), ON_CHIP],
        out_specs=(ON_CHIP, ON_CHIP),
        scratch_shapes=[
            pltpu.VMEM((rows, many * lanes), F32),
            pltpu.VMEM(w.shape, BF16),
            pltpu.SemaphoreType.DMA((PIECES,)),
        ],
        compiler_params=pltpu.CompilerParams(vmem_limit_bytes=50 * 1024 * 1024),
        cost_estimate=pl.CostEstimate(flops=2 * rows * half * many * lanes, bytes_accessed=5_000_000, transcendentals=0),
    )(at, middle, w, kept)


def halves(part, c):
    half = part.shape[1] // 2
    mine, other = pick(c, part[:, :half], part[:, half:]), pick(c, part[:, half:], part[:, :half])
    return mine, lax.all_gather(other.astype(BF16), "c", axis=0)


def local(planes, w_reduce, w_group, w_expand, gains, biases):
    nx, ny, nc, nz = (lax.axis_size(a) for a in ("x", "y", "c", "z"))
    x, y, c, z = (lax.axis_index(a) for a in ("x", "y", "c", "z"))
    tiles, rows, side, lanes = planes.shape
    blocks, _, width, _ = w_group.shape
    channels = lanes * nz
    half = channels // nc
    zhalf = nz // nc
    own = zhalf * width
    across = nz // tiles
    patch = side // across
    tall = rows * ny * nc
    frame = patch + 2 * LEFT

    early = lax.all_gather(prepare(y, c, w_reduce, w_expand, w_group, gains, biases), "z", axis=1, tiled=True)
    table = lax.optimization_barrier(lax.dynamic_slice(early, (5, own * c, 0), (1, own, half))[0])
    final = lax.dynamic_slice_in_dim(w_expand[2], half * c, half, axis=0)
    final = final.reshape(zhalf, ny, width, lanes).transpose(1, 0, 2, 3).reshape(half, lanes)
    final = lax.all_gather(final, "z", axis=0)

    wide = jnp.pad(planes, ((0, 0), (0, 0), (LEFT, LEFT), (0, 0)))
    strips = jnp.stack([wide[:, :, patch * q : patch * q + frame] for q in range(across)], axis=1)
    strips = strips.reshape(nz, rows, frame, lanes)
    mixed = lax.all_to_all(strips, "z", 0, 0, tiled=True)
    mine = pick(c, mixed[:zhalf], mixed[zhalf:])
    theirs = swap_core(pick(c, mixed[zhalf:], mixed[:zhalf]), c)
    chip = jnp.concatenate([pick(c, mine, theirs), pick(c, theirs, mine)], axis=1)
    chip = chip.transpose(1, 2, 0, 3).reshape(rows * nc, frame, half)
    body = lax.all_gather(chip, "y", axis=0, tiled=True)
    above = lax.ppermute(body[tall - HALO :], "x", [(i, i + 1) for i in range(nx - 1)])
    below = lax.ppermute(body[:HALO], "x", [(i + 1, i) for i in range(nx - 1)])
    gathered = jnp.concatenate([above, body, below], axis=0)

    last = early[5, :, LAST : LAST + 3 * LAST_STEP].astype(F32).reshape(nz, width, 3, ny, 2)
    last = (last[:, :, 0] + last[:, :, 1] + last[:, :, 2]).transpose(3, 0, 2, 1).reshape(2, nz, lanes)

    j = lax.broadcasted_iota(jnp.int32, (half, own), 0)
    k = lax.broadcasted_iota(jnp.int32, (half, own), 1)
    pull = (j == (k // width) * lanes + width * y + k % width).astype(BF16)
    stream = jnp.dot(gathered.reshape(-1, half), pull, preferred_element_type=F32).astype(BF16)
    stream = stream.reshape(tall + 2 * HALO, frame, own)

    for b in range(blocks):
        high = tall + 2 * (HALO - b)
        if b:
            gathered = lax.all_gather(stream.reshape(-1, own), "y", axis=1, tiled=True)
        part = dot_nt(gathered.reshape(-1, half), early[2 * b])
        other = pick(c, part[:, own:], part[:, :own]).astype(BF16)
        at = jnp.stack([c, tall * x - (HALO - b), patch * (z % across) - LEFT])
        high -= 2
        trim = (LEFT, LEFT + patch) if b == blocks - 1 else None
        middle, after = convolve(b, high, width, trim, side, at, part, lax.all_gather(other, "c", axis=0), table)
        if b < blocks - 1:
            middle = lax.all_gather(middle, "y", axis=1, tiled=True)
            mine, got = halves(dot_nt(middle, early[2 * b + 1]), c)
            second = (mine + pick(c, got[1], got[0]).astype(F32)).reshape(high, frame, own)
            stream = jnp.maximum(after[0] * second + after[1] + stream[1:-1].astype(F32), 0.0).astype(BF16)

    deep = rows * nc
    spots_of_chip = deep * patch
    middle = lax.all_to_all(middle.reshape(ny, spots_of_chip, own), "y", 0, 0, tiled=True)
    kept = gathered.reshape(tall + 2, frame, half)[:, LEFT : LEFT + patch]
    kept = lax.dynamic_slice_in_dim(kept, 1 + deep * y, deep, axis=0).reshape(spots_of_chip, half)
    j = lax.broadcasted_iota(jnp.int32, (half, half), 0)
    k = lax.broadcasted_iota(jnp.int32, (half, half), 1)
    natural = (j == (k // width % ny) * own + k // lanes * width + k % width).astype(BF16)
    kept = jnp.dot(kept, natural, preferred_element_type=F32).astype(BF16)
    second, send = multiply_last(at, middle, final, kept)
    got = swap_core(send, c)
    kept = kept.reshape(nc, rows * patch, half)
    mine, theirs = pick(c, kept[0], kept[1]), got[:, nz * lanes :]
    residual = jnp.concatenate([pick(c, mine, theirs), pick(c, theirs, mine)], axis=1)
    second = second + got[:, : nz * lanes].astype(F32)
    gain, bias = last.reshape(2, 1, nz * lanes)
    out = jnp.maximum(gain * second + bias + residual.astype(F32), 0.0).astype(BF16)
    out = out.reshape(rows * patch, nz, lanes)
    out = out.transpose(1, 0, 2).reshape(nz, rows, patch, lanes)
    out = lax.all_to_all(out, "z", 0, 0, tiled=True).reshape(tiles, across, rows, patch, lanes)
    return out.transpose(0, 2, 1, 3, 4).reshape(tiles, rows, side, lanes)


def solution(mesh):
    grid = Mesh(mesh.devices.reshape(4, 4, 2, 16), ("x", "y", "c", "z"))
    placed = (
        P(None, SEG, None, "z"),
        P(None, None, "z"),
        P(None, None, None, "z"),
        P(None, None, "z"),
        P(None, None, "z"),
        P(None, None, "z"),
    )
    return jax.shard_map(local, mesh=grid, in_specs=placed, out_specs=P(None, SEG, None, "z"), check_vma=False)
```

```python
import functools

import jax
import jax.numpy as jnp
from jax import lax
from jax.experimental import pallas as pl
from jax.experimental.pallas import tpu as pltpu
from jax.sharding import Mesh
from jax.sharding import PartitionSpec as P

BF16 = jnp.bfloat16
F32 = jnp.float32
SEG = ("x", "y", "c")
LEFT = 4
HALO = 3


def dot_nt(a, b):
    return lax.dot_general(a, b, (((1,), (1,)), ((), ())), preferred_element_type=F32)


def selector(rows, cols, base):
    i = lax.broadcasted_iota(jnp.int32, (rows, cols), 0)
    j = lax.broadcasted_iota(jnp.int32, (rows, cols), 1)
    return (j == i + base).astype(BF16)


def terms(v):
    out = []
    for _ in range(3):
        t = v.astype(BF16).astype(F32)
        out.append(t)
        v = v - t
    return out


def pick(c, a, b):
    return jnp.where(c == 0, a, b)


def swap_core(v, c):
    both = lax.all_gather(v, "c", axis=0)
    return pick(c, both[1], both[0])


SPOTS = (0, 320, 640)
OWNED, OWNED_STEP = 928, 24
LAST, LAST_STEP = 1000, 8
VMEM_LIMIT = 12 * 1024 * 1024
FIRST_LIMIT = 50 * 1024 * 1024


def prep_kernel(at, wr_hbm, we_hbm, wg_hbm, gains_ref, biases_ref, out_ref, wr_ref, we_ref, wg_ref, table, sems):
    y, c = at[0], at[1]
    width, half = out_ref.shape[1:]
    lanes = wr_ref.shape[2]
    ny = lanes // width
    zhalf = half // lanes
    rows = pl.ds(pl.multiple_of(half * c, half), half)
    copies = [pltpu.make_async_copy(wg_hbm, wg_ref, sems.at[0])]
    for b in range(3):
        copies.append(pltpu.make_async_copy(wr_hbm.at[b, rows], wr_ref.at[b], sems.at[1 + b]))
    for b in range(2):
        copies.append(pltpu.make_async_copy(we_hbm.at[b, rows], we_ref.at[b], sems.at[4 + b]))
    for copy in copies:
        copy.start()
    sel = selector(width, lanes, width * y)

    table[...] = jnp.zeros_like(table)
    for which, ref in enumerate((gains_ref, biases_ref)):
        for b in range(3):
            for t, v in enumerate(terms(ref[b])):
                spot = OWNED + OWNED_STEP * t + 3 * (3 * which + b)
                table[spot : spot + 3] = v
                if b == 2:
                    for g in range(ny):
                        spot = LAST + LAST_STEP * t + 2 * g + which
                        table[spot : spot + 1] = v[2:3]
    copies[0].wait()
    for b, spot in enumerate(SPOTS):
        table[spot : spot + wg_ref.shape[1]] = wg_ref[b].astype(F32)
    row = lax.broadcasted_iota(jnp.int32, table.shape, 0)
    lane = lax.broadcasted_iota(jnp.int32, table.shape, 1)
    wanted = jnp.where(row < LAST, y, ((row - LAST) & (LAST_STEP - 1)) >> 1)
    kept = jnp.where((lane >> 5) == wanted, table[...], 0.0).astype(BF16)
    i = lax.broadcasted_iota(jnp.int32, (width, lanes), 0)
    j = lax.broadcasted_iota(jnp.int32, (width, lanes), 1)
    out_ref[5] = dot_nt(((j & (width - 1)) == i).astype(BF16), kept).astype(BF16)

    def put(slot, w):
        w = w.reshape(zhalf, ny, width, lanes)
        for g in range(ny):
            rows = w[:, g].reshape(zhalf * width, lanes)
            out_ref[slot, :, g * zhalf * width : (g + 1) * zhalf * width] = dot_nt(sel, rows).astype(BF16)

    copies[1].wait()
    out_ref[0] = dot_nt(sel, wr_ref[0]).astype(BF16)
    copies[2].wait()
    put(2, wr_ref[1])
    copies[3].wait()
    put(4, wr_ref[2])
    copies[4].wait()
    put(1, we_ref[0])
    copies[5].wait()
    put(3, we_ref[1])


def prepare(y, c, w_reduce, w_expand, w_group, gains, biases):
    blocks, depth, lanes = w_reduce.shape
    width = w_group.shape[2]
    half = depth // 2
    whole = lambda *shape: pl.BlockSpec(shape, lambda i, at: (0,) * len(shape))
    there = pl.BlockSpec(memory_space=pl.ANY)
    return pl.pallas_call(
        prep_kernel,
        out_shape=jax.ShapeDtypeStruct((6, width, half), BF16),
        grid_spec=pltpu.PrefetchScalarGridSpec(
            num_scalar_prefetch=1,
            grid=(1,),
            in_specs=[there, there, there, whole(*gains.shape), whole(*biases.shape)],
            out_specs=whole(6, width, half),
            scratch_shapes=[
                pltpu.VMEM((3, half, lanes), BF16),
                pltpu.VMEM((2, half, lanes), BF16),
                pltpu.VMEM((blocks, 9 * width, lanes), BF16),
                pltpu.VMEM((half, lanes), F32),
                pltpu.SemaphoreType.DMA((6,)),
            ],
        ),
        compiler_params=pltpu.CompilerParams(vmem_limit_bytes=60 * 1024 * 1024),
        cost_estimate=pl.CostEstimate(flops=2 * 6 * half * lanes * width, bytes_accessed=2_500_000, transcendentals=0),
    )(jnp.stack([y, c]), w_reduce, w_expand, w_group.reshape(blocks, -1, lanes), gains, biases)


def conv_kernel(b, high, frame, width, trim, side, at, part_ref, got_ref, table_ref, out_ref, after_ref, sums):
    c, row0, col0 = at[0], at[1], at[2]
    count, own = got_ref.shape[1:]
    i = lax.broadcasted_iota(jnp.int32, (own, own), 0)
    j = lax.broadcasted_iota(jnp.int32, (own, own), 1)
    eye = (i == j).astype(BF16)

    def columns(start, count):
        some = table_ref[:, start : start + count]
        return lax.dot_general(some, eye, (((0,), (0,)), ((), ())), preferred_element_type=F32)

    rows = columns(OWNED // 128 * 128, 128)

    def param(which, k):
        at_row = OWNED % 128 + (which * 3 + b) * 3 + k
        return sum(rows[at_row + OWNED_STEP * t : at_row + OWNED_STEP * t + 1] for t in range(3))

    if part_ref.shape[1] == own:
        mine = part_ref[...]
    else:
        mine = part_ref[:, pl.ds(pl.multiple_of(own * c, own), own)]
    hidden = jnp.maximum(param(0, 0) * (mine + got_ref[1 - c].astype(F32)) + param(1, 0), 0.0)
    spot = lax.broadcasted_iota(jnp.int32, hidden.shape, 0)
    row = ((spot.astype(F32) + 0.5) * (1.0 / frame)).astype(jnp.int32)
    col = col0 + spot - row * frame
    row = row0 + row
    inside = (row >= 0) & (row < side) & (col >= 0) & (col < side)
    hidden = jnp.where(inside, hidden, 0.0)
    spread = (
        (lax.broadcasted_iota(jnp.int32, (own, width), 0) & (width - 1))
        == lax.broadcasted_iota(jnp.int32, (own, width), 1)
    ).astype(BF16)
    same = (i >> 5) == (j >> 5)
    base = SPOTS[b] // 128 * 128
    filters = columns(base, 384).astype(BF16)
    fit = high * frame
    shifted = jnp.concatenate([hidden[frame * r : frame * r + fit].astype(BF16) for r in range(3)], axis=1)
    terms_of = []
    for s in range(3):
        taps = []
        for r in range(3):
            spot = SPOTS[b] - base + (3 * r + s) * width
            tap = jnp.dot(spread, filters[spot : spot + width], preferred_element_type=F32)
            taps.append(jnp.where(same, tap, 0.0).astype(BF16))
        terms_of.append(jnp.dot(shifted, jnp.concatenate(taps, axis=0), preferred_element_type=F32))
    spatial = pltpu.roll(terms_of[0], 1, 0) + terms_of[1] + pltpu.roll(terms_of[2], fit - 1, 0)
    middle = jnp.maximum(param(0, 1) * spatial + param(1, 1), 0.0)
    if trim:
        lo, hi = trim
        for r in range(high):
            sums[r * (hi - lo) : (r + 1) * (hi - lo)] = middle[r * frame + lo : r * frame + hi]
        middle = sums[...]
    out_ref[...] = middle.astype(BF16)
    after_ref[0:1] = param(0, 2)
    after_ref[1:2] = param(1, 2)


ON_CHIP = pl.BlockSpec(memory_space=pltpu.VMEM)
SCALARS = pl.BlockSpec(memory_space=pltpu.SMEM)


def convolve(b, high, frame, width, trim, side, at, part, got, table):
    own = got.shape[2]
    cols = trim[1] - trim[0] if trim else frame
    return pl.pallas_call(
        functools.partial(conv_kernel, b, high, frame, width, trim, side),
        out_shape=(jax.ShapeDtypeStruct((high * cols, own), BF16), jax.ShapeDtypeStruct((8, own), F32)),
        in_specs=[SCALARS, ON_CHIP, ON_CHIP, ON_CHIP],
        out_specs=(ON_CHIP, ON_CHIP),
        scratch_shapes=[pltpu.VMEM((high * cols, own), F32)],
        compiler_params=pltpu.CompilerParams(vmem_limit_bytes=VMEM_LIMIT),
        cost_estimate=pl.CostEstimate(flops=18 * high * frame * own * own, bytes_accessed=2_500_000, transcendentals=0),
    )(at, part, got, table)


def first_kernel(at, x_ref, early_hbm, mine_ref, other_ref, table_ref, w_ref, sems):
    c = at[0]
    own = mine_ref.shape[1]
    mine = pl.ds(pl.multiple_of(own * c, own), own)
    other = pl.ds(pl.multiple_of(own * (1 - c), own), own)
    copies = [
        pltpu.make_async_copy(early_hbm.at[0, other], w_ref.at[0], sems.at[0]),
        pltpu.make_async_copy(early_hbm.at[0, mine], w_ref.at[1], sems.at[1]),
        pltpu.make_async_copy(early_hbm.at[5, mine], table_ref, sems.at[2]),
    ]
    for copy in copies:
        copy.start()
    copies[0].wait()
    other_ref[...] = dot_nt(x_ref[...], w_ref[0]).astype(BF16)
    copies[1].wait()
    mine_ref[...] = dot_nt(x_ref[...], w_ref[1])
    copies[2].wait()


def multiply_first(at, x, early, own):
    count, half = x.shape
    return pl.pallas_call(
        first_kernel,
        out_shape=(
            jax.ShapeDtypeStruct((count, own), F32),
            jax.ShapeDtypeStruct((count, own), BF16),
            jax.ShapeDtypeStruct((own, half), BF16),
        ),
        in_specs=[SCALARS, ON_CHIP, pl.BlockSpec(memory_space=pl.ANY)],
        out_specs=(ON_CHIP, ON_CHIP, ON_CHIP),
        scratch_shapes=[pltpu.VMEM((2, own, half), BF16), pltpu.SemaphoreType.DMA((3,))],
        compiler_params=pltpu.CompilerParams(vmem_limit_bytes=FIRST_LIMIT),
        cost_estimate=pl.CostEstimate(flops=4 * count * half * own, bytes_accessed=4_000_000, transcendentals=0),
    )(at, x, early)


PIECES = 4


def last_kernel(at, middle_ref, w_hbm, kept_ref, mine_ref, send_ref, sums, w_ref, sems):
    c = at[0]
    many, half, lanes = w_ref.shape
    each = many // PIECES
    copies = [
        pltpu.make_async_copy(w_hbm.at[pl.ds(p * each, each)], w_ref.at[pl.ds(p * each, each)], sems.at[p])
        for p in range(PIECES)
    ]
    for copy in copies:
        copy.start()
    middle = jnp.concatenate([middle_ref[g] for g in range(middle_ref.shape[0])], axis=1)
    for k in range(many):
        if k % each == 0:
            copies[k // each].wait()
        sums[:, k * lanes : (k + 1) * lanes] = jnp.dot(middle, w_ref[k], preferred_element_type=F32)
    rows = mine_ref.shape[0]
    mine = pl.ds(pl.multiple_of(rows * c, rows), rows)
    other = pl.ds(pl.multiple_of(rows * (1 - c), rows), rows)
    mine_ref[...] = sums[mine]
    send_ref[:, : many * lanes] = sums[other].astype(BF16)
    send_ref[:, many * lanes :] = kept_ref[other]


def multiply_last(at, middle, w, kept):
    many, half, lanes = w.shape
    rows = kept.shape[0]
    return pl.pallas_call(
        last_kernel,
        out_shape=(
            jax.ShapeDtypeStruct((rows // 2, many * lanes), F32),
            jax.ShapeDtypeStruct((rows // 2, many * lanes + half), BF16),
        ),
        in_specs=[SCALARS, ON_CHIP, pl.BlockSpec(memory_space=pl.ANY), ON_CHIP],
        out_specs=(ON_CHIP, ON_CHIP),
        scratch_shapes=[
            pltpu.VMEM((rows, many * lanes), F32),
            pltpu.VMEM(w.shape, BF16),
            pltpu.SemaphoreType.DMA((PIECES,)),
        ],
        compiler_params=pltpu.CompilerParams(vmem_limit_bytes=50 * 1024 * 1024),
        cost_estimate=pl.CostEstimate(flops=2 * rows * half * many * lanes, bytes_accessed=5_000_000, transcendentals=0),
    )(at, middle, w, kept)


def halves(part, c):
    half = part.shape[1] // 2
    mine, other = pick(c, part[:, :half], part[:, half:]), pick(c, part[:, half:], part[:, :half])
    return mine, lax.all_gather(other.astype(BF16), "c", axis=0)


def local(planes, w_reduce, w_group, w_expand, gains, biases):
    nx, ny, nc, nz = (lax.axis_size(a) for a in ("x", "y", "c", "z"))
    x, y, c, z = (lax.axis_index(a) for a in ("x", "y", "c", "z"))
    tiles, rows, side, lanes = planes.shape
    blocks, _, width, _ = w_group.shape
    channels = lanes * nz
    half = channels // nc
    zhalf = nz // nc
    own = zhalf * width
    across = nz // tiles
    patch = side // across
    tall = rows * ny * nc
    frame = patch + 2 * LEFT

    early = lax.all_gather(prepare(y, c, w_reduce, w_expand, w_group, gains, biases), "z", axis=1, tiled=True)
    final = lax.dynamic_slice_in_dim(w_expand[2], half * c, half, axis=0)
    final = final.reshape(zhalf, ny, width, lanes).transpose(1, 0, 2, 3).reshape(half, lanes)
    final = lax.all_gather(final, "z", axis=0)

    wide = jnp.pad(planes, ((0, 0), (0, 0), (LEFT, LEFT), (0, 0)))
    strips = jnp.stack([wide[:, :, patch * q : patch * q + frame] for q in range(across)], axis=1)
    strips = strips.reshape(nz, rows, frame, lanes)
    mixed = lax.all_to_all(strips, "z", 0, 0, tiled=True)
    mine = pick(c, mixed[:zhalf], mixed[zhalf:])
    theirs = swap_core(pick(c, mixed[zhalf:], mixed[:zhalf]), c)
    chip = jnp.concatenate([pick(c, mine, theirs), pick(c, theirs, mine)], axis=1)
    chip = chip.transpose(1, 2, 0, 3).reshape(rows * nc, frame, half)
    body = lax.all_gather(chip, "y", axis=0, tiled=True)
    above = lax.ppermute(body[tall - HALO :], "x", [(i, i + 1) for i in range(nx - 1)])
    below = lax.ppermute(body[:HALO], "x", [(i + 1, i) for i in range(nx - 1)])
    gathered = jnp.concatenate([above, body, below], axis=0)

    last = early[5, :, LAST : LAST + 3 * LAST_STEP].astype(F32).reshape(nz, width, 3, ny, 2)
    last = (last[:, :, 0] + last[:, :, 1] + last[:, :, 2]).transpose(3, 0, 2, 1).reshape(2, nz, lanes)

    j = lax.broadcasted_iota(jnp.int32, (half, own), 0)
    k = lax.broadcasted_iota(jnp.int32, (half, own), 1)
    pull = (j == (k // width) * lanes + width * y + k % width).astype(BF16)
    stream = jnp.dot(gathered.reshape(-1, half), pull, preferred_element_type=F32).astype(BF16)
    lean = patch + LEFT
    margin = (frame - lean) // 2
    stream = stream.reshape(tall + 2 * HALO, frame, own)[1:-1, margin : margin + lean].reshape(-1, own)
    for b in range(blocks):
        high = tall + 2 * (HALO - b)
        left = LEFT if b == 0 else LEFT - margin
        at = jnp.stack([c, tall * x - (HALO - b), patch * (z % across) - left])
        if b:
            gathered = lax.all_gather(stream, "y", axis=1, tiled=True)
            part = dot_nt(gathered, early[2 * b])
            other = pick(c, part[:, own:], part[:, :own]).astype(BF16)
            stream = stream[lean:-lean]
        else:
            part, other, table = multiply_first(at, gathered.reshape(-1, half), early, own)
            early, other = lax.optimization_barrier((early, other))
        high -= 2
        trim = (margin, margin + lean) if b == 0 else (left, left + patch) if b == blocks - 1 else None
        got = lax.all_gather(other, "c", axis=0)
        middle, after = convolve(b, high, lean if b else frame, width, trim, side, at, part, got, table)
        if b < blocks - 1:
            middle = lax.all_gather(middle, "y", axis=1, tiled=True)
            mine, got = halves(dot_nt(middle, early[2 * b + 1]), c)
            second = mine + pick(c, got[1], got[0]).astype(F32)
            stream = jnp.maximum(after[0] * second + after[1] + stream.astype(F32), 0.0).astype(BF16)

    deep = rows * nc
    spots_of_chip = deep * patch
    middle = lax.all_to_all(middle.reshape(ny, spots_of_chip, own), "y", 0, 0, tiled=True)
    t = lax.broadcasted_iota(jnp.int32, (spots_of_chip, gathered.shape[0]), 0)
    j = lax.broadcasted_iota(jnp.int32, (spots_of_chip, gathered.shape[0]), 1)
    of_chip = (j == (1 + deep * y + t // patch) * lean + LEFT - margin + t % patch).astype(BF16)
    kept = jnp.dot(of_chip, gathered, preferred_element_type=F32).astype(BF16)
    j = lax.broadcasted_iota(jnp.int32, (half, half), 0)
    k = lax.broadcasted_iota(jnp.int32, (half, half), 1)
    natural = (j == (k // width % ny) * own + k // lanes * width + k % width).astype(BF16)
    kept = jnp.dot(kept, natural, preferred_element_type=F32).astype(BF16)
    second, send = multiply_last(at, middle, final, kept)
    got = swap_core(send, c)
    kept = kept.reshape(nc, rows * patch, half)
    mine, theirs = pick(c, kept[0], kept[1]), got[:, nz * lanes :]
    residual = jnp.concatenate([pick(c, mine, theirs), pick(c, theirs, mine)], axis=1)
    second = second + got[:, : nz * lanes].astype(F32)
    gain, bias = last.reshape(2, 1, nz * lanes)
    out = jnp.maximum(gain * second + bias + residual.astype(F32), 0.0).astype(BF16)
    out = out.reshape(rows * patch, nz, lanes)
    out = out.transpose(1, 0, 2).reshape(nz, rows, patch, lanes)
    out = lax.all_to_all(out, "z", 0, 0, tiled=True).reshape(tiles, across, rows, patch, lanes)
    return out.transpose(0, 2, 1, 3, 4).reshape(tiles, rows, side, lanes)


def solution(mesh):
    grid = Mesh(mesh.devices.reshape(4, 4, 2, 16), ("x", "y", "c", "z"))
    placed = (
        P(None, SEG, None, "z"),
        P(None, None, "z"),
        P(None, None, None, "z"),
        P(None, None, "z"),
        P(None, None, "z"),
        P(None, None, "z"),
    )
    return jax.shard_map(local, mesh=grid, in_specs=placed, out_specs=P(None, SEG, None, "z"), check_vma=False)
```

```python
import functools

import jax
import jax.numpy as jnp
from jax import lax
from jax.experimental import pallas as pl
from jax.experimental.pallas import tpu as pltpu
from jax.sharding import Mesh
from jax.sharding import PartitionSpec as P

BF16 = jnp.bfloat16
F32 = jnp.float32
SEG = ("x", "y", "c")
LEFT = 4
HALO = 3


def dot_nt(a, b):
    return lax.dot_general(a, b, (((1,), (1,)), ((), ())), preferred_element_type=F32)


def selector(rows, cols, base):
    i = lax.broadcasted_iota(jnp.int32, (rows, cols), 0)
    j = lax.broadcasted_iota(jnp.int32, (rows, cols), 1)
    return (j == i + base).astype(BF16)


def terms(v):
    out = []
    for _ in range(3):
        t = v.astype(BF16).astype(F32)
        out.append(t)
        v = v - t
    return out


def pick(c, a, b):
    return jnp.where(c == 0, a, b)


def swap_core(v, c):
    both = lax.all_gather(v, "c", axis=0)
    return pick(c, both[1], both[0])


SPOTS = (0, 320, 640)
OWNED, OWNED_STEP = 928, 24
LAST, LAST_STEP = 1000, 8
VMEM_LIMIT = 12 * 1024 * 1024
FIRST_LIMIT = 49 * 1024 * 1024
FETCH_LIMIT = 46 * 1024 * 1024


def prep_kernel(at, wr_hbm, we_hbm, wg_hbm, gains_ref, biases_ref, out_ref, wr_ref, we_ref, wg_ref, table, sems):
    y, c = at[0], at[1]
    width, half = out_ref.shape[1:]
    lanes = wr_ref.shape[2]
    ny = lanes // width
    zhalf = half // lanes
    rows = pl.ds(pl.multiple_of(half * c, half), half)
    copies = [pltpu.make_async_copy(wg_hbm, wg_ref, sems.at[0])]
    for b in range(3):
        copies.append(pltpu.make_async_copy(wr_hbm.at[b, rows], wr_ref.at[b], sems.at[1 + b]))
    for b in range(2):
        copies.append(pltpu.make_async_copy(we_hbm.at[b, rows], we_ref.at[b], sems.at[4 + b]))
    for copy in copies:
        copy.start()
    sel = selector(width, lanes, width * y)

    table[...] = jnp.zeros_like(table)
    for which, ref in enumerate((gains_ref, biases_ref)):
        for b in range(3):
            for t, v in enumerate(terms(ref[b])):
                spot = OWNED + OWNED_STEP * t + 3 * (3 * which + b)
                table[spot : spot + 3] = v
                if b == 2:
                    for g in range(ny):
                        spot = LAST + LAST_STEP * t + 2 * g + which
                        table[spot : spot + 1] = v[2:3]
    copies[0].wait()
    for b, spot in enumerate(SPOTS):
        table[spot : spot + wg_ref.shape[1]] = wg_ref[b].astype(F32)
    row = lax.broadcasted_iota(jnp.int32, table.shape, 0)
    lane = lax.broadcasted_iota(jnp.int32, table.shape, 1)
    wanted = jnp.where(row < LAST, y, ((row - LAST) & (LAST_STEP - 1)) >> 1)
    kept = jnp.where((lane >> 5) == wanted, table[...], 0.0).astype(BF16)
    i = lax.broadcasted_iota(jnp.int32, (width, lanes), 0)
    j = lax.broadcasted_iota(jnp.int32, (width, lanes), 1)
    out_ref[5] = dot_nt(((j & (width - 1)) == i).astype(BF16), kept).astype(BF16)

    def put(slot, w):
        w = w.reshape(zhalf, ny, width, lanes)
        for g in range(ny):
            rows = w[:, g].reshape(zhalf * width, lanes)
            out_ref[slot, :, g * zhalf * width : (g + 1) * zhalf * width] = dot_nt(sel, rows).astype(BF16)

    copies[1].wait()
    out_ref[0] = dot_nt(sel, wr_ref[0]).astype(BF16)
    copies[2].wait()
    put(2, wr_ref[1])
    copies[3].wait()
    put(4, wr_ref[2])
    copies[4].wait()
    put(1, we_ref[0])
    copies[5].wait()
    put(3, we_ref[1])


def prepare(y, c, w_reduce, w_expand, w_group, gains, biases):
    blocks, depth, lanes = w_reduce.shape
    width = w_group.shape[2]
    half = depth // 2
    whole = lambda *shape: pl.BlockSpec(shape, lambda i, at: (0,) * len(shape))
    there = pl.BlockSpec(memory_space=pl.ANY)
    return pl.pallas_call(
        prep_kernel,
        out_shape=jax.ShapeDtypeStruct((6, width, half), BF16),
        grid_spec=pltpu.PrefetchScalarGridSpec(
            num_scalar_prefetch=1,
            grid=(1,),
            in_specs=[there, there, there, whole(*gains.shape), whole(*biases.shape)],
            out_specs=whole(6, width, half),
            scratch_shapes=[
                pltpu.VMEM((3, half, lanes), BF16),
                pltpu.VMEM((2, half, lanes), BF16),
                pltpu.VMEM((blocks, 9 * width, lanes), BF16),
                pltpu.VMEM((half, lanes), F32),
                pltpu.SemaphoreType.DMA((6,)),
            ],
        ),
        compiler_params=pltpu.CompilerParams(vmem_limit_bytes=60 * 1024 * 1024),
        cost_estimate=pl.CostEstimate(flops=2 * 6 * half * lanes * width, bytes_accessed=2_500_000, transcendentals=0),
    )(jnp.stack([y, c]), w_reduce, w_expand, w_group.reshape(blocks, -1, lanes), gains, biases)


def conv_and_fetch_kernel(*args):
    *first, early_hbm, out_ref, after_ref, later_ref, sums, sem = args
    copy = pltpu.make_async_copy(early_hbm.at[pl.ds(1, later_ref.shape[0])], later_ref, sem)
    copy.start()
    conv_kernel(*first, out_ref, after_ref, sums)
    copy.wait()


def conv_kernel(b, high, frame, width, trim, side, at, part_ref, got_ref, table_ref, out_ref, after_ref, sums):
    c, row0, col0 = at[0], at[1], at[2]
    count, own = got_ref.shape[1:]
    i = lax.broadcasted_iota(jnp.int32, (own, own), 0)
    j = lax.broadcasted_iota(jnp.int32, (own, own), 1)
    eye = (i == j).astype(BF16)

    def columns(start, count):
        some = table_ref[:, start : start + count]
        return lax.dot_general(some, eye, (((0,), (0,)), ((), ())), preferred_element_type=F32)

    rows = columns(OWNED // 128 * 128, 128)

    def param(which, k):
        at_row = OWNED % 128 + (which * 3 + b) * 3 + k
        return sum(rows[at_row + OWNED_STEP * t : at_row + OWNED_STEP * t + 1] for t in range(3))

    if part_ref.shape[1] == own:
        mine = part_ref[...]
    else:
        mine = part_ref[:, pl.ds(pl.multiple_of(own * c, own), own)]
    hidden = jnp.maximum(param(0, 0) * (mine + got_ref[1 - c].astype(F32)) + param(1, 0), 0.0)
    spot = lax.broadcasted_iota(jnp.int32, hidden.shape, 0)
    row = ((spot.astype(F32) + 0.5) * (1.0 / frame)).astype(jnp.int32)
    col = col0 + spot - row * frame
    row = row0 + row
    inside = (row >= 0) & (row < side) & (col >= 0) & (col < side)
    hidden = jnp.where(inside, hidden, 0.0)
    spread = (
        (lax.broadcasted_iota(jnp.int32, (own, width), 0) & (width - 1))
        == lax.broadcasted_iota(jnp.int32, (own, width), 1)
    ).astype(BF16)
    same = (i >> 5) == (j >> 5)
    base = SPOTS[b] // 128 * 128
    filters = columns(base, 384).astype(BF16)
    fit = high * frame
    shifted = jnp.concatenate([hidden[frame * r : frame * r + fit].astype(BF16) for r in range(3)], axis=1)
    terms_of = []
    for s in range(3):
        taps = []
        for r in range(3):
            spot = SPOTS[b] - base + (3 * r + s) * width
            tap = jnp.dot(spread, filters[spot : spot + width], preferred_element_type=F32)
            taps.append(jnp.where(same, tap, 0.0).astype(BF16))
        terms_of.append(jnp.dot(shifted, jnp.concatenate(taps, axis=0), preferred_element_type=F32))
    spatial = pltpu.roll(terms_of[0], 1, 0) + terms_of[1] + pltpu.roll(terms_of[2], fit - 1, 0)
    middle = jnp.maximum(param(0, 1) * spatial + param(1, 1), 0.0)
    if trim:
        lo, hi = trim
        for r in range(high):
            sums[r * (hi - lo) : (r + 1) * (hi - lo)] = middle[r * frame + lo : r * frame + hi]
        middle = sums[...]
    out_ref[...] = middle.astype(BF16)
    after_ref[0:1] = param(0, 2)
    after_ref[1:2] = param(1, 2)


ON_CHIP = pl.BlockSpec(memory_space=pltpu.VMEM)
SCALARS = pl.BlockSpec(memory_space=pltpu.SMEM)


def convolve(b, high, frame, width, trim, side, at, part, got, table, early=None):
    own = got.shape[2]
    cols = trim[1] - trim[0] if trim else frame
    fetch = early is not None
    out_shape = (jax.ShapeDtypeStruct((high * cols, own), BF16), jax.ShapeDtypeStruct((8, own), F32))
    scratch = [pltpu.VMEM((high * cols, own), F32)]
    if fetch:
        out_shape += (jax.ShapeDtypeStruct((4, *early.shape[1:]), BF16),)
        scratch.append(pltpu.SemaphoreType.DMA)
    body = conv_and_fetch_kernel if fetch else conv_kernel
    return pl.pallas_call(
        functools.partial(body, b, high, frame, width, trim, side),
        out_shape=out_shape,
        in_specs=[SCALARS, ON_CHIP, ON_CHIP, ON_CHIP] + [pl.BlockSpec(memory_space=pl.ANY)] * fetch,
        out_specs=(ON_CHIP,) * len(out_shape),
        scratch_shapes=scratch,
        compiler_params=pltpu.CompilerParams(vmem_limit_bytes=FETCH_LIMIT if fetch else VMEM_LIMIT),
        cost_estimate=pl.CostEstimate(flops=18 * high * frame * own * own, bytes_accessed=2_500_000, transcendentals=0),
    )(at, part, got, table, *([early] if fetch else []))


def first_kernel(at, x_ref, early_hbm, mine_ref, other_ref, table_ref, w_ref, sems):
    c = at[0]
    own = mine_ref.shape[1]
    mine = pl.ds(pl.multiple_of(own * c, own), own)
    other = pl.ds(pl.multiple_of(own * (1 - c), own), own)
    copies = [
        pltpu.make_async_copy(early_hbm.at[0, other], w_ref.at[0], sems.at[0]),
        pltpu.make_async_copy(early_hbm.at[0, mine], w_ref.at[1], sems.at[1]),
        pltpu.make_async_copy(early_hbm.at[5, mine], table_ref, sems.at[2]),
    ]
    for copy in copies:
        copy.start()
    copies[0].wait()
    other_ref[...] = dot_nt(x_ref[...], w_ref[0]).astype(BF16)
    copies[1].wait()
    mine_ref[...] = dot_nt(x_ref[...], w_ref[1])
    copies[2].wait()


def multiply_first(at, x, early, own):
    count, half = x.shape
    return pl.pallas_call(
        first_kernel,
        out_shape=(
            jax.ShapeDtypeStruct((count, own), F32),
            jax.ShapeDtypeStruct((count, own), BF16),
            jax.ShapeDtypeStruct((own, half), BF16),
        ),
        in_specs=[SCALARS, ON_CHIP, pl.BlockSpec(memory_space=pl.ANY)],
        out_specs=(ON_CHIP, ON_CHIP, ON_CHIP),
        scratch_shapes=[pltpu.VMEM((2, own, half), BF16), pltpu.SemaphoreType.DMA((3,))],
        compiler_params=pltpu.CompilerParams(vmem_limit_bytes=FIRST_LIMIT),
        cost_estimate=pl.CostEstimate(flops=4 * count * half * own, bytes_accessed=4_000_000, transcendentals=0),
    )(at, x, early)


PIECES = 4


def last_kernel(at, middle_ref, w_hbm, kept_ref, mine_ref, send_ref, sums, w_ref, sems):
    c = at[0]
    many, half, lanes = w_ref.shape
    each = many // PIECES
    copies = [
        pltpu.make_async_copy(w_hbm.at[pl.ds(p * each, each)], w_ref.at[pl.ds(p * each, each)], sems.at[p])
        for p in range(PIECES)
    ]
    for copy in copies:
        copy.start()
    middle = jnp.concatenate([middle_ref[g] for g in range(middle_ref.shape[0])], axis=1)
    for k in range(many):
        if k % each == 0:
            copies[k // each].wait()
        sums[:, k * lanes : (k + 1) * lanes] = jnp.dot(middle, w_ref[k], preferred_element_type=F32)
    rows = mine_ref.shape[0]
    mine = pl.ds(pl.multiple_of(rows * c, rows), rows)
    other = pl.ds(pl.multiple_of(rows * (1 - c), rows), rows)
    mine_ref[...] = sums[mine]
    send_ref[:, : many * lanes] = sums[other].astype(BF16)
    send_ref[:, many * lanes :] = kept_ref[other]


def multiply_last(at, middle, w, kept):
    many, half, lanes = w.shape
    rows = kept.shape[0]
    return pl.pallas_call(
        last_kernel,
        out_shape=(
            jax.ShapeDtypeStruct((rows // 2, many * lanes), F32),
            jax.ShapeDtypeStruct((rows // 2, many * lanes + half), BF16),
        ),
        in_specs=[SCALARS, ON_CHIP, pl.BlockSpec(memory_space=pl.ANY), ON_CHIP],
        out_specs=(ON_CHIP, ON_CHIP),
        scratch_shapes=[
            pltpu.VMEM((rows, many * lanes), F32),
            pltpu.VMEM(w.shape, BF16),
            pltpu.SemaphoreType.DMA((PIECES,)),
        ],
        compiler_params=pltpu.CompilerParams(vmem_limit_bytes=50 * 1024 * 1024),
        cost_estimate=pl.CostEstimate(flops=2 * rows * half * many * lanes, bytes_accessed=5_000_000, transcendentals=0),
    )(at, middle, w, kept)


def halves(part, c):
    half = part.shape[1] // 2
    mine, other = pick(c, part[:, :half], part[:, half:]), pick(c, part[:, half:], part[:, :half])
    return mine, lax.all_gather(other.astype(BF16), "c", axis=0)


def local(planes, w_reduce, w_group, w_expand, gains, biases):
    nx, ny, nc, nz = (lax.axis_size(a) for a in ("x", "y", "c", "z"))
    x, y, c, z = (lax.axis_index(a) for a in ("x", "y", "c", "z"))
    tiles, rows, side, lanes = planes.shape
    blocks, _, width, _ = w_group.shape
    channels = lanes * nz
    half = channels // nc
    zhalf = nz // nc
    own = zhalf * width
    across = nz // tiles
    patch = side // across
    tall = rows * ny * nc
    frame = patch + 2 * LEFT

    early = lax.all_gather(prepare(y, c, w_reduce, w_expand, w_group, gains, biases), "z", axis=1, tiled=True)
    final = lax.dynamic_slice_in_dim(w_expand[2], half * c, half, axis=0)
    final = final.reshape(zhalf, ny, width, lanes).transpose(1, 0, 2, 3).reshape(half, lanes)
    final = lax.all_gather(final, "z", axis=0)

    wide = jnp.pad(planes, ((0, 0), (0, 0), (LEFT, LEFT), (0, 0)))
    strips = jnp.stack([wide[:, :, patch * q : patch * q + frame] for q in range(across)], axis=1)
    strips = strips.reshape(nz, rows, frame, lanes)
    mixed = lax.all_to_all(strips, "z", 0, 0, tiled=True)
    mine = pick(c, mixed[:zhalf], mixed[zhalf:])
    theirs = swap_core(pick(c, mixed[zhalf:], mixed[:zhalf]), c)
    chip = jnp.concatenate([pick(c, mine, theirs), pick(c, theirs, mine)], axis=1)
    chip = chip.transpose(1, 2, 0, 3).reshape(rows * nc, frame, half)
    body = lax.all_gather(chip, "y", axis=0, tiled=True)
    above = lax.ppermute(body[tall - HALO :], "x", [(i, i + 1) for i in range(nx - 1)])
    below = lax.ppermute(body[:HALO], "x", [(i + 1, i) for i in range(nx - 1)])
    gathered = jnp.concatenate([above, body, below], axis=0)

    last = early[5, :, LAST : LAST + 3 * LAST_STEP].astype(F32).reshape(nz, width, 3, ny, 2)
    last = (last[:, :, 0] + last[:, :, 1] + last[:, :, 2]).transpose(3, 0, 2, 1).reshape(2, nz, lanes)

    j = lax.broadcasted_iota(jnp.int32, (half, own), 0)
    k = lax.broadcasted_iota(jnp.int32, (half, own), 1)
    pull = (j == (k // width) * lanes + width * y + k % width).astype(BF16)
    stream = jnp.dot(gathered.reshape(-1, half), pull, preferred_element_type=F32).astype(BF16)
    lean = patch + LEFT
    margin = (frame - lean) // 2
    stream = stream.reshape(tall + 2 * HALO, frame, own)[1:-1, margin : margin + lean].reshape(-1, own)
    for b in range(blocks):
        high = tall + 2 * (HALO - b)
        left = LEFT if b == 0 else LEFT - margin
        at = jnp.stack([c, tall * x - (HALO - b), patch * (z % across) - left])
        if b:
            gathered = lax.all_gather(stream, "y", axis=1, tiled=True)
            part = dot_nt(gathered, later[2 * b - 1])
            other = pick(c, part[:, own:], part[:, :own]).astype(BF16)
            stream = stream[lean:-lean]
        else:
            part, other, table = multiply_first(at, gathered.reshape(-1, half), early, own)
        high -= 2
        trim = (margin, margin + lean) if b == 0 else (left, left + patch) if b == blocks - 1 else None
        got = lax.all_gather(other, "c", axis=0)
        if b:
            middle, after = convolve(b, high, lean, width, trim, side, at, part, got, table)
        else:
            middle, after, later = convolve(b, high, frame, width, trim, side, at, part, got, table, early)
        if b < blocks - 1:
            middle = lax.all_gather(middle, "y", axis=1, tiled=True)
            mine, got = halves(dot_nt(middle, later[2 * b]), c)
            second = mine + pick(c, got[1], got[0]).astype(F32)
            stream = jnp.maximum(after[0] * second + after[1] + stream.astype(F32), 0.0).astype(BF16)

    deep = rows * nc
    spots_of_chip = deep * patch
    middle = lax.all_to_all(middle.reshape(ny, spots_of_chip, own), "y", 0, 0, tiled=True)
    t = lax.broadcasted_iota(jnp.int32, (spots_of_chip, gathered.shape[0]), 0)
    j = lax.broadcasted_iota(jnp.int32, (spots_of_chip, gathered.shape[0]), 1)
    of_chip = (j == (1 + deep * y + t // patch) * lean + LEFT - margin + t % patch).astype(BF16)
    kept = jnp.dot(of_chip, gathered, preferred_element_type=F32).astype(BF16)
    j = lax.broadcasted_iota(jnp.int32, (half, half), 0)
    k = lax.broadcasted_iota(jnp.int32, (half, half), 1)
    natural = (j == (k // width % ny) * own + k // lanes * width + k % width).astype(BF16)
    kept = jnp.dot(kept, natural, preferred_element_type=F32).astype(BF16)
    second, send = multiply_last(at, middle, final, kept)
    got = swap_core(send, c)
    kept = kept.reshape(nc, rows * patch, half)
    mine, theirs = pick(c, kept[0], kept[1]), got[:, nz * lanes :]
    residual = jnp.concatenate([pick(c, mine, theirs), pick(c, theirs, mine)], axis=1)
    second = second + got[:, : nz * lanes].astype(F32)
    gain, bias = last.reshape(2, 1, nz * lanes)
    out = jnp.maximum(gain * second + bias + residual.astype(F32), 0.0).astype(BF16)
    out = out.reshape(rows * patch, nz, lanes)
    out = out.transpose(1, 0, 2).reshape(nz, rows, patch, lanes)
    out = lax.all_to_all(out, "z", 0, 0, tiled=True).reshape(tiles, across, rows, patch, lanes)
    return out.transpose(0, 2, 1, 3, 4).reshape(tiles, rows, side, lanes)


def solution(mesh):
    grid = Mesh(mesh.devices.reshape(4, 4, 2, 16), ("x", "y", "c", "z"))
    placed = (
        P(None, SEG, None, "z"),
        P(None, None, "z"),
        P(None, None, None, "z"),
        P(None, None, "z"),
        P(None, None, "z"),
        P(None, None, "z"),
    )
    return jax.shard_map(local, mesh=grid, in_specs=placed, out_specs=P(None, SEG, None, "z"), check_vma=False)
```

```python
import functools

import jax
import jax.numpy as jnp
from jax import lax
from jax.experimental import pallas as pl
from jax.experimental.pallas import tpu as pltpu
from jax.sharding import Mesh
from jax.sharding import PartitionSpec as P

BF16 = jnp.bfloat16
F32 = jnp.float32
SEG = ("x", "y", "c")
LEFT = 4
HALO = 3


def dot_nt(a, b):
    return lax.dot_general(a, b, (((1,), (1,)), ((), ())), preferred_element_type=F32)


def selector(rows, cols, base):
    i = lax.broadcasted_iota(jnp.int32, (rows, cols), 0)
    j = lax.broadcasted_iota(jnp.int32, (rows, cols), 1)
    return (j == i + base).astype(BF16)


def terms(v):
    out = []
    for _ in range(3):
        t = v.astype(BF16).astype(F32)
        out.append(t)
        v = v - t
    return out


def pick(c, a, b):
    return jnp.where(c == 0, a, b)


def swap_core(v, c):
    both = lax.all_gather(v, "c", axis=0)
    return pick(c, both[1], both[0])


SPOTS = (0, 320, 640)
OWNED, OWNED_STEP = 928, 24
LAST, LAST_STEP = 1000, 8
VMEM_LIMIT = 12 * 1024 * 1024
ON_CHIP = pl.BlockSpec(memory_space=pltpu.VMEM)
SCALARS = pl.BlockSpec(memory_space=pltpu.SMEM)
FIRST_LIMIT = 49 * 1024 * 1024
FETCH_LIMIT = 46 * 1024 * 1024


TABLE = 4


def put_columns(w, ny, sel, store):
    half, lanes = w.shape
    each = half // ny
    w = w.reshape(half // lanes, ny, lanes // ny, lanes)
    for g in range(ny):
        store(slice(g * each, (g + 1) * each), dot_nt(sel, w[:, g].reshape(each, lanes)).astype(BF16))


def prep_kernel(at, wr_hbm, we_hbm, wg_hbm, gains_ref, biases_ref, out_ref, wr_ref, we_ref, wg_ref, table, sems):
    y, c = at[0], at[1]
    width, half = out_ref.shape[1:]
    lanes = wr_ref.shape[2]
    ny = lanes // width
    zhalf = half // lanes
    rows = pl.ds(pl.multiple_of(half * c, half), half)
    copies = [pltpu.make_async_copy(wg_hbm, wg_ref, sems.at[0])]
    for b in range(2):
        copies.append(pltpu.make_async_copy(wr_hbm.at[b, rows], wr_ref.at[b], sems.at[1 + b]))
    for b in range(2):
        copies.append(pltpu.make_async_copy(we_hbm.at[b, rows], we_ref.at[b], sems.at[3 + b]))
    for copy in copies:
        copy.start()
    sel = selector(width, lanes, width * y)

    table[...] = jnp.zeros_like(table)
    for which, ref in enumerate((gains_ref, biases_ref)):
        for b in range(3):
            for t, v in enumerate(terms(ref[b])):
                spot = OWNED + OWNED_STEP * t + 3 * (3 * which + b)
                table[spot : spot + 3] = v
                if b == 2:
                    for g in range(ny):
                        spot = LAST + LAST_STEP * t + 2 * g + which
                        table[spot : spot + 1] = v[2:3]
    copies[0].wait()
    for b, spot in enumerate(SPOTS):
        table[spot : spot + wg_ref.shape[1]] = wg_ref[b].astype(F32)
    row = lax.broadcasted_iota(jnp.int32, table.shape, 0)
    lane = lax.broadcasted_iota(jnp.int32, table.shape, 1)
    wanted = jnp.where(row < LAST, y, ((row - LAST) & (LAST_STEP - 1)) >> 1)
    kept = jnp.where((lane >> 5) == wanted, table[...], 0.0).astype(BF16)
    i = lax.broadcasted_iota(jnp.int32, (width, lanes), 0)
    j = lax.broadcasted_iota(jnp.int32, (width, lanes), 1)
    out_ref[TABLE] = dot_nt(((j & (width - 1)) == i).astype(BF16), kept).astype(BF16)

    def into(slot):
        def store(spots, v):
            out_ref[slot, :, spots] = v

        return store

    copies[1].wait()
    out_ref[0] = dot_nt(sel, wr_ref[0]).astype(BF16)
    copies[2].wait()
    put_columns(wr_ref[1], ny, sel, into(2))
    copies[3].wait()
    put_columns(we_ref[0], ny, sel, into(1))
    copies[4].wait()
    put_columns(we_ref[1], ny, sel, into(3))


def late_kernel(at, wr_hbm, we_hbm, out_ref, wr_ref, we_ref, sems):
    y, c = at[0], at[1]
    half, lanes = wr_ref.shape
    width = out_ref.shape[0] - lanes
    rows = pl.ds(pl.multiple_of(half * c, half), half)
    copies = [
        pltpu.make_async_copy(we_hbm.at[2, rows], we_ref, sems.at[0]),
        pltpu.make_async_copy(wr_hbm.at[2, rows], wr_ref, sems.at[1]),
    ]
    for copy in copies:
        copy.start()
    for copy in copies:
        copy.wait()

    def every(spots, v):
        out_ref[:lanes, spots] = v

    def owned(spots, v):
        out_ref[lanes:, spots] = v

    put_columns(we_ref[...], lanes // width, selector(lanes, lanes, 0), every)
    put_columns(wr_ref[...], lanes // width, selector(width, lanes, width * y), owned)


def prepare_late(at, w_reduce, w_expand, width):
    depth, lanes = w_reduce.shape[1:]
    half = depth // 2
    there = pl.BlockSpec(memory_space=pl.ANY)
    return pl.pallas_call(
        late_kernel,
        out_shape=jax.ShapeDtypeStruct((lanes + width, half), BF16),
        in_specs=[SCALARS, there, there],
        out_specs=ON_CHIP,
        scratch_shapes=[pltpu.VMEM((half, lanes), BF16)] * 2 + [pltpu.SemaphoreType.DMA((2,))],
        compiler_params=pltpu.CompilerParams(vmem_limit_bytes=VMEM_LIMIT),
        cost_estimate=pl.CostEstimate(flops=2 * half * lanes * (lanes + width), bytes_accessed=1_000_000, transcendentals=0),
    )(at, w_reduce, w_expand)


def prepare(y, c, w_reduce, w_expand, w_group, gains, biases):
    blocks, depth, lanes = w_reduce.shape
    width = w_group.shape[2]
    half = depth // 2
    whole = lambda *shape: pl.BlockSpec(shape, lambda i, at: (0,) * len(shape))
    there = pl.BlockSpec(memory_space=pl.ANY)
    return pl.pallas_call(
        prep_kernel,
        out_shape=jax.ShapeDtypeStruct((5, width, half), BF16),
        grid_spec=pltpu.PrefetchScalarGridSpec(
            num_scalar_prefetch=1,
            grid=(1,),
            in_specs=[there, there, there, whole(*gains.shape), whole(*biases.shape)],
            out_specs=whole(5, width, half),
            scratch_shapes=[
                pltpu.VMEM((2, half, lanes), BF16),
                pltpu.VMEM((2, half, lanes), BF16),
                pltpu.VMEM((blocks, 9 * width, lanes), BF16),
                pltpu.VMEM((half, lanes), F32),
                pltpu.SemaphoreType.DMA((5,)),
            ],
        ),
        compiler_params=pltpu.CompilerParams(vmem_limit_bytes=60 * 1024 * 1024),
        cost_estimate=pl.CostEstimate(flops=2 * 6 * half * lanes * width, bytes_accessed=2_500_000, transcendentals=0),
    )(jnp.stack([y, c]), w_reduce, w_expand, w_group.reshape(blocks, -1, lanes), gains, biases)


def conv_and_fetch_kernel(*args):
    *first, early_hbm, out_ref, after_ref, late1, late2, late3, sums, sems = args
    copies = [
        pltpu.make_async_copy(early_hbm.at[:, 1 + m], ref, sems.at[m]) for m, ref in enumerate((late1, late2, late3))
    ]
    for copy in copies:
        copy.start()
    conv_kernel(*first, out_ref, after_ref, sums)
    for copy in copies:
        copy.wait()


def conv_kernel(b, high, frame, width, trim, side, at, part_ref, got_ref, table_ref, out_ref, after_ref, sums):
    c, row0, col0 = at[0], at[1], at[2]
    count, own = got_ref.shape[1:]
    i = lax.broadcasted_iota(jnp.int32, (own, own), 0)
    j = lax.broadcasted_iota(jnp.int32, (own, own), 1)
    eye = (i == j).astype(BF16)

    def columns(start, count):
        some = table_ref[:, start : start + count]
        return lax.dot_general(some, eye, (((0,), (0,)), ((), ())), preferred_element_type=F32)

    rows = columns(OWNED // 128 * 128, 128)

    def param(which, k):
        at_row = OWNED % 128 + (which * 3 + b) * 3 + k
        return sum(rows[at_row + OWNED_STEP * t : at_row + OWNED_STEP * t + 1] for t in range(3))

    if part_ref.shape[1] == own:
        mine = part_ref[...]
    else:
        mine = part_ref[:, pl.ds(pl.multiple_of(own * c, own), own)]
    hidden = jnp.maximum(param(0, 0) * (mine + got_ref[1 - c].astype(F32)) + param(1, 0), 0.0)
    spot = lax.broadcasted_iota(jnp.int32, hidden.shape, 0)
    row = ((spot.astype(F32) + 0.5) * (1.0 / frame)).astype(jnp.int32)
    col = col0 + spot - row * frame
    row = row0 + row
    inside = (row >= 0) & (row < side) & (col >= 0) & (col < side)
    hidden = jnp.where(inside, hidden, 0.0)
    spread = (
        (lax.broadcasted_iota(jnp.int32, (own, width), 0) & (width - 1))
        == lax.broadcasted_iota(jnp.int32, (own, width), 1)
    ).astype(BF16)
    same = (i >> 5) == (j >> 5)
    base = SPOTS[b] // 128 * 128
    filters = columns(base, 384).astype(BF16)
    fit = high * frame
    shifted = jnp.concatenate([hidden[frame * r : frame * r + fit].astype(BF16) for r in range(3)], axis=1)
    terms_of = []
    for s in range(3):
        taps = []
        for r in range(3):
            spot = SPOTS[b] - base + (3 * r + s) * width
            tap = jnp.dot(spread, filters[spot : spot + width], preferred_element_type=F32)
            taps.append(jnp.where(same, tap, 0.0).astype(BF16))
        terms_of.append(jnp.dot(shifted, jnp.concatenate(taps, axis=0), preferred_element_type=F32))
    spatial = pltpu.roll(terms_of[0], 1, 0) + terms_of[1] + pltpu.roll(terms_of[2], fit - 1, 0)
    middle = jnp.maximum(param(0, 1) * spatial + param(1, 1), 0.0)
    if trim:
        lo, hi = trim
        for r in range(high):
            sums[r * (hi - lo) : (r + 1) * (hi - lo)] = middle[r * frame + lo : r * frame + hi]
        middle = sums[...]
    out_ref[...] = middle.astype(BF16)
    after_ref[0:1] = param(0, 2)
    after_ref[1:2] = param(1, 2)


def convolve(b, high, frame, width, trim, side, at, part, got, table, early=None):
    own = got.shape[2]
    cols = trim[1] - trim[0] if trim else frame
    fetch = early is not None
    out_shape = (jax.ShapeDtypeStruct((high * cols, own), BF16), jax.ShapeDtypeStruct((8, own), F32))
    scratch = [pltpu.VMEM((high * cols, own), F32)]
    if fetch:
        many, _, *rest = early.shape
        out_shape += (jax.ShapeDtypeStruct((many, *rest), BF16),) * (TABLE - 1)
        scratch.append(pltpu.SemaphoreType.DMA((TABLE - 1,)))
    body = conv_and_fetch_kernel if fetch else conv_kernel
    return pl.pallas_call(
        functools.partial(body, b, high, frame, width, trim, side),
        out_shape=out_shape,
        in_specs=[SCALARS, ON_CHIP, ON_CHIP, ON_CHIP] + [pl.BlockSpec(memory_space=pl.ANY)] * fetch,
        out_specs=(ON_CHIP,) * len(out_shape),
        scratch_shapes=scratch,
        compiler_params=pltpu.CompilerParams(vmem_limit_bytes=FETCH_LIMIT if fetch else VMEM_LIMIT),
        cost_estimate=pl.CostEstimate(flops=18 * high * frame * own * own, bytes_accessed=2_500_000, transcendentals=0),
    )(at, part, got, table, *([early] if fetch else []))


def first_kernel(at, x_ref, early_hbm, mine_ref, other_ref, table_ref, w_ref, sems):
    c = at[0]
    own = mine_ref.shape[1]
    many = table_ref.shape[0]
    mine = pl.ds(many * c, many)
    other = pl.ds(many * (1 - c), many)
    copies = [
        pltpu.make_async_copy(early_hbm.at[other, 0], w_ref.at[0], sems.at[0]),
        pltpu.make_async_copy(early_hbm.at[mine, 0], w_ref.at[1], sems.at[1]),
        pltpu.make_async_copy(early_hbm.at[mine, TABLE], table_ref, sems.at[2]),
    ]
    for copy in copies:
        copy.start()
    copies[0].wait()
    other_ref[...] = dot_nt(x_ref[...], w_ref[0].reshape(own, -1)).astype(BF16)
    copies[1].wait()
    mine_ref[...] = dot_nt(x_ref[...], w_ref[1].reshape(own, -1))
    copies[2].wait()


def multiply_first(at, x, early, own):
    count, half = x.shape
    mine_of = (early.shape[0] // 2, *early.shape[2:])
    return pl.pallas_call(
        first_kernel,
        out_shape=(
            jax.ShapeDtypeStruct((count, own), F32),
            jax.ShapeDtypeStruct((count, own), BF16),
            jax.ShapeDtypeStruct(mine_of, BF16),
        ),
        in_specs=[SCALARS, ON_CHIP, pl.BlockSpec(memory_space=pl.ANY)],
        out_specs=(ON_CHIP, ON_CHIP, ON_CHIP),
        scratch_shapes=[pltpu.VMEM((2, *mine_of), BF16), pltpu.SemaphoreType.DMA((3,))],
        compiler_params=pltpu.CompilerParams(vmem_limit_bytes=FIRST_LIMIT),
        cost_estimate=pl.CostEstimate(flops=4 * count * half * own, bytes_accessed=4_000_000, transcendentals=0),
    )(at, x, early)


PIECES = 4


def last_kernel(at, middle_ref, w_hbm, kept_ref, mine_ref, send_ref, sums, w_ref, sems):
    c = at[0]
    many, lanes, half = w_ref.shape
    each = many // PIECES
    copies = [
        pltpu.make_async_copy(
            w_hbm.at[pl.ds(p * each, each), pl.ds(0, lanes)], w_ref.at[pl.ds(p * each, each)], sems.at[p]
        )
        for p in range(PIECES)
    ]
    for copy in copies:
        copy.start()
    middle = jnp.concatenate([middle_ref[g] for g in range(middle_ref.shape[0])], axis=1)
    for k in range(many):
        if k % each == 0:
            copies[k // each].wait()
        sums[:, k * lanes : (k + 1) * lanes] = dot_nt(middle, w_ref[k])
    rows = mine_ref.shape[0]
    mine = pl.ds(pl.multiple_of(rows * c, rows), rows)
    other = pl.ds(pl.multiple_of(rows * (1 - c), rows), rows)
    mine_ref[...] = sums[mine]
    send_ref[:, : many * lanes] = sums[other].astype(BF16)
    send_ref[:, many * lanes :] = kept_ref[other]


def multiply_last(at, middle, w, kept, lanes):
    many, _, half = w.shape
    rows = kept.shape[0]
    return pl.pallas_call(
        last_kernel,
        out_shape=(
            jax.ShapeDtypeStruct((rows // 2, many * lanes), F32),
            jax.ShapeDtypeStruct((rows // 2, many * lanes + half), BF16),
        ),
        in_specs=[SCALARS, ON_CHIP, pl.BlockSpec(memory_space=pl.ANY), ON_CHIP],
        out_specs=(ON_CHIP, ON_CHIP),
        scratch_shapes=[
            pltpu.VMEM((rows, many * lanes), F32),
            pltpu.VMEM((many, lanes, half), BF16),
            pltpu.SemaphoreType.DMA((PIECES,)),
        ],
        compiler_params=pltpu.CompilerParams(vmem_limit_bytes=50 * 1024 * 1024),
        cost_estimate=pl.CostEstimate(flops=2 * rows * half * many * lanes, bytes_accessed=5_000_000, transcendentals=0),
    )(at, middle, w, kept)


def halves(part, c):
    half = part.shape[1] // 2
    mine, other = pick(c, part[:, :half], part[:, half:]), pick(c, part[:, half:], part[:, :half])
    return mine, lax.all_gather(other.astype(BF16), "c", axis=0)


def local(planes, w_reduce, w_group, w_expand, gains, biases):
    nx, ny, nc, nz = (lax.axis_size(a) for a in ("x", "y", "c", "z"))
    x, y, c, z = (lax.axis_index(a) for a in ("x", "y", "c", "z"))
    tiles, rows, side, lanes = planes.shape
    blocks, _, width, _ = w_group.shape
    channels = lanes * nz
    half = channels // nc
    zhalf = nz // nc
    own = zhalf * width
    across = nz // tiles
    patch = side // across
    tall = rows * ny * nc
    frame = patch + 2 * LEFT

    early = prepare(y, c, w_reduce, w_expand, w_group, gains, biases)
    at, early = lax.optimization_barrier((jnp.stack([y, c]), early))
    final = prepare_late(at, w_reduce, w_expand, width)
    early = lax.all_gather(early, "z", axis=0)
    final = lax.all_gather(final, "z", axis=0)

    wide = jnp.pad(planes, ((0, 0), (0, 0), (LEFT, LEFT), (0, 0)))
    strips = jnp.stack([wide[:, :, patch * q : patch * q + frame] for q in range(across)], axis=1)
    strips = strips.reshape(nz, rows, frame, lanes)
    mixed = lax.all_to_all(strips, "z", 0, 0, tiled=True)
    mine = pick(c, mixed[:zhalf], mixed[zhalf:])
    theirs = swap_core(pick(c, mixed[zhalf:], mixed[:zhalf]), c)
    chip = jnp.concatenate([pick(c, mine, theirs), pick(c, theirs, mine)], axis=1)
    chip = chip.transpose(1, 2, 0, 3).reshape(rows * nc, frame, half)
    body = lax.all_gather(chip, "y", axis=0, tiled=True)
    above = lax.ppermute(body[tall - HALO :], "x", [(i, i + 1) for i in range(nx - 1)])
    below = lax.ppermute(body[:HALO], "x", [(i + 1, i) for i in range(nx - 1)])
    gathered = jnp.concatenate([above, body, below], axis=0)

    j = lax.broadcasted_iota(jnp.int32, (half, own), 0)
    k = lax.broadcasted_iota(jnp.int32, (half, own), 1)
    pull = (j == (k // width) * lanes + width * y + k % width).astype(BF16)
    stream = jnp.dot(gathered.reshape(-1, half), pull, preferred_element_type=F32).astype(BF16)
    lean = patch + LEFT
    margin = (frame - lean) // 2
    stream = stream.reshape(tall + 2 * HALO, frame, own)[1:-1, margin : margin + lean].reshape(-1, own)
    for b in range(blocks):
        high = tall + 2 * (HALO - b)
        left = LEFT if b == 0 else LEFT - margin
        at = jnp.stack([c, tall * x - (HALO - b), patch * (z % across) - left])
        if b:
            gathered = lax.all_gather(stream, "y", axis=1, tiled=True)
            if b < blocks - 1:
                w = later[2 * b - 1]
            else:
                gathered, final = lax.optimization_barrier((gathered, final))
                w = final[:, lanes:].reshape(-1, half)
            part = dot_nt(gathered, w)
            other = pick(c, part[:, own:], part[:, :own]).astype(BF16)
            stream = stream[lean:-lean]
        else:
            part, other, table = multiply_first(at, gathered.reshape(-1, half), early, own)
            table = table.reshape(own, half)
        high -= 2
        trim = (margin, margin + lean) if b == 0 else (left, left + patch) if b == blocks - 1 else None
        got = lax.all_gather(other, "c", axis=0)
        if b:
            middle, after = convolve(b, high, lean, width, trim, side, at, part, got, table)
        else:
            middle, after, *later = convolve(b, high, frame, width, trim, side, at, part, got, table, early)
            later = [w.reshape(-1, half) for w in later]
        if b < blocks - 1:
            middle = lax.all_gather(middle, "y", axis=1, tiled=True)
            mine, got = halves(dot_nt(middle, later[2 * b]), c)
            second = mine + pick(c, got[1], got[0]).astype(F32)
            stream = jnp.maximum(after[0] * second + after[1] + stream.astype(F32), 0.0).astype(BF16)

    deep = rows * nc
    spots_of_chip = deep * patch
    early, middle = lax.optimization_barrier((early, middle))
    last = early[:, TABLE, :, LAST : LAST + 3 * LAST_STEP].astype(F32).reshape(nz, width, 3, ny, 2)
    last = (last[:, :, 0] + last[:, :, 1] + last[:, :, 2]).transpose(3, 0, 2, 1).reshape(2, nz, lanes)
    middle = lax.all_to_all(middle.reshape(ny, spots_of_chip, own), "y", 0, 0, tiled=True)
    t = lax.broadcasted_iota(jnp.int32, (spots_of_chip, gathered.shape[0]), 0)
    j = lax.broadcasted_iota(jnp.int32, (spots_of_chip, gathered.shape[0]), 1)
    of_chip = (j == (1 + deep * y + t // patch) * lean + LEFT - margin + t % patch).astype(BF16)
    kept = jnp.dot(of_chip, gathered, preferred_element_type=F32).astype(BF16)
    j = lax.broadcasted_iota(jnp.int32, (half, half), 0)
    k = lax.broadcasted_iota(jnp.int32, (half, half), 1)
    natural = (j == (k // width % ny) * own + k // lanes * width + k % width).astype(BF16)
    kept = jnp.dot(kept, natural, preferred_element_type=F32).astype(BF16)
    second, send = multiply_last(at, middle, final, kept, lanes)
    got = swap_core(send, c)
    kept = kept.reshape(nc, rows * patch, half)
    mine, theirs = pick(c, kept[0], kept[1]), got[:, nz * lanes :]
    residual = jnp.concatenate([pick(c, mine, theirs), pick(c, theirs, mine)], axis=1)
    second = second + got[:, : nz * lanes].astype(F32)
    gain, bias = last.reshape(2, 1, nz * lanes)
    out = jnp.maximum(gain * second + bias + residual.astype(F32), 0.0).astype(BF16)
    out = out.reshape(rows * patch, nz, lanes)
    out = out.transpose(1, 0, 2).reshape(nz, rows, patch, lanes)
    out = lax.all_to_all(out, "z", 0, 0, tiled=True).reshape(tiles, across, rows, patch, lanes)
    return out.transpose(0, 2, 1, 3, 4).reshape(tiles, rows, side, lanes)


def solution(mesh):
    grid = Mesh(mesh.devices.reshape(4, 4, 2, 16), ("x", "y", "c", "z"))
    placed = (
        P(None, SEG, None, "z"),
        P(None, None, "z"),
        P(None, None, None, "z"),
        P(None, None, "z"),
        P(None, None, "z"),
        P(None, None, "z"),
    )
    return jax.shard_map(local, mesh=grid, in_specs=placed, out_specs=P(None, SEG, None, "z"), check_vma=False)
```

```python
import functools

import jax
import jax.numpy as jnp
from jax import lax
from jax.experimental import pallas as pl
from jax.experimental.pallas import tpu as pltpu
from jax.sharding import Mesh
from jax.sharding import PartitionSpec as P

BF16 = jnp.bfloat16
F32 = jnp.float32
SEG = ("x", "y", "c")
LEFT = 4
HALO = 3


def dot_nt(a, b):
    return lax.dot_general(a, b, (((1,), (1,)), ((), ())), preferred_element_type=F32)


def selector(rows, cols, base):
    i = lax.broadcasted_iota(jnp.int32, (rows, cols), 0)
    j = lax.broadcasted_iota(jnp.int32, (rows, cols), 1)
    return (j == i + base).astype(BF16)


def terms(v):
    out = []
    for _ in range(3):
        t = v.astype(BF16).astype(F32)
        out.append(t)
        v = v - t
    return out


def pick(c, a, b):
    return jnp.where(c == 0, a, b)


def swap_core(v, c):
    both = lax.all_gather(v, "c", axis=0)
    return pick(c, both[1], both[0])


SPOTS = (0, 320, 640)
OWNED, OWNED_STEP = 928, 24
LAST, LAST_STEP = 1000, 8
VMEM_LIMIT = 12 * 1024 * 1024
FIRST_LIMIT = 50 * 1024 * 1024


def prep_kernel(
    wr_hbm, we_hbm, wg_hbm, gains_hbm, biases_hbm, out_hbm,
    wr_ref, we_ref, wg_ref, gains_ref, biases_ref, table, out_ref, sems, out_sems,
):
    y, c = lax.axis_index("y"), lax.axis_index("c")
    width, half = out_ref.shape[1:]
    lanes = wr_ref.shape[2]
    ny = lanes // width
    zhalf = half // lanes
    rows = pl.ds(pl.multiple_of(half * c, half), half)
    small = [
        pltpu.make_async_copy(gains_hbm, gains_ref, sems.at[6]),
        pltpu.make_async_copy(biases_hbm, biases_ref, sems.at[7]),
    ]
    copies = [pltpu.make_async_copy(wg_hbm, wg_ref, sems.at[0])]
    for b in range(3):
        copies.append(pltpu.make_async_copy(wr_hbm.at[b, rows], wr_ref.at[b], sems.at[1 + b]))
    for b in range(2):
        copies.append(pltpu.make_async_copy(we_hbm.at[b, rows], we_ref.at[b], sems.at[4 + b]))
    for copy in small + copies:
        copy.start()

    def done(slot):
        copy = pltpu.make_async_copy(out_ref.at[slot], out_hbm.at[slot], out_sems.at[slot])
        copy.start()
        return copy

    sel = selector(width, lanes, width * y)

    table[...] = jnp.zeros_like(table)
    for copy in small:
        copy.wait()
    for which, ref in enumerate((gains_ref, biases_ref)):
        for b in range(3):
            for t, v in enumerate(terms(ref[b])):
                spot = OWNED + OWNED_STEP * t + 3 * (3 * which + b)
                table[spot : spot + 3] = v
                if b == 2:
                    for g in range(ny):
                        spot = LAST + LAST_STEP * t + 2 * g + which
                        table[spot : spot + 1] = v[2:3]
    copies[0].wait()
    for b, spot in enumerate(SPOTS):
        table[spot : spot + wg_ref.shape[1]] = wg_ref[b].astype(F32)
    row = lax.broadcasted_iota(jnp.int32, table.shape, 0)
    lane = lax.broadcasted_iota(jnp.int32, table.shape, 1)
    wanted = jnp.where(row < LAST, y, ((row - LAST) & (LAST_STEP - 1)) >> 1)
    kept = jnp.where((lane >> 5) == wanted, table[...], 0.0).astype(BF16)
    i = lax.broadcasted_iota(jnp.int32, (width, lanes), 0)
    j = lax.broadcasted_iota(jnp.int32, (width, lanes), 1)
    out_ref[5] = dot_nt(((j & (width - 1)) == i).astype(BF16), kept).astype(BF16)
    outs = [done(5)]

    def put(slot, w):
        w = w.reshape(zhalf, ny, width, lanes)
        for g in range(ny):
            rows = w[:, g].reshape(zhalf * width, lanes)
            out_ref[slot, :, g * zhalf * width : (g + 1) * zhalf * width] = dot_nt(sel, rows).astype(BF16)

    copies[1].wait()
    out_ref[0] = dot_nt(sel, wr_ref[0]).astype(BF16)
    outs.append(done(0))
    for copy, slot, ref in ((2, 2, wr_ref.at[1]), (3, 4, wr_ref.at[2]), (4, 1, we_ref.at[0]), (5, 3, we_ref.at[1])):
        copies[copy].wait()
        put(slot, ref[...])
        outs.append(done(slot))
    for copy in outs:
        copy.wait()


def prepare(w_reduce, w_expand, w_group, gains, biases):
    blocks, depth, lanes = w_reduce.shape
    width = w_group.shape[2]
    half = depth // 2
    there = pl.BlockSpec(memory_space=pl.ANY)
    return pl.pallas_call(
        prep_kernel,
        out_shape=jax.ShapeDtypeStruct((6, width, half), BF16),
        in_specs=[there] * 5,
        out_specs=there,
        scratch_shapes=[
            pltpu.VMEM((3, half, lanes), BF16),
            pltpu.VMEM((2, half, lanes), BF16),
            pltpu.VMEM((blocks, 9 * width, lanes), BF16),
            pltpu.VMEM(gains.shape, F32),
            pltpu.VMEM(biases.shape, F32),
            pltpu.VMEM((half, lanes), F32),
            pltpu.VMEM((6, width, half), BF16),
            pltpu.SemaphoreType.DMA((8,)),
            pltpu.SemaphoreType.DMA((6,)),
        ],
        compiler_params=pltpu.CompilerParams(vmem_limit_bytes=60 * 1024 * 1024),
        cost_estimate=pl.CostEstimate(flops=2 * 6 * half * lanes * width, bytes_accessed=2_500_000, transcendentals=0),
    )(w_reduce, w_expand, w_group.reshape(blocks, -1, lanes), gains, biases)


def conv_kernel(b, high, frame, width, trim, side, at, part_ref, got_ref, table_ref, out_ref, after_ref, sums):
    c, row0, col0 = at[0], at[1], at[2]
    count, own = got_ref.shape[1:]
    i = lax.broadcasted_iota(jnp.int32, (own, own), 0)
    j = lax.broadcasted_iota(jnp.int32, (own, own), 1)
    eye = (i == j).astype(BF16)

    def columns(start, count):
        some = table_ref[:, start : start + count]
        return lax.dot_general(some, eye, (((0,), (0,)), ((), ())), preferred_element_type=F32)

    rows = columns(OWNED // 128 * 128, 128)

    def param(which, k):
        at_row = OWNED % 128 + (which * 3 + b) * 3 + k
        return sum(rows[at_row + OWNED_STEP * t : at_row + OWNED_STEP * t + 1] for t in range(3))

    if part_ref.shape[1] == own:
        mine = part_ref[...]
    else:
        mine = part_ref[:, pl.ds(pl.multiple_of(own * c, own), own)]
    hidden = jnp.maximum(param(0, 0) * (mine + got_ref[1 - c].astype(F32)) + param(1, 0), 0.0)
    spot = lax.broadcasted_iota(jnp.int32, hidden.shape, 0)
    row = ((spot.astype(F32) + 0.5) * (1.0 / frame)).astype(jnp.int32)
    col = col0 + spot - row * frame
    row = row0 + row
    inside = (row >= 0) & (row < side) & (col >= 0) & (col < side)
    hidden = jnp.where(inside, hidden, 0.0)
    spread = (
        (lax.broadcasted_iota(jnp.int32, (own, width), 0) & (width - 1))
        == lax.broadcasted_iota(jnp.int32, (own, width), 1)
    ).astype(BF16)
    same = (i >> 5) == (j >> 5)
    base = SPOTS[b] // 128 * 128
    filters = columns(base, 384).astype(BF16)
    fit = high * frame
    shifted = jnp.concatenate([hidden[frame * r : frame * r + fit].astype(BF16) for r in range(3)], axis=1)
    terms_of = []
    for s in range(3):
        taps = []
        for r in range(3):
            spot = SPOTS[b] - base + (3 * r + s) * width
            tap = jnp.dot(spread, filters[spot : spot + width], preferred_element_type=F32)
            taps.append(jnp.where(same, tap, 0.0).astype(BF16))
        terms_of.append(jnp.dot(shifted, jnp.concatenate(taps, axis=0), preferred_element_type=F32))
    spatial = pltpu.roll(terms_of[0], 1, 0) + terms_of[1] + pltpu.roll(terms_of[2], fit - 1, 0)
    middle = jnp.maximum(param(0, 1) * spatial + param(1, 1), 0.0)
    if trim:
        lo, hi = trim
        for r in range(high):
            sums[r * (hi - lo) : (r + 1) * (hi - lo)] = middle[r * frame + lo : r * frame + hi]
        middle = sums[...]
    out_ref[...] = middle.astype(BF16)
    after_ref[0:1] = param(0, 2)
    after_ref[1:2] = param(1, 2)


ON_CHIP = pl.BlockSpec(memory_space=pltpu.VMEM)
SCALARS = pl.BlockSpec(memory_space=pltpu.SMEM)


def convolve(b, high, frame, width, trim, side, at, part, got, table):
    own = got.shape[2]
    cols = trim[1] - trim[0] if trim else frame
    return pl.pallas_call(
        functools.partial(conv_kernel, b, high, frame, width, trim, side),
        out_shape=(jax.ShapeDtypeStruct((high * cols, own), BF16), jax.ShapeDtypeStruct((8, own), F32)),
        in_specs=[SCALARS, ON_CHIP, ON_CHIP, ON_CHIP],
        out_specs=(ON_CHIP, ON_CHIP),
        scratch_shapes=[pltpu.VMEM((high * cols, own), F32)],
        compiler_params=pltpu.CompilerParams(vmem_limit_bytes=VMEM_LIMIT),
        cost_estimate=pl.CostEstimate(flops=18 * high * frame * own * own, bytes_accessed=2_500_000, transcendentals=0),
    )(at, part, got, table)


def first_kernel(at, x_ref, early_hbm, mine_ref, other_ref, table_ref, w_ref, sems):
    c = at[0]
    own = mine_ref.shape[1]
    mine = pl.ds(pl.multiple_of(own * c, own), own)
    other = pl.ds(pl.multiple_of(own * (1 - c), own), own)
    copies = [
        pltpu.make_async_copy(early_hbm.at[0, other], w_ref.at[0], sems.at[0]),
        pltpu.make_async_copy(early_hbm.at[0, mine], w_ref.at[1], sems.at[1]),
        pltpu.make_async_copy(early_hbm.at[5, mine], table_ref, sems.at[2]),
    ]
    for copy in copies:
        copy.start()
    copies[0].wait()
    other_ref[...] = dot_nt(x_ref[...], w_ref[0]).astype(BF16)
    copies[1].wait()
    mine_ref[...] = dot_nt(x_ref[...], w_ref[1])
    copies[2].wait()


def multiply_first(at, x, early, own):
    count, half = x.shape
    return pl.pallas_call(
        first_kernel,
        out_shape=(
            jax.ShapeDtypeStruct((count, own), F32),
            jax.ShapeDtypeStruct((count, own), BF16),
            jax.ShapeDtypeStruct((own, half), BF16),
        ),
        in_specs=[SCALARS, ON_CHIP, pl.BlockSpec(memory_space=pl.ANY)],
        out_specs=(ON_CHIP, ON_CHIP, ON_CHIP),
        scratch_shapes=[pltpu.VMEM((2, own, half), BF16), pltpu.SemaphoreType.DMA((3,))],
        compiler_params=pltpu.CompilerParams(vmem_limit_bytes=FIRST_LIMIT),
        cost_estimate=pl.CostEstimate(flops=4 * count * half * own, bytes_accessed=4_000_000, transcendentals=0),
    )(at, x, early)


PIECES = 4


def last_kernel(at, middle_ref, w_hbm, kept_ref, mine_ref, send_ref, sums, w_ref, sems):
    c = at[0]
    many, half, lanes = w_ref.shape
    each = many // PIECES
    copies = [
        pltpu.make_async_copy(w_hbm.at[pl.ds(p * each, each)], w_ref.at[pl.ds(p * each, each)], sems.at[p])
        for p in range(PIECES)
    ]
    for copy in copies:
        copy.start()
    middle = jnp.concatenate([middle_ref[g] for g in range(middle_ref.shape[0])], axis=1)
    for k in range(many):
        if k % each == 0:
            copies[k // each].wait()
        sums[:, k * lanes : (k + 1) * lanes] = jnp.dot(middle, w_ref[k], preferred_element_type=F32)
    rows = mine_ref.shape[0]
    mine = pl.ds(pl.multiple_of(rows * c, rows), rows)
    other = pl.ds(pl.multiple_of(rows * (1 - c), rows), rows)
    mine_ref[...] = sums[mine]
    send_ref[:, : many * lanes] = sums[other].astype(BF16)
    send_ref[:, many * lanes :] = kept_ref[other]


def multiply_last(at, middle, w, kept):
    many, half, lanes = w.shape
    rows = kept.shape[0]
    return pl.pallas_call(
        last_kernel,
        out_shape=(
            jax.ShapeDtypeStruct((rows // 2, many * lanes), F32),
            jax.ShapeDtypeStruct((rows // 2, many * lanes + half), BF16),
        ),
        in_specs=[SCALARS, ON_CHIP, pl.BlockSpec(memory_space=pl.ANY), ON_CHIP],
        out_specs=(ON_CHIP, ON_CHIP),
        scratch_shapes=[
            pltpu.VMEM((rows, many * lanes), F32),
            pltpu.VMEM(w.shape, BF16),
            pltpu.SemaphoreType.DMA((PIECES,)),
        ],
        compiler_params=pltpu.CompilerParams(vmem_limit_bytes=50 * 1024 * 1024),
        cost_estimate=pl.CostEstimate(flops=2 * rows * half * many * lanes, bytes_accessed=5_000_000, transcendentals=0),
    )(at, middle, w, kept)


def halves(part, c):
    half = part.shape[1] // 2
    mine, other = pick(c, part[:, :half], part[:, half:]), pick(c, part[:, half:], part[:, :half])
    return mine, lax.all_gather(other.astype(BF16), "c", axis=0)


def local(planes, w_reduce, w_group, w_expand, gains, biases):
    nx, ny, nc, nz = (lax.axis_size(a) for a in ("x", "y", "c", "z"))
    x, y, c, z = (lax.axis_index(a) for a in ("x", "y", "c", "z"))
    tiles, rows, side, lanes = planes.shape
    blocks, _, width, _ = w_group.shape
    channels = lanes * nz
    half = channels // nc
    zhalf = nz // nc
    own = zhalf * width
    across = nz // tiles
    patch = side // across
    tall = rows * ny * nc
    frame = patch + 2 * LEFT

    early = lax.all_gather(prepare(w_reduce, w_expand, w_group, gains, biases), "z", axis=1, tiled=True)
    final = lax.dynamic_slice_in_dim(w_expand[2], half * c, half, axis=0)
    final = final.reshape(zhalf, ny, width, lanes).transpose(1, 0, 2, 3).reshape(half, lanes)
    final = lax.all_gather(final, "z", axis=0)

    wide = jnp.pad(planes, ((0, 0), (0, 0), (LEFT, LEFT), (0, 0)))
    strips = jnp.stack([wide[:, :, patch * q : patch * q + frame] for q in range(across)], axis=1)
    strips = strips.reshape(nz, rows, frame, lanes)
    mixed = lax.all_to_all(strips, "z", 0, 0, tiled=True)
    mine = pick(c, mixed[:zhalf], mixed[zhalf:])
    theirs = swap_core(pick(c, mixed[zhalf:], mixed[:zhalf]), c)
    chip = jnp.concatenate([pick(c, mine, theirs), pick(c, theirs, mine)], axis=1)
    chip = chip.transpose(1, 2, 0, 3).reshape(rows * nc, frame, half)
    body = lax.all_gather(chip, "y", axis=0, tiled=True)
    above = lax.ppermute(body[tall - HALO :], "x", [(i, i + 1) for i in range(nx - 1)])
    below = lax.ppermute(body[:HALO], "x", [(i + 1, i) for i in range(nx - 1)])
    gathered = jnp.concatenate([above, body, below], axis=0)

    last = early[5, :, LAST : LAST + 3 * LAST_STEP].astype(F32).reshape(nz, width, 3, ny, 2)
    last = (last[:, :, 0] + last[:, :, 1] + last[:, :, 2]).transpose(3, 0, 2, 1).reshape(2, nz, lanes)

    j = lax.broadcasted_iota(jnp.int32, (half, own), 0)
    k = lax.broadcasted_iota(jnp.int32, (half, own), 1)
    pull = (j == (k // width) * lanes + width * y + k % width).astype(BF16)
    stream = jnp.dot(gathered.reshape(-1, half), pull, preferred_element_type=F32).astype(BF16)
    lean = patch + LEFT
    margin = (frame - lean) // 2
    stream = stream.reshape(tall + 2 * HALO, frame, own)[1:-1, margin : margin + lean].reshape(-1, own)
    for b in range(blocks):
        high = tall + 2 * (HALO - b)
        left = LEFT if b == 0 else LEFT - margin
        at = jnp.stack([c, tall * x - (HALO - b), patch * (z % across) - left])
        if b:
            gathered = lax.all_gather(stream, "y", axis=1, tiled=True)
            part = dot_nt(gathered, early[2 * b])
            other = pick(c, part[:, own:], part[:, :own]).astype(BF16)
            stream = stream[lean:-lean]
        else:
            part, other, table = multiply_first(at, gathered.reshape(-1, half), early, own)
            early, other = lax.optimization_barrier((early, other))
        high -= 2
        trim = (margin, margin + lean) if b == 0 else (left, left + patch) if b == blocks - 1 else None
        got = lax.all_gather(other, "c", axis=0)
        middle, after = convolve(b, high, lean if b else frame, width, trim, side, at, part, got, table)
        if b < blocks - 1:
            middle = lax.all_gather(middle, "y", axis=1, tiled=True)
            mine, got = halves(dot_nt(middle, early[2 * b + 1]), c)
            second = mine + pick(c, got[1], got[0]).astype(F32)
            stream = jnp.maximum(after[0] * second + after[1] + stream.astype(F32), 0.0).astype(BF16)

    deep = rows * nc
    spots_of_chip = deep * patch
    middle = lax.all_to_all(middle.reshape(ny, spots_of_chip, own), "y", 0, 0, tiled=True)
    t = lax.broadcasted_iota(jnp.int32, (spots_of_chip, gathered.shape[0]), 0)
    j = lax.broadcasted_iota(jnp.int32, (spots_of_chip, gathered.shape[0]), 1)
    of_chip = (j == (1 + deep * y + t // patch) * lean + LEFT - margin + t % patch).astype(BF16)
    kept = jnp.dot(of_chip, gathered, preferred_element_type=F32).astype(BF16)
    j = lax.broadcasted_iota(jnp.int32, (half, half), 0)
    k = lax.broadcasted_iota(jnp.int32, (half, half), 1)
    natural = (j == (k // width % ny) * own + k // lanes * width + k % width).astype(BF16)
    kept = jnp.dot(kept, natural, preferred_element_type=F32).astype(BF16)
    second, send = multiply_last(at, middle, final, kept)
    got = swap_core(send, c)
    kept = kept.reshape(nc, rows * patch, half)
    mine, theirs = pick(c, kept[0], kept[1]), got[:, nz * lanes :]
    residual = jnp.concatenate([pick(c, mine, theirs), pick(c, theirs, mine)], axis=1)
    second = second + got[:, : nz * lanes].astype(F32)
    gain, bias = last.reshape(2, 1, nz * lanes)
    out = jnp.maximum(gain * second + bias + residual.astype(F32), 0.0).astype(BF16)
    out = out.reshape(rows * patch, nz, lanes)
    out = out.transpose(1, 0, 2).reshape(nz, rows, patch, lanes)
    out = lax.all_to_all(out, "z", 0, 0, tiled=True).reshape(tiles, across, rows, patch, lanes)
    return out.transpose(0, 2, 1, 3, 4).reshape(tiles, rows, side, lanes)


def solution(mesh):
    grid = Mesh(mesh.devices.reshape(4, 4, 2, 16), ("x", "y", "c", "z"))
    placed = (
        P(None, SEG, None, "z"),
        P(None, None, "z"),
        P(None, None, None, "z"),
        P(None, None, "z"),
        P(None, None, "z"),
        P(None, None, "z"),
    )
    return jax.shard_map(local, mesh=grid, in_specs=placed, out_specs=P(None, SEG, None, "z"), check_vma=False)
```

```python
import functools

import jax
import jax.numpy as jnp
from jax import lax
from jax.experimental import pallas as pl
from jax.experimental.pallas import tpu as pltpu
from jax.sharding import Mesh
from jax.sharding import PartitionSpec as P

BF16 = jnp.bfloat16
F32 = jnp.float32
SEG = ("x", "y", "c")
LEFT = 4
HALO = 3


def dot_nt(a, b):
    return lax.dot_general(a, b, (((1,), (1,)), ((), ())), preferred_element_type=F32)


def selector(rows, cols, base):
    i = lax.broadcasted_iota(jnp.int32, (rows, cols), 0)
    j = lax.broadcasted_iota(jnp.int32, (rows, cols), 1)
    return (j == i + base).astype(BF16)


def terms(v):
    out = []
    for _ in range(3):
        t = v.astype(BF16).astype(F32)
        out.append(t)
        v = v - t
    return out


def pick(c, a, b):
    return jnp.where(c == 0, a, b)


def swap_core(v, c):
    both = lax.all_gather(v, "c", axis=0)
    return pick(c, both[1], both[0])


SPOTS = (0, 320, 640)
OWNED, OWNED_STEP = 928, 24
LAST, LAST_STEP = 1000, 8
VMEM_LIMIT = 12 * 1024 * 1024
FIRST_LIMIT = 50 * 1024 * 1024


def prep_kernel(
    wr_hbm, we_hbm, wg_hbm, gains_hbm, biases_hbm, out_hbm,
    wr_ref, we_ref, wg_ref, gains_ref, biases_ref, table, out_ref, sems, out_sems,
):
    y, c = lax.axis_index("y"), lax.axis_index("c")
    width, half = out_ref.shape[1:]
    lanes = wr_ref.shape[2]
    ny = lanes // width
    zhalf = half // lanes
    rows = pl.ds(pl.multiple_of(half * c, half), half)
    small = [
        pltpu.make_async_copy(gains_hbm, gains_ref, sems.at[6]),
        pltpu.make_async_copy(biases_hbm, biases_ref, sems.at[7]),
    ]
    copies = [pltpu.make_async_copy(wg_hbm, wg_ref, sems.at[0])]
    for b in range(3):
        copies.append(pltpu.make_async_copy(wr_hbm.at[b, rows], wr_ref.at[b], sems.at[1 + b]))
    for b in range(2):
        copies.append(pltpu.make_async_copy(we_hbm.at[b, rows], we_ref.at[b], sems.at[4 + b]))
    for copy in small + copies:
        copy.start()

    def done(slot):
        copy = pltpu.make_async_copy(out_ref.at[slot], out_hbm.at[slot], out_sems.at[slot])
        copy.start()
        return copy

    sel = selector(width, lanes, width * y)

    table[...] = jnp.zeros_like(table)
    for copy in small:
        copy.wait()
    for which, ref in enumerate((gains_ref, biases_ref)):
        for b in range(3):
            for t, v in enumerate(terms(ref[b])):
                spot = OWNED + OWNED_STEP * t + 3 * (3 * which + b)
                table[spot : spot + 3] = v
                if b == 2:
                    for g in range(ny):
                        spot = LAST + LAST_STEP * t + 2 * g + which
                        table[spot : spot + 1] = v[2:3]
    copies[0].wait()
    for b, spot in enumerate(SPOTS):
        table[spot : spot + wg_ref.shape[1]] = wg_ref[b].astype(F32)
    row = lax.broadcasted_iota(jnp.int32, table.shape, 0)
    lane = lax.broadcasted_iota(jnp.int32, table.shape, 1)
    wanted = jnp.where(row < LAST, y, ((row - LAST) & (LAST_STEP - 1)) >> 1)
    kept = jnp.where((lane >> 5) == wanted, table[...], 0.0).astype(BF16)
    i = lax.broadcasted_iota(jnp.int32, (width, lanes), 0)
    j = lax.broadcasted_iota(jnp.int32, (width, lanes), 1)
    out_ref[5] = dot_nt(((j & (width - 1)) == i).astype(BF16), kept).astype(BF16)
    outs = [done(5)]

    def put(slot, w):
        w = w.reshape(zhalf, ny, width, lanes)
        for g in range(ny):
            rows = w[:, g].reshape(zhalf * width, lanes)
            out_ref[slot, :, g * zhalf * width : (g + 1) * zhalf * width] = dot_nt(sel, rows).astype(BF16)

    copies[1].wait()
    out_ref[0] = dot_nt(sel, wr_ref[0]).astype(BF16)
    outs.append(done(0))
    for copy, slot, ref in ((2, 2, wr_ref.at[1]), (3, 4, wr_ref.at[2]), (4, 1, we_ref.at[0]), (5, 3, we_ref.at[1])):
        copies[copy].wait()
        put(slot, ref[...])
        outs.append(done(slot))
    for copy in outs:
        copy.wait()


def prepare(w_reduce, w_expand, w_group, gains, biases):
    blocks, depth, lanes = w_reduce.shape
    width = w_group.shape[2]
    half = depth // 2
    there = pl.BlockSpec(memory_space=pl.ANY)
    return pl.pallas_call(
        prep_kernel,
        out_shape=jax.ShapeDtypeStruct((6, width, half), BF16),
        in_specs=[there] * 5,
        out_specs=there,
        scratch_shapes=[
            pltpu.VMEM((3, half, lanes), BF16),
            pltpu.VMEM((2, half, lanes), BF16),
            pltpu.VMEM((blocks, 9 * width, lanes), BF16),
            pltpu.VMEM(gains.shape, F32),
            pltpu.VMEM(biases.shape, F32),
            pltpu.VMEM((half, lanes), F32),
            pltpu.VMEM((6, width, half), BF16),
            pltpu.SemaphoreType.DMA((8,)),
            pltpu.SemaphoreType.DMA((6,)),
        ],
        compiler_params=pltpu.CompilerParams(vmem_limit_bytes=60 * 1024 * 1024),
        cost_estimate=pl.CostEstimate(flops=2 * 6 * half * lanes * width, bytes_accessed=2_500_000, transcendentals=0),
    )(w_reduce, w_expand, w_group.reshape(blocks, -1, lanes), gains, biases)


def conv_kernel(b, high, frame, width, trim, side, at, part_ref, got_ref, table_ref, out_ref, after_ref, sums):
    c, row0, col0 = at[0], at[1], at[2]
    count, own = got_ref.shape[1:]
    i = lax.broadcasted_iota(jnp.int32, (own, own), 0)
    j = lax.broadcasted_iota(jnp.int32, (own, own), 1)
    eye = (i == j).astype(BF16)

    def columns(start, count):
        some = table_ref[:, start : start + count]
        return lax.dot_general(some, eye, (((0,), (0,)), ((), ())), preferred_element_type=F32)

    rows = columns(OWNED // 128 * 128, 128)

    def param(which, k):
        at_row = OWNED % 128 + (which * 3 + b) * 3 + k
        return sum(rows[at_row + OWNED_STEP * t : at_row + OWNED_STEP * t + 1] for t in range(3))

    if part_ref.shape[1] == own:
        mine = part_ref[...]
    else:
        mine = part_ref[:, pl.ds(pl.multiple_of(own * c, own), own)]
    hidden = jnp.maximum(param(0, 0) * (mine + got_ref[1 - c].astype(F32)) + param(1, 0), 0.0)
    spot = lax.broadcasted_iota(jnp.int32, (hidden.shape[0], 1), 0)
    row = ((spot.astype(F32) + 0.5) * (1.0 / frame)).astype(jnp.int32)
    col = col0 + spot - row * frame
    row = row0 + row
    inside = (row >= 0) & (row < side) & (col >= 0) & (col < side)
    hidden = jnp.where(inside, hidden, 0.0)
    spread = (
        (lax.broadcasted_iota(jnp.int32, (own, width), 0) & (width - 1))
        == lax.broadcasted_iota(jnp.int32, (own, width), 1)
    ).astype(BF16)
    same = (i >> 5) == (j >> 5)
    base = SPOTS[b] // 128 * 128
    filters = columns(base, 384).astype(BF16)
    fit = high * frame
    shifted = jnp.concatenate([hidden[frame * r : frame * r + fit].astype(BF16) for r in range(3)], axis=1)
    terms_of = []
    for s in range(3):
        taps = []
        for r in range(3):
            spot = SPOTS[b] - base + (3 * r + s) * width
            tap = jnp.dot(spread, filters[spot : spot + width], preferred_element_type=F32)
            taps.append(jnp.where(same, tap, 0.0).astype(BF16))
        terms_of.append(jnp.dot(shifted, jnp.concatenate(taps, axis=0), preferred_element_type=F32))
    spatial = pltpu.roll(terms_of[0], 1, 0) + terms_of[1] + pltpu.roll(terms_of[2], fit - 1, 0)
    middle = jnp.maximum(param(0, 1) * spatial + param(1, 1), 0.0)
    if trim:
        lo, hi = trim
        for r in range(high):
            sums[r * (hi - lo) : (r + 1) * (hi - lo)] = middle[r * frame + lo : r * frame + hi]
        middle = sums[...]
    out_ref[...] = middle.astype(BF16)
    after_ref[0:1] = param(0, 2)
    after_ref[1:2] = param(1, 2)


ON_CHIP = pl.BlockSpec(memory_space=pltpu.VMEM)
SCALARS = pl.BlockSpec(memory_space=pltpu.SMEM)


def convolve(b, high, frame, width, trim, side, at, part, got, table):
    own = got.shape[2]
    cols = trim[1] - trim[0] if trim else frame
    return pl.pallas_call(
        functools.partial(conv_kernel, b, high, frame, width, trim, side),
        out_shape=(jax.ShapeDtypeStruct((high * cols, own), BF16), jax.ShapeDtypeStruct((8, own), F32)),
        in_specs=[SCALARS, ON_CHIP, ON_CHIP, ON_CHIP],
        out_specs=(ON_CHIP, ON_CHIP),
        scratch_shapes=[pltpu.VMEM((high * cols, own), F32)],
        compiler_params=pltpu.CompilerParams(vmem_limit_bytes=VMEM_LIMIT),
        cost_estimate=pl.CostEstimate(flops=18 * high * frame * own * own, bytes_accessed=2_500_000, transcendentals=0),
    )(at, part, got, table)


def first_kernel(at, x_ref, early_hbm, mine_ref, other_ref, table_ref, w_ref, sems):
    c = at[0]
    own = mine_ref.shape[1]
    mine = pl.ds(pl.multiple_of(own * c, own), own)
    other = pl.ds(pl.multiple_of(own * (1 - c), own), own)
    copies = [
        pltpu.make_async_copy(early_hbm.at[0, other], w_ref.at[0], sems.at[0]),
        pltpu.make_async_copy(early_hbm.at[0, mine], w_ref.at[1], sems.at[1]),
        pltpu.make_async_copy(early_hbm.at[5, mine], table_ref, sems.at[2]),
    ]
    for copy in copies:
        copy.start()
    copies[0].wait()
    other_ref[...] = dot_nt(x_ref[...], w_ref[0]).astype(BF16)
    copies[1].wait()
    mine_ref[...] = dot_nt(x_ref[...], w_ref[1])
    copies[2].wait()


def multiply_first(at, x, early, own):
    count, half = x.shape
    return pl.pallas_call(
        first_kernel,
        out_shape=(
            jax.ShapeDtypeStruct((count, own), F32),
            jax.ShapeDtypeStruct((count, own), BF16),
            jax.ShapeDtypeStruct((own, half), BF16),
        ),
        in_specs=[SCALARS, ON_CHIP, pl.BlockSpec(memory_space=pl.ANY)],
        out_specs=(ON_CHIP, ON_CHIP, ON_CHIP),
        scratch_shapes=[pltpu.VMEM((2, own, half), BF16), pltpu.SemaphoreType.DMA((3,))],
        compiler_params=pltpu.CompilerParams(vmem_limit_bytes=FIRST_LIMIT),
        cost_estimate=pl.CostEstimate(flops=4 * count * half * own, bytes_accessed=4_000_000, transcendentals=0),
    )(at, x, early)


PIECES = 8


def last_kernel(at, middle_ref, w_hbm, kept_ref, mine_ref, send_ref, sums, w_ref, sems):
    c = at[0]
    many, half, lanes = w_ref.shape
    each = many // PIECES
    copies = [
        pltpu.make_async_copy(w_hbm.at[pl.ds(p * each, each)], w_ref.at[pl.ds(p * each, each)], sems.at[p])
        for p in range(PIECES)
    ]
    for copy in copies:
        copy.start()
    middle = jnp.concatenate([middle_ref[g] for g in range(middle_ref.shape[0])], axis=1)
    for k in range(many):
        if k % each == 0:
            copies[k // each].wait()
        sums[:, k * lanes : (k + 1) * lanes] = jnp.dot(middle, w_ref[k], preferred_element_type=F32)
    rows = mine_ref.shape[0]
    mine = pl.ds(pl.multiple_of(rows * c, rows), rows)
    other = pl.ds(pl.multiple_of(rows * (1 - c), rows), rows)
    mine_ref[...] = sums[mine]
    send_ref[:, : many * lanes] = sums[other].astype(BF16)
    send_ref[:, many * lanes :] = kept_ref[other]


def multiply_last(at, middle, w, kept):
    many, half, lanes = w.shape
    rows = kept.shape[0]
    return pl.pallas_call(
        last_kernel,
        out_shape=(
            jax.ShapeDtypeStruct((rows // 2, many * lanes), F32),
            jax.ShapeDtypeStruct((rows // 2, many * lanes + half), BF16),
        ),
        in_specs=[SCALARS, ON_CHIP, pl.BlockSpec(memory_space=pl.ANY), ON_CHIP],
        out_specs=(ON_CHIP, ON_CHIP),
        scratch_shapes=[
            pltpu.VMEM((rows, many * lanes), F32),
            pltpu.VMEM(w.shape, BF16),
            pltpu.SemaphoreType.DMA((PIECES,)),
        ],
        compiler_params=pltpu.CompilerParams(vmem_limit_bytes=50 * 1024 * 1024),
        cost_estimate=pl.CostEstimate(flops=2 * rows * half * many * lanes, bytes_accessed=5_000_000, transcendentals=0),
    )(at, middle, w, kept)


def halves(part, c):
    half = part.shape[1] // 2
    mine, other = pick(c, part[:, :half], part[:, half:]), pick(c, part[:, half:], part[:, :half])
    return mine, lax.all_gather(other.astype(BF16), "c", axis=0)


def local(planes, w_reduce, w_group, w_expand, gains, biases):
    nx, ny, nc, nz = (lax.axis_size(a) for a in ("x", "y", "c", "z"))
    x, y, c, z = (lax.axis_index(a) for a in ("x", "y", "c", "z"))
    tiles, rows, side, lanes = planes.shape
    blocks, _, width, _ = w_group.shape
    channels = lanes * nz
    half = channels // nc
    zhalf = nz // nc
    own = zhalf * width
    across = nz // tiles
    patch = side // across
    tall = rows * ny * nc
    frame = patch + 2 * LEFT

    early = lax.all_gather(prepare(w_reduce, w_expand, w_group, gains, biases), "z", axis=1, tiled=True)
    final = lax.dynamic_slice_in_dim(w_expand[2], half * c, half, axis=0)
    final = final.reshape(zhalf, ny, width, lanes).transpose(1, 0, 2, 3).reshape(half, lanes)
    final = lax.all_gather(final, "z", axis=0)

    wide = jnp.pad(planes, ((0, 0), (0, 0), (LEFT, LEFT), (0, 0)))
    strips = jnp.stack([wide[:, :, patch * q : patch * q + frame] for q in range(across)], axis=1)
    strips = strips.reshape(nz, rows, frame, lanes)
    mixed = lax.all_to_all(strips, "z", 0, 0, tiled=True)
    mine = pick(c, mixed[:zhalf], mixed[zhalf:])
    theirs = swap_core(pick(c, mixed[zhalf:], mixed[:zhalf]), c)
    chip = jnp.concatenate([pick(c, mine, theirs), pick(c, theirs, mine)], axis=1)
    chip = chip.transpose(1, 2, 0, 3).reshape(rows * nc, frame, half)
    body = lax.all_gather(chip, "y", axis=0, tiled=True)
    above = lax.ppermute(body[tall - HALO :], "x", [(i, i + 1) for i in range(nx - 1)])
    below = lax.ppermute(body[:HALO], "x", [(i + 1, i) for i in range(nx - 1)])
    gathered = jnp.concatenate([above, body, below], axis=0)

    last = early[5, :, LAST : LAST + 3 * LAST_STEP].astype(F32).reshape(nz, width, 3, ny, 2)
    last = (last[:, :, 0] + last[:, :, 1] + last[:, :, 2]).transpose(3, 0, 2, 1).reshape(2, nz, lanes)

    j = lax.broadcasted_iota(jnp.int32, (half, own), 0)
    k = lax.broadcasted_iota(jnp.int32, (half, own), 1)
    pull = (j == (k // width) * lanes + width * y + k % width).astype(BF16)
    stream = jnp.dot(gathered.reshape(-1, half), pull, preferred_element_type=F32).astype(BF16)
    lean = patch + LEFT
    margin = (frame - lean) // 2
    stream = stream.reshape(tall + 2 * HALO, frame, own)[1:-1, margin : margin + lean].reshape(-1, own)
    for b in range(blocks):
        high = tall + 2 * (HALO - b)
        left = LEFT if b == 0 else LEFT - margin
        at = jnp.stack([c, tall * x - (HALO - b), patch * (z % across) - left])
        if b:
            gathered = lax.all_gather(stream, "y", axis=1, tiled=True)
            part = dot_nt(gathered, early[2 * b])
            other = pick(c, part[:, own:], part[:, :own]).astype(BF16)
            stream = stream[lean:-lean]
        else:
            part, other, table = multiply_first(at, gathered.reshape(-1, half), early, own)
            early, other = lax.optimization_barrier((early, other))
        high -= 2
        trim = (margin, margin + lean) if b == 0 else (left, left + patch) if b == blocks - 1 else None
        got = lax.all_gather(other, "c", axis=0)
        middle, after = convolve(b, high, lean if b else frame, width, trim, side, at, part, got, table)
        if b < blocks - 1:
            middle = lax.all_gather(middle, "y", axis=1, tiled=True)
            mine, got = halves(dot_nt(middle, early[2 * b + 1]), c)
            second = mine + pick(c, got[1], got[0]).astype(F32)
            stream = jnp.maximum(after[0] * second + after[1] + stream.astype(F32), 0.0).astype(BF16)

    deep = rows * nc
    spots_of_chip = deep * patch
    middle = lax.all_to_all(middle.reshape(ny, spots_of_chip, own), "y", 0, 0, tiled=True)
    t = lax.broadcasted_iota(jnp.int32, (spots_of_chip, gathered.shape[0]), 0)
    j = lax.broadcasted_iota(jnp.int32, (spots_of_chip, gathered.shape[0]), 1)
    of_chip = (j == (1 + deep * y + t // patch) * lean + LEFT - margin + t % patch).astype(BF16)
    kept = jnp.dot(of_chip, gathered, preferred_element_type=F32).astype(BF16)
    j = lax.broadcasted_iota(jnp.int32, (half, half), 0)
    k = lax.broadcasted_iota(jnp.int32, (half, half), 1)
    natural = (j == (k // width % ny) * own + k // lanes * width + k % width).astype(BF16)
    kept = jnp.dot(kept, natural, preferred_element_type=F32).astype(BF16)
    second, send = multiply_last(at, middle, final, kept)
    got = swap_core(send, c)
    kept = kept.reshape(nc, rows * patch, half)
    mine, theirs = pick(c, kept[0], kept[1]), got[:, nz * lanes :]
    residual = jnp.concatenate([pick(c, mine, theirs), pick(c, theirs, mine)], axis=1)
    second = second + got[:, : nz * lanes].astype(F32)
    gain, bias = last.reshape(2, 1, nz * lanes)
    out = jnp.maximum(gain * second + bias + residual.astype(F32), 0.0).astype(BF16)
    out = out.reshape(rows * patch, nz, lanes)
    out = out.transpose(1, 0, 2).reshape(nz, rows, patch, lanes)
    out = lax.all_to_all(out, "z", 0, 0, tiled=True).reshape(tiles, across, rows, patch, lanes)
    return out.transpose(0, 2, 1, 3, 4).reshape(tiles, rows, side, lanes)


def solution(mesh):
    grid = Mesh(mesh.devices.reshape(4, 4, 2, 16), ("x", "y", "c", "z"))
    placed = (
        P(None, SEG, None, "z"),
        P(None, None, "z"),
        P(None, None, None, "z"),
        P(None, None, "z"),
        P(None, None, "z"),
        P(None, None, "z"),
    )
    return jax.shard_map(local, mesh=grid, in_specs=placed, out_specs=P(None, SEG, None, "z"), check_vma=False)
```

```python
import functools

import jax
import jax.numpy as jnp
from jax import lax
from jax.experimental import pallas as pl
from jax.experimental.pallas import tpu as pltpu
from jax.sharding import Mesh
from jax.sharding import PartitionSpec as P

BF16 = jnp.bfloat16
F32 = jnp.float32
SEG = ("x", "y", "c")
LEFT = 4
HALO = 3


def dot_nt(a, b):
    return lax.dot_general(a, b, (((1,), (1,)), ((), ())), preferred_element_type=F32)


def selector(rows, cols, base):
    i = lax.broadcasted_iota(jnp.int32, (rows, cols), 0)
    j = lax.broadcasted_iota(jnp.int32, (rows, cols), 1)
    return (j == i + base).astype(BF16)


def terms(v):
    out = []
    for _ in range(3):
        t = v.astype(BF16).astype(F32)
        out.append(t)
        v = v - t
    return out


def pick(c, a, b):
    return jnp.where(c == 0, a, b)


def swap_core(v, c):
    both = lax.all_gather(v, "c", axis=0)
    return pick(c, both[1], both[0])


SPOTS = (0, 320, 640)
OWNED, OWNED_STEP = 928, 24
LAST, LAST_STEP = 1000, 8
VMEM_LIMIT = 12 * 1024 * 1024
FIRST_LIMIT = 50 * 1024 * 1024


def prep_kernel(
    wr_hbm, we_hbm, wg_hbm, gains_hbm, biases_hbm, out_hbm,
    wr_ref, we_ref, wg_ref, gains_ref, biases_ref, table, out_ref, sems, out_sems,
):
    y, c = lax.axis_index("y"), lax.axis_index("c")
    width, half = out_ref.shape[1:]
    lanes = wr_ref.shape[2]
    ny = lanes // width
    zhalf = half // lanes
    rows = pl.ds(pl.multiple_of(half * c, half), half)
    small = [
        pltpu.make_async_copy(gains_hbm, gains_ref, sems.at[6]),
        pltpu.make_async_copy(biases_hbm, biases_ref, sems.at[7]),
    ]
    copies = [pltpu.make_async_copy(wg_hbm, wg_ref, sems.at[0])]
    for b in range(3):
        copies.append(pltpu.make_async_copy(wr_hbm.at[b, rows], wr_ref.at[b], sems.at[1 + b]))
    for b in range(2):
        copies.append(pltpu.make_async_copy(we_hbm.at[b, rows], we_ref.at[b], sems.at[4 + b]))
    for copy in small + copies:
        copy.start()

    def done(slot):
        copy = pltpu.make_async_copy(out_ref.at[slot], out_hbm.at[slot], out_sems.at[slot])
        copy.start()
        return copy

    sel = selector(width, lanes, width * y)

    table[...] = jnp.zeros_like(table)
    for copy in small:
        copy.wait()
    for which, ref in enumerate((gains_ref, biases_ref)):
        for b in range(3):
            for t, v in enumerate(terms(ref[b])):
                spot = OWNED + OWNED_STEP * t + 3 * (3 * which + b)
                table[spot : spot + 3] = v
                if b == 2:
                    for g in range(ny):
                        spot = LAST + LAST_STEP * t + 2 * g + which
                        table[spot : spot + 1] = v[2:3]
    copies[0].wait()
    for b, spot in enumerate(SPOTS):
        table[spot : spot + wg_ref.shape[1]] = wg_ref[b].astype(F32)
    row = lax.broadcasted_iota(jnp.int32, table.shape, 0)
    lane = lax.broadcasted_iota(jnp.int32, table.shape, 1)
    wanted = jnp.where(row < LAST, y, ((row - LAST) & (LAST_STEP - 1)) >> 1)
    kept = jnp.where((lane >> 5) == wanted, table[...], 0.0).astype(BF16)
    i = lax.broadcasted_iota(jnp.int32, (width, lanes), 0)
    j = lax.broadcasted_iota(jnp.int32, (width, lanes), 1)
    out_ref[5] = dot_nt(((j & (width - 1)) == i).astype(BF16), kept).astype(BF16)
    outs = [done(5)]

    def put(slot, w):
        w = w.reshape(zhalf, ny, width, lanes)
        for g in range(ny):
            rows = w[:, g].reshape(zhalf * width, lanes)
            out_ref[slot, :, g * zhalf * width : (g + 1) * zhalf * width] = dot_nt(sel, rows).astype(BF16)

    copies[1].wait()
    out_ref[0] = dot_nt(sel, wr_ref[0]).astype(BF16)
    outs.append(done(0))
    for copy, slot, ref in ((2, 2, wr_ref.at[1]), (3, 4, wr_ref.at[2]), (4, 1, we_ref.at[0]), (5, 3, we_ref.at[1])):
        copies[copy].wait()
        put(slot, ref[...])
        outs.append(done(slot))
    for copy in outs:
        copy.wait()


def prepare(w_reduce, w_expand, w_group, gains, biases):
    blocks, depth, lanes = w_reduce.shape
    width = w_group.shape[2]
    half = depth // 2
    there = pl.BlockSpec(memory_space=pl.ANY)
    return pl.pallas_call(
        prep_kernel,
        out_shape=jax.ShapeDtypeStruct((6, width, half), BF16),
        in_specs=[there] * 5,
        out_specs=there,
        scratch_shapes=[
            pltpu.VMEM((3, half, lanes), BF16),
            pltpu.VMEM((2, half, lanes), BF16),
            pltpu.VMEM((blocks, 9 * width, lanes), BF16),
            pltpu.VMEM(gains.shape, F32),
            pltpu.VMEM(biases.shape, F32),
            pltpu.VMEM((half, lanes), F32),
            pltpu.VMEM((6, width, half), BF16),
            pltpu.SemaphoreType.DMA((8,)),
            pltpu.SemaphoreType.DMA((6,)),
        ],
        compiler_params=pltpu.CompilerParams(vmem_limit_bytes=60 * 1024 * 1024),
        cost_estimate=pl.CostEstimate(flops=2 * 6 * half * lanes * width, bytes_accessed=2_500_000, transcendentals=0),
    )(w_reduce, w_expand, w_group.reshape(blocks, -1, lanes), gains, biases)


def conv_kernel(b, high, frame, width, trim, side, at, part_ref, got_ref, table_ref, out_ref, after_ref, sums):
    c, row0, col0 = at[0], at[1], at[2]
    count, own = got_ref.shape[1:]
    i = lax.broadcasted_iota(jnp.int32, (own, own), 0)
    j = lax.broadcasted_iota(jnp.int32, (own, own), 1)
    eye = (i == j).astype(BF16)

    def columns(start, count):
        some = table_ref[:, start : start + count]
        return lax.dot_general(some, eye, (((0,), (0,)), ((), ())), preferred_element_type=F32)

    rows = columns(OWNED // 128 * 128, 128)

    def param(which, k):
        at_row = OWNED % 128 + (which * 3 + b) * 3 + k
        return sum(rows[at_row + OWNED_STEP * t : at_row + OWNED_STEP * t + 1] for t in range(3))

    if part_ref.shape[1] == own:
        mine = part_ref[...]
    else:
        mine = part_ref[:, pl.ds(pl.multiple_of(own * c, own), own)]
    hidden = jnp.maximum(param(0, 0) * (mine + got_ref[1 - c].astype(F32)) + param(1, 0), 0.0)
    spot = lax.broadcasted_iota(jnp.int32, hidden.shape, 0)
    row = ((spot.astype(F32) + 0.5) * (1.0 / frame)).astype(jnp.int32)
    col = col0 + spot - row * frame
    row = row0 + row
    inside = (row >= 0) & (row < side) & (col >= 0) & (col < side)
    hidden = jnp.where(inside, hidden, 0.0)
    spread = (
        (lax.broadcasted_iota(jnp.int32, (own, width), 0) & (width - 1))
        == lax.broadcasted_iota(jnp.int32, (own, width), 1)
    ).astype(BF16)
    same = (i >> 5) == (j >> 5)
    base = SPOTS[b] // 128 * 128
    filters = columns(base, 384).astype(BF16)
    fit = high * frame
    shifted = jnp.concatenate([hidden[frame * r : frame * r + fit].astype(BF16) for r in range(3)], axis=1)
    terms_of = []
    for s in range(3):
        taps = []
        for r in range(3):
            spot = SPOTS[b] - base + (3 * r + s) * width
            tap = jnp.dot(spread, filters[spot : spot + width], preferred_element_type=F32)
            taps.append(jnp.where(same, tap, 0.0).astype(BF16))
        terms_of.append(jnp.dot(shifted, jnp.concatenate(taps, axis=0), preferred_element_type=F32))
    spatial = pltpu.roll(terms_of[0], 1, 0) + terms_of[1] + pltpu.roll(terms_of[2], fit - 1, 0)
    middle = jnp.maximum(param(0, 1) * spatial + param(1, 1), 0.0)
    if trim:
        lo, hi = trim
        for r in range(high):
            sums[r * (hi - lo) : (r + 1) * (hi - lo)] = middle[r * frame + lo : r * frame + hi]
        middle = sums[...]
    out_ref[...] = middle.astype(BF16)
    after_ref[0:1] = param(0, 2)
    after_ref[1:2] = param(1, 2)


ON_CHIP = pl.BlockSpec(memory_space=pltpu.VMEM)
SCALARS = pl.BlockSpec(memory_space=pltpu.SMEM)


def convolve(b, high, frame, width, trim, side, at, part, got, table):
    own = got.shape[2]
    cols = trim[1] - trim[0] if trim else frame
    return pl.pallas_call(
        functools.partial(conv_kernel, b, high, frame, width, trim, side),
        out_shape=(jax.ShapeDtypeStruct((high * cols, own), BF16), jax.ShapeDtypeStruct((8, own), F32)),
        in_specs=[SCALARS, ON_CHIP, ON_CHIP, ON_CHIP],
        out_specs=(ON_CHIP, ON_CHIP),
        scratch_shapes=[pltpu.VMEM((high * cols, own), F32)],
        compiler_params=pltpu.CompilerParams(vmem_limit_bytes=VMEM_LIMIT),
        cost_estimate=pl.CostEstimate(flops=18 * high * frame * own * own, bytes_accessed=2_500_000, transcendentals=0),
    )(at, part, got, table)


def first_kernel(at, x_ref, early_hbm, mine_ref, other_ref, table_ref, w_ref, sems):
    c = at[0]
    own = mine_ref.shape[1]
    part = own // 2
    copies = []
    for h, start in enumerate((own * (1 - c), own * c)):
        for p in range(2):
            rows = pl.ds(pl.multiple_of(start + p * part, part), part)
            spots = pl.ds(p * part, part)
            copies.append(pltpu.make_async_copy(early_hbm.at[0, rows], w_ref.at[h, spots], sems.at[2 * h + p]))
    mine = pl.ds(pl.multiple_of(own * c, own), own)
    copies.append(pltpu.make_async_copy(early_hbm.at[5, mine], table_ref, sems.at[4]))
    for copy in copies:
        copy.start()
    for h, ref in enumerate((other_ref, mine_ref)):
        for p in range(2):
            copies[2 * h + p].wait()
            spots = slice(p * part, (p + 1) * part)
            ref[:, spots] = dot_nt(x_ref[...], w_ref[h, spots]).astype(ref.dtype)
    copies[4].wait()


def multiply_first(at, x, early, own):
    count, half = x.shape
    return pl.pallas_call(
        first_kernel,
        out_shape=(
            jax.ShapeDtypeStruct((count, own), F32),
            jax.ShapeDtypeStruct((count, own), BF16),
            jax.ShapeDtypeStruct((own, half), BF16),
        ),
        in_specs=[SCALARS, ON_CHIP, pl.BlockSpec(memory_space=pl.ANY)],
        out_specs=(ON_CHIP, ON_CHIP, ON_CHIP),
        scratch_shapes=[pltpu.VMEM((2, own, half), BF16), pltpu.SemaphoreType.DMA((5,))],
        compiler_params=pltpu.CompilerParams(vmem_limit_bytes=FIRST_LIMIT),
        cost_estimate=pl.CostEstimate(flops=4 * count * half * own, bytes_accessed=4_000_000, transcendentals=0),
    )(at, x, early)


PIECES = 4


def last_kernel(at, middle_ref, w_hbm, kept_ref, mine_ref, send_ref, sums, w_ref, sems):
    c = at[0]
    many, half, lanes = w_ref.shape
    each = many // PIECES
    copies = [
        pltpu.make_async_copy(w_hbm.at[pl.ds(p * each, each)], w_ref.at[pl.ds(p * each, each)], sems.at[p])
        for p in range(PIECES)
    ]
    for copy in copies:
        copy.start()
    middle = jnp.concatenate([middle_ref[g] for g in range(middle_ref.shape[0])], axis=1)
    for k in range(many):
        if k % each == 0:
            copies[k // each].wait()
        sums[:, k * lanes : (k + 1) * lanes] = jnp.dot(middle, w_ref[k], preferred_element_type=F32)
    rows = mine_ref.shape[0]
    mine = pl.ds(pl.multiple_of(rows * c, rows), rows)
    other = pl.ds(pl.multiple_of(rows * (1 - c), rows), rows)
    mine_ref[...] = sums[mine]
    send_ref[:, : many * lanes] = sums[other].astype(BF16)
    send_ref[:, many * lanes :] = kept_ref[other]


def multiply_last(at, middle, w, kept):
    many, half, lanes = w.shape
    rows = kept.shape[0]
    return pl.pallas_call(
        last_kernel,
        out_shape=(
            jax.ShapeDtypeStruct((rows // 2, many * lanes), F32),
            jax.ShapeDtypeStruct((rows // 2, many * lanes + half), BF16),
        ),
        in_specs=[SCALARS, ON_CHIP, pl.BlockSpec(memory_space=pl.ANY), ON_CHIP],
        out_specs=(ON_CHIP, ON_CHIP),
        scratch_shapes=[
            pltpu.VMEM((rows, many * lanes), F32),
            pltpu.VMEM(w.shape, BF16),
            pltpu.SemaphoreType.DMA((PIECES,)),
        ],
        compiler_params=pltpu.CompilerParams(vmem_limit_bytes=50 * 1024 * 1024),
        cost_estimate=pl.CostEstimate(flops=2 * rows * half * many * lanes, bytes_accessed=5_000_000, transcendentals=0),
    )(at, middle, w, kept)


def halves(part, c):
    half = part.shape[1] // 2
    mine, other = pick(c, part[:, :half], part[:, half:]), pick(c, part[:, half:], part[:, :half])
    return mine, lax.all_gather(other.astype(BF16), "c", axis=0)


def local(planes, w_reduce, w_group, w_expand, gains, biases):
    nx, ny, nc, nz = (lax.axis_size(a) for a in ("x", "y", "c", "z"))
    x, y, c, z = (lax.axis_index(a) for a in ("x", "y", "c", "z"))
    tiles, rows, side, lanes = planes.shape
    blocks, _, width, _ = w_group.shape
    channels = lanes * nz
    half = channels // nc
    zhalf = nz // nc
    own = zhalf * width
    across = nz // tiles
    patch = side // across
    tall = rows * ny * nc
    frame = patch + 2 * LEFT

    early = lax.all_gather(prepare(w_reduce, w_expand, w_group, gains, biases), "z", axis=1, tiled=True)
    final = lax.dynamic_slice_in_dim(w_expand[2], half * c, half, axis=0)
    final = final.reshape(zhalf, ny, width, lanes).transpose(1, 0, 2, 3).reshape(half, lanes)
    final = lax.all_gather(final, "z", axis=0)

    wide = jnp.pad(planes, ((0, 0), (0, 0), (LEFT, LEFT), (0, 0)))
    strips = jnp.stack([wide[:, :, patch * q : patch * q + frame] for q in range(across)], axis=1)
    strips = strips.reshape(nz, rows, frame, lanes)
    mixed = lax.all_to_all(strips, "z", 0, 0, tiled=True)
    mine = pick(c, mixed[:zhalf], mixed[zhalf:])
    theirs = swap_core(pick(c, mixed[zhalf:], mixed[:zhalf]), c)
    chip = jnp.concatenate([pick(c, mine, theirs), pick(c, theirs, mine)], axis=1)
    chip = chip.transpose(1, 2, 0, 3).reshape(rows * nc, frame, half)
    body = lax.all_gather(chip, "y", axis=0, tiled=True)
    above = lax.ppermute(body[tall - HALO :], "x", [(i, i + 1) for i in range(nx - 1)])
    below = lax.ppermute(body[:HALO], "x", [(i + 1, i) for i in range(nx - 1)])
    gathered = jnp.concatenate([above, body, below], axis=0)

    last = early[5, :, LAST : LAST + 3 * LAST_STEP].astype(F32).reshape(nz, width, 3, ny, 2)
    last = (last[:, :, 0] + last[:, :, 1] + last[:, :, 2]).transpose(3, 0, 2, 1).reshape(2, nz, lanes)

    j = lax.broadcasted_iota(jnp.int32, (half, own), 0)
    k = lax.broadcasted_iota(jnp.int32, (half, own), 1)
    pull = (j == (k // width) * lanes + width * y + k % width).astype(BF16)
    stream = jnp.dot(gathered.reshape(-1, half), pull, preferred_element_type=F32).astype(BF16)
    lean = patch + LEFT
    margin = (frame - lean) // 2
    stream = stream.reshape(tall + 2 * HALO, frame, own)[1:-1, margin : margin + lean].reshape(-1, own)
    for b in range(blocks):
        high = tall + 2 * (HALO - b)
        left = LEFT if b == 0 else LEFT - margin
        at = jnp.stack([c, tall * x - (HALO - b), patch * (z % across) - left])
        if b:
            gathered = lax.all_gather(stream, "y", axis=1, tiled=True)
            part = dot_nt(gathered, early[2 * b])
            other = pick(c, part[:, own:], part[:, :own]).astype(BF16)
            stream = stream[lean:-lean]
        else:
            part, other, table = multiply_first(at, gathered.reshape(-1, half), early, own)
            early, other = lax.optimization_barrier((early, other))
        high -= 2
        trim = (margin, margin + lean) if b == 0 else (left, left + patch) if b == blocks - 1 else None
        got = lax.all_gather(other, "c", axis=0)
        middle, after = convolve(b, high, lean if b else frame, width, trim, side, at, part, got, table)
        if b < blocks - 1:
            middle = lax.all_gather(middle, "y", axis=1, tiled=True)
            mine, got = halves(dot_nt(middle, early[2 * b + 1]), c)
            second = mine + pick(c, got[1], got[0]).astype(F32)
            stream = jnp.maximum(after[0] * second + after[1] + stream.astype(F32), 0.0).astype(BF16)

    deep = rows * nc
    spots_of_chip = deep * patch
    middle = lax.all_to_all(middle.reshape(ny, spots_of_chip, own), "y", 0, 0, tiled=True)
    t = lax.broadcasted_iota(jnp.int32, (spots_of_chip, gathered.shape[0]), 0)
    j = lax.broadcasted_iota(jnp.int32, (spots_of_chip, gathered.shape[0]), 1)
    of_chip = (j == (1 + deep * y + t // patch) * lean + LEFT - margin + t % patch).astype(BF16)
    kept = jnp.dot(of_chip, gathered, preferred_element_type=F32).astype(BF16)
    j = lax.broadcasted_iota(jnp.int32, (half, half), 0)
    k = lax.broadcasted_iota(jnp.int32, (half, half), 1)
    natural = (j == (k // width % ny) * own + k // lanes * width + k % width).astype(BF16)
    kept = jnp.dot(kept, natural, preferred_element_type=F32).astype(BF16)
    second, send = multiply_last(at, middle, final, kept)
    got = swap_core(send, c)
    kept = kept.reshape(nc, rows * patch, half)
    mine, theirs = pick(c, kept[0], kept[1]), got[:, nz * lanes :]
    residual = jnp.concatenate([pick(c, mine, theirs), pick(c, theirs, mine)], axis=1)
    second = second + got[:, : nz * lanes].astype(F32)
    gain, bias = last.reshape(2, 1, nz * lanes)
    out = jnp.maximum(gain * second + bias + residual.astype(F32), 0.0).astype(BF16)
    out = out.reshape(rows * patch, nz, lanes)
    out = out.transpose(1, 0, 2).reshape(nz, rows, patch, lanes)
    out = lax.all_to_all(out, "z", 0, 0, tiled=True).reshape(tiles, across, rows, patch, lanes)
    return out.transpose(0, 2, 1, 3, 4).reshape(tiles, rows, side, lanes)


def solution(mesh):
    grid = Mesh(mesh.devices.reshape(4, 4, 2, 16), ("x", "y", "c", "z"))
    placed = (
        P(None, SEG, None, "z"),
        P(None, None, "z"),
        P(None, None, None, "z"),
        P(None, None, "z"),
        P(None, None, "z"),
        P(None, None, "z"),
    )
    return jax.shard_map(local, mesh=grid, in_specs=placed, out_specs=P(None, SEG, None, "z"), check_vma=False)
```

```python
import functools

import jax
import jax.numpy as jnp
from jax import lax
from jax.experimental import pallas as pl
from jax.experimental.pallas import tpu as pltpu
from jax.sharding import Mesh
from jax.sharding import PartitionSpec as P

BF16 = jnp.bfloat16
F32 = jnp.float32
SEG = ("x", "y", "c")
LEFT = 4
HALO = 3


def dot_nt(a, b):
    return lax.dot_general(a, b, (((1,), (1,)), ((), ())), preferred_element_type=F32)


def selector(rows, cols, base):
    i = lax.broadcasted_iota(jnp.int32, (rows, cols), 0)
    j = lax.broadcasted_iota(jnp.int32, (rows, cols), 1)
    return (j == i + base).astype(BF16)


def terms(v):
    out = []
    for _ in range(3):
        t = v.astype(BF16).astype(F32)
        out.append(t)
        v = v - t
    return out


def pick(c, a, b):
    return jnp.where(c == 0, a, b)


def swap_core(v, c):
    both = lax.all_gather(v, "c", axis=0)
    return pick(c, both[1], both[0])


SPOTS = (0, 320, 640)
OWNED, OWNED_STEP = 928, 24
LAST, LAST_STEP = 1000, 8
VMEM_LIMIT = 12 * 1024 * 1024
FIRST_LIMIT = 50 * 1024 * 1024


def prep_kernel(
    wr_hbm, we_hbm, wg_hbm, gains_hbm, biases_hbm, out_hbm,
    wr_ref, we_ref, wg_ref, gains_ref, biases_ref, table, out_ref, sems, out_sems,
):
    y, c = lax.axis_index("y"), lax.axis_index("c")
    width, half = out_ref.shape[1:]
    lanes = wr_ref.shape[2]
    ny = lanes // width
    zhalf = half // lanes
    rows = pl.ds(pl.multiple_of(half * c, half), half)
    small = [
        pltpu.make_async_copy(gains_hbm, gains_ref, sems.at[6]),
        pltpu.make_async_copy(biases_hbm, biases_ref, sems.at[7]),
    ]
    copies = [pltpu.make_async_copy(wg_hbm, wg_ref, sems.at[0])]
    for b in range(3):
        copies.append(pltpu.make_async_copy(wr_hbm.at[b, rows], wr_ref.at[b], sems.at[1 + b]))
    for b in range(2):
        copies.append(pltpu.make_async_copy(we_hbm.at[b, rows], we_ref.at[b], sems.at[4 + b]))
    for copy in small + copies:
        copy.start()

    def done(slot):
        copy = pltpu.make_async_copy(out_ref.at[slot], out_hbm.at[slot], out_sems.at[slot])
        copy.start()
        return copy

    sel = selector(width, lanes, width * y)

    table[...] = jnp.zeros_like(table)
    for copy in small:
        copy.wait()
    for which, ref in enumerate((gains_ref, biases_ref)):
        for b in range(3):
            for t, v in enumerate(terms(ref[b])):
                spot = OWNED + OWNED_STEP * t + 3 * (3 * which + b)
                table[spot : spot + 3] = v
                if b == 2:
                    for g in range(ny):
                        spot = LAST + LAST_STEP * t + 2 * g + which
                        table[spot : spot + 1] = v[2:3]
    copies[0].wait()
    for b, spot in enumerate(SPOTS):
        table[spot : spot + wg_ref.shape[1]] = wg_ref[b].astype(F32)
    row = lax.broadcasted_iota(jnp.int32, table.shape, 0)
    lane = lax.broadcasted_iota(jnp.int32, table.shape, 1)
    wanted = jnp.where(row < LAST, y, ((row - LAST) & (LAST_STEP - 1)) >> 1)
    kept = jnp.where((lane >> 5) == wanted, table[...], 0.0).astype(BF16)
    i = lax.broadcasted_iota(jnp.int32, (width, lanes), 0)
    j = lax.broadcasted_iota(jnp.int32, (width, lanes), 1)
    out_ref[5] = dot_nt(((j & (width - 1)) == i).astype(BF16), kept).astype(BF16)
    outs = [done(5)]

    def put(slot, w):
        w = w.reshape(zhalf, ny, width, lanes)
        for g in range(ny):
            rows = w[:, g].reshape(zhalf * width, lanes)
            out_ref[slot, :, g * zhalf * width : (g + 1) * zhalf * width] = dot_nt(sel, rows).astype(BF16)

    copies[1].wait()
    out_ref[0] = dot_nt(sel, wr_ref[0]).astype(BF16)
    outs.append(done(0))
    for copy, slot, ref in ((2, 2, wr_ref.at[1]), (3, 4, wr_ref.at[2]), (4, 1, we_ref.at[0]), (5, 3, we_ref.at[1])):
        copies[copy].wait()
        put(slot, ref[...])
        outs.append(done(slot))
    for copy in outs:
        copy.wait()


def prepare(w_reduce, w_expand, w_group, gains, biases):
    blocks, depth, lanes = w_reduce.shape
    width = w_group.shape[2]
    half = depth // 2
    there = pl.BlockSpec(memory_space=pl.ANY)
    return pl.pallas_call(
        prep_kernel,
        out_shape=jax.ShapeDtypeStruct((6, width, half), BF16),
        in_specs=[there] * 5,
        out_specs=there,
        scratch_shapes=[
            pltpu.VMEM((3, half, lanes), BF16),
            pltpu.VMEM((2, half, lanes), BF16),
            pltpu.VMEM((blocks, 9 * width, lanes), BF16),
            pltpu.VMEM(gains.shape, F32),
            pltpu.VMEM(biases.shape, F32),
            pltpu.VMEM((half, lanes), F32),
            pltpu.VMEM((6, width, half), BF16),
            pltpu.SemaphoreType.DMA((8,)),
            pltpu.SemaphoreType.DMA((6,)),
        ],
        compiler_params=pltpu.CompilerParams(vmem_limit_bytes=60 * 1024 * 1024),
        cost_estimate=pl.CostEstimate(flops=2 * 6 * half * lanes * width, bytes_accessed=2_500_000, transcendentals=0),
    )(w_reduce, w_expand, w_group.reshape(blocks, -1, lanes), gains, biases)


def conv_kernel(b, high, frame, width, trim, side, at, part_ref, got_ref, table_ref, out_ref, after_ref, sums):
    c, row0, col0 = at[0], at[1], at[2]
    count, own = got_ref.shape[1:]
    i = lax.broadcasted_iota(jnp.int32, (own, own), 0)
    j = lax.broadcasted_iota(jnp.int32, (own, own), 1)
    eye = (i == j).astype(BF16)

    def columns(start, count):
        some = table_ref[:, start : start + count]
        return lax.dot_general(some, eye, (((0,), (0,)), ((), ())), preferred_element_type=F32)

    rows = columns(OWNED // 128 * 128, 128)

    def param(which, k):
        at_row = OWNED % 128 + (which * 3 + b) * 3 + k
        return sum(rows[at_row + OWNED_STEP * t : at_row + OWNED_STEP * t + 1] for t in range(3))

    if part_ref.shape[1] == own:
        mine = part_ref[...]
    else:
        mine = part_ref[:, pl.ds(pl.multiple_of(own * c, own), own)]
    hidden = jnp.maximum(param(0, 0) * (mine + got_ref[1 - c].astype(F32)) + param(1, 0), 0.0)
    spot = lax.broadcasted_iota(jnp.int32, hidden.shape, 0)
    row = ((spot.astype(F32) + 0.5) * (1.0 / frame)).astype(jnp.int32)
    col = col0 + spot - row * frame
    row = row0 + row
    inside = (row >= 0) & (row < side) & (col >= 0) & (col < side)
    hidden = jnp.where(inside, hidden, 0.0)
    spread = (
        (lax.broadcasted_iota(jnp.int32, (own, width), 0) & (width - 1))
        == lax.broadcasted_iota(jnp.int32, (own, width), 1)
    ).astype(BF16)
    same = (i >> 5) == (j >> 5)
    base = SPOTS[b] // 128 * 128
    filters = columns(base, 384).astype(BF16)
    fit = high * frame
    shifted = jnp.concatenate([hidden[frame * r : frame * r + fit].astype(BF16) for r in range(3)], axis=1)
    terms_of = []
    for s in range(3):
        taps = []
        for r in range(3):
            spot = SPOTS[b] - base + (3 * r + s) * width
            tap = jnp.dot(spread, filters[spot : spot + width], preferred_element_type=F32)
            taps.append(jnp.where(same, tap, 0.0).astype(BF16))
        terms_of.append(jnp.dot(shifted, jnp.concatenate(taps, axis=0), preferred_element_type=F32))
    spatial = pltpu.roll(terms_of[0], 1, 0) + terms_of[1] + pltpu.roll(terms_of[2], fit - 1, 0)
    middle = jnp.maximum(param(0, 1) * spatial + param(1, 1), 0.0)
    if trim:
        lo, hi = trim
        for r in range(high):
            sums[r * (hi - lo) : (r + 1) * (hi - lo)] = middle[r * frame + lo : r * frame + hi]
        middle = sums[...]
    out_ref[...] = middle.astype(BF16)
    after_ref[0:1] = param(0, 2)
    after_ref[1:2] = param(1, 2)


ON_CHIP = pl.BlockSpec(memory_space=pltpu.VMEM)
SCALARS = pl.BlockSpec(memory_space=pltpu.SMEM)


def convolve(b, high, frame, width, trim, side, at, part, got, table):
    own = got.shape[2]
    cols = trim[1] - trim[0] if trim else frame
    return pl.pallas_call(
        functools.partial(conv_kernel, b, high, frame, width, trim, side),
        out_shape=(jax.ShapeDtypeStruct((high * cols, own), BF16), jax.ShapeDtypeStruct((8, own), F32)),
        in_specs=[SCALARS, ON_CHIP, ON_CHIP, ON_CHIP],
        out_specs=(ON_CHIP, ON_CHIP),
        scratch_shapes=[pltpu.VMEM((high * cols, own), F32)],
        compiler_params=pltpu.CompilerParams(vmem_limit_bytes=VMEM_LIMIT),
        cost_estimate=pl.CostEstimate(flops=18 * high * frame * own * own, bytes_accessed=2_500_000, transcendentals=0),
    )(at, part, got, table)


def first_kernel(at, x_ref, early_hbm, mine_ref, other_ref, table_ref, w_ref, sems):
    c = at[0]
    own = mine_ref.shape[1]
    mine = pl.ds(pl.multiple_of(own * c, own), own)
    other = pl.ds(pl.multiple_of(own * (1 - c), own), own)
    copies = [
        pltpu.make_async_copy(early_hbm.at[0, other], w_ref.at[0], sems.at[0]),
        pltpu.make_async_copy(early_hbm.at[0, mine], w_ref.at[1], sems.at[1]),
        pltpu.make_async_copy(early_hbm.at[5, mine], table_ref, sems.at[2]),
    ]
    for copy in copies:
        copy.start()
    copies[0].wait()
    other_ref[...] = dot_nt(x_ref[...], w_ref[0]).astype(BF16)
    copies[1].wait()
    mine_ref[...] = dot_nt(x_ref[...], w_ref[1])
    copies[2].wait()


def multiply_first(at, x, early, own):
    count, half = x.shape
    return pl.pallas_call(
        first_kernel,
        out_shape=(
            jax.ShapeDtypeStruct((count, own), F32),
            jax.ShapeDtypeStruct((count, own), BF16),
            jax.ShapeDtypeStruct((own, half), BF16),
        ),
        in_specs=[SCALARS, ON_CHIP, pl.BlockSpec(memory_space=pl.ANY)],
        out_specs=(ON_CHIP, ON_CHIP, ON_CHIP),
        scratch_shapes=[pltpu.VMEM((2, own, half), BF16), pltpu.SemaphoreType.DMA((3,))],
        compiler_params=pltpu.CompilerParams(vmem_limit_bytes=FIRST_LIMIT),
        cost_estimate=pl.CostEstimate(flops=4 * count * half * own, bytes_accessed=4_000_000, transcendentals=0),
    )(at, x, early)


PIECES = 2


def last_kernel(at, middle_ref, w_hbm, kept_ref, mine_ref, send_ref, sums, w_ref, sems):
    c = at[0]
    many, half, lanes = w_ref.shape
    each = many // PIECES
    copies = [
        pltpu.make_async_copy(w_hbm.at[pl.ds(p * each, each)], w_ref.at[pl.ds(p * each, each)], sems.at[p])
        for p in range(PIECES)
    ]
    for copy in copies:
        copy.start()
    middle = jnp.concatenate([middle_ref[g] for g in range(middle_ref.shape[0])], axis=1)
    for k in range(many):
        if k % each == 0:
            copies[k // each].wait()
        sums[:, k * lanes : (k + 1) * lanes] = jnp.dot(middle, w_ref[k], preferred_element_type=F32)
    rows = mine_ref.shape[0]
    mine = pl.ds(pl.multiple_of(rows * c, rows), rows)
    other = pl.ds(pl.multiple_of(rows * (1 - c), rows), rows)
    mine_ref[...] = sums[mine]
    send_ref[:, : many * lanes] = sums[other].astype(BF16)
    send_ref[:, many * lanes :] = kept_ref[other]


def multiply_last(at, middle, w, kept):
    many, half, lanes = w.shape
    rows = kept.shape[0]
    return pl.pallas_call(
        last_kernel,
        out_shape=(
            jax.ShapeDtypeStruct((rows // 2, many * lanes), F32),
            jax.ShapeDtypeStruct((rows // 2, many * lanes + half), BF16),
        ),
        in_specs=[SCALARS, ON_CHIP, pl.BlockSpec(memory_space=pl.ANY), ON_CHIP],
        out_specs=(ON_CHIP, ON_CHIP),
        scratch_shapes=[
            pltpu.VMEM((rows, many * lanes), F32),
            pltpu.VMEM(w.shape, BF16),
            pltpu.SemaphoreType.DMA((PIECES,)),
        ],
        compiler_params=pltpu.CompilerParams(vmem_limit_bytes=50 * 1024 * 1024),
        cost_estimate=pl.CostEstimate(flops=2 * rows * half * many * lanes, bytes_accessed=5_000_000, transcendentals=0),
    )(at, middle, w, kept)


def halves(part, c):
    half = part.shape[1] // 2
    mine, other = pick(c, part[:, :half], part[:, half:]), pick(c, part[:, half:], part[:, :half])
    return mine, lax.all_gather(other.astype(BF16), "c", axis=0)


def local(planes, w_reduce, w_group, w_expand, gains, biases):
    nx, ny, nc, nz = (lax.axis_size(a) for a in ("x", "y", "c", "z"))
    x, y, c, z = (lax.axis_index(a) for a in ("x", "y", "c", "z"))
    tiles, rows, side, lanes = planes.shape
    blocks, _, width, _ = w_group.shape
    channels = lanes * nz
    half = channels // nc
    zhalf = nz // nc
    own = zhalf * width
    across = nz // tiles
    patch = side // across
    tall = rows * ny * nc
    frame = patch + 2 * LEFT

    early = lax.all_gather(prepare(w_reduce, w_expand, w_group, gains, biases), "z", axis=1, tiled=True)
    final = lax.dynamic_slice_in_dim(w_expand[2], half * c, half, axis=0)
    final = final.reshape(zhalf, ny, width, lanes).transpose(1, 0, 2, 3).reshape(half, lanes)
    final = lax.all_gather(final, "z", axis=0)

    wide = jnp.pad(planes, ((0, 0), (0, 0), (LEFT, LEFT), (0, 0)))
    strips = jnp.stack([wide[:, :, patch * q : patch * q + frame] for q in range(across)], axis=1)
    strips = strips.reshape(nz, rows, frame, lanes)
    mixed = lax.all_to_all(strips, "z", 0, 0, tiled=True)
    mine = pick(c, mixed[:zhalf], mixed[zhalf:])
    theirs = swap_core(pick(c, mixed[zhalf:], mixed[:zhalf]), c)
    chip = jnp.concatenate([pick(c, mine, theirs), pick(c, theirs, mine)], axis=1)
    chip = chip.transpose(1, 2, 0, 3).reshape(rows * nc, frame, half)
    body = lax.all_gather(chip, "y", axis=0, tiled=True)
    above = lax.ppermute(body[tall - HALO :], "x", [(i, i + 1) for i in range(nx - 1)])
    below = lax.ppermute(body[:HALO], "x", [(i + 1, i) for i in range(nx - 1)])
    gathered = jnp.concatenate([above, body, below], axis=0)

    last = early[5, :, LAST : LAST + 3 * LAST_STEP].astype(F32).reshape(nz, width, 3, ny, 2)
    last = (last[:, :, 0] + last[:, :, 1] + last[:, :, 2]).transpose(3, 0, 2, 1).reshape(2, nz, lanes)

    j = lax.broadcasted_iota(jnp.int32, (half, own), 0)
    k = lax.broadcasted_iota(jnp.int32, (half, own), 1)
    pull = (j == (k // width) * lanes + width * y + k % width).astype(BF16)
    stream = jnp.dot(gathered.reshape(-1, half), pull, preferred_element_type=F32).astype(BF16)
    lean = patch + LEFT
    margin = (frame - lean) // 2
    stream = stream.reshape(tall + 2 * HALO, frame, own)[1:-1, margin : margin + lean].reshape(-1, own)
    for b in range(blocks):
        high = tall + 2 * (HALO - b)
        left = LEFT if b == 0 else LEFT - margin
        at = jnp.stack([c, tall * x - (HALO - b), patch * (z % across) - left])
        if b:
            gathered = lax.all_gather(stream, "y", axis=1, tiled=True)
            part = dot_nt(gathered, early[2 * b])
            other = pick(c, part[:, own:], part[:, :own]).astype(BF16)
            stream = stream[lean:-lean]
        else:
            part, other, table = multiply_first(at, gathered.reshape(-1, half), early, own)
            early, other = lax.optimization_barrier((early, other))
        high -= 2
        trim = (margin, margin + lean) if b == 0 else (left, left + patch) if b == blocks - 1 else None
        got = lax.all_gather(other, "c", axis=0)
        middle, after = convolve(b, high, lean if b else frame, width, trim, side, at, part, got, table)
        if b < blocks - 1:
            middle = lax.all_gather(middle, "y", axis=1, tiled=True)
            mine, got = halves(dot_nt(middle, early[2 * b + 1]), c)
            second = mine + pick(c, got[1], got[0]).astype(F32)
            stream = jnp.maximum(after[0] * second + after[1] + stream.astype(F32), 0.0).astype(BF16)

    deep = rows * nc
    spots_of_chip = deep * patch
    middle = lax.all_to_all(middle.reshape(ny, spots_of_chip, own), "y", 0, 0, tiled=True)
    t = lax.broadcasted_iota(jnp.int32, (spots_of_chip, gathered.shape[0]), 0)
    j = lax.broadcasted_iota(jnp.int32, (spots_of_chip, gathered.shape[0]), 1)
    of_chip = (j == (1 + deep * y + t // patch) * lean + LEFT - margin + t % patch).astype(BF16)
    kept = jnp.dot(of_chip, gathered, preferred_element_type=F32).astype(BF16)
    j = lax.broadcasted_iota(jnp.int32, (half, half), 0)
    k = lax.broadcasted_iota(jnp.int32, (half, half), 1)
    natural = (j == (k // width % ny) * own + k // lanes * width + k % width).astype(BF16)
    kept = jnp.dot(kept, natural, preferred_element_type=F32).astype(BF16)
    second, send = multiply_last(at, middle, final, kept)
    got = swap_core(send, c)
    kept = kept.reshape(nc, rows * patch, half)
    mine, theirs = pick(c, kept[0], kept[1]), got[:, nz * lanes :]
    residual = jnp.concatenate([pick(c, mine, theirs), pick(c, theirs, mine)], axis=1)
    second = second + got[:, : nz * lanes].astype(F32)
    gain, bias = last.reshape(2, 1, nz * lanes)
    out = jnp.maximum(gain * second + bias + residual.astype(F32), 0.0).astype(BF16)
    out = out.reshape(rows * patch, nz, lanes)
    out = out.transpose(1, 0, 2).reshape(nz, rows, patch, lanes)
    out = lax.all_to_all(out, "z", 0, 0, tiled=True).reshape(tiles, across, rows, patch, lanes)
    return out.transpose(0, 2, 1, 3, 4).reshape(tiles, rows, side, lanes)


def solution(mesh):
    grid = Mesh(mesh.devices.reshape(4, 4, 2, 16), ("x", "y", "c", "z"))
    placed = (
        P(None, SEG, None, "z"),
        P(None, None, "z"),
        P(None, None, None, "z"),
        P(None, None, "z"),
        P(None, None, "z"),
        P(None, None, "z"),
    )
    return jax.shard_map(local, mesh=grid, in_specs=placed, out_specs=P(None, SEG, None, "z"), check_vma=False)
```
